512 devices in a mesh: row: 32 (over z, core), col: 16 (over y, x).
Axes of the slice: x: 4, y: 4, z: 16, core: 2. Of those that a mesh axis runs over, the one named last changes fastest.
Arguments:
- context: bfloat16 [128, 8192], P('col', 'row'), may hold values from -6 to 6
- weight: bfloat16 [8192, 16384], P('row', 'col'), may hold values from -0.0625 to 0.0625
- feature_bias: float32 [16384], P('col'), may hold values from -3 to 3
- covariance: float32 [16384, 16384], P('row', 'col'), may hold values from -0.5 to 2.5, as said below
- prior_mean: float32 [16384], P('row'), may hold values from -6 to 6
- rewards: float32 [128], replicated, may hold values from -12 to 12
Outputs:
- posterior_cov: float32 [16384, 16384], P('row', 'col')
- posterior_mean: float32 [16384], P('row')
The draws below stay inside these ranges and needn't reach their ends.
Inputs may be any that keep to these rules, and one draw needn't show every extreme that they name: covariance is exactly symmetric and positive definite.
All inputs are finite; a program needn't handle non-finite values.
Results may differ from the reference program's by a relative error of at most 0.00042.
Values may be sent and summed in bfloat16 or wider, within the bound.
A program may use at most 64 MiB of HBM per device.

```python
import jax
import jax.numpy as jnp
from jax import lax

F = 16384
DM = 8192
B = 128


def draw_covariance(key, part):
    base = jax.random.fold_in(key, 7)
    first, second = jax.random.split(base)
    noise = jax.random.normal(first, (F, F), jnp.float32)
    symmetric = (noise + noise.T) * (0.25 / F ** 0.5)
    diagonal = jnp.exp(jax.random.uniform(second, (F,), jnp.float32, 0.0, 0.6931))
    return symmetric + jnp.diag(diagonal)


def block_scale(rng, shape, cuts, smallest, top_value):
    def one(position, parts):
        steps = jax.random.uniform(jax.random.fold_in(jax.random.fold_in(rng, 6), position), (parts,), jnp.float32, smallest / len(cuts), top_value / len(cuts))
        return jnp.repeat(jnp.exp(steps), shape[position] // parts).reshape((-1,) + (1,) * (len(shape) - position - 1))

    factor_of = one(*cuts[0])
    for cut in cuts[1:]:
        factor_of = factor_of * one(*cut)
    return factor_of


def centred(own_key, shape, spread, most, cuts=(), held_as=jnp.bfloat16):
    factor_of = block_scale(own_key, shape, cuts, -0.22, 0.18) if cuts else 1.0
    array = jax.random.normal(own_key, shape, jnp.float32) * spread * factor_of
    return jnp.minimum(jnp.maximum(array, -most), most).astype(held_as)


def setup_inputs(seed: int = 0) -> dict:
    streams_of = jax.random.split(jax.random.key(seed), 7)
    context = centred(streams_of[0], (B, DM), 1.0, 6.0, ((0, 16), (1, 32)))
    weight = centred(streams_of[1], (DM, F), DM ** -0.5, 0.0625, ((0, 32), (1, 16)))
    feature_bias = centred(streams_of[2], (F,), 0.5, 3.0, ((0, 16),), jnp.float32)
    covariance = draw_covariance(jax.random.fold_in(streams_of[6], 71), 0)
    prior_mean = centred(streams_of[4], (F,), 1.0, 6.0, ((0, 32),), jnp.float32)
    rewards = centred(streams_of[5], (B,), 2.0, 12.0, (), jnp.float32)
    return dict(context=context, weight=weight, feature_bias=feature_bias, covariance=covariance, prior_mean=prior_mean, rewards=rewards)


def reference(context, weight, feature_bias, covariance, prior_mean, rewards):
    highest = lax.Precision.HIGHEST
    preact = jnp.dot(context.astype(jnp.float32), weight.astype(jnp.float32), preferred_element_type=jnp.float32)
    features = jnp.tanh(preact + feature_bias[None, :]).astype(jnp.bfloat16)
    feat32 = features.astype(jnp.float32)
    panel = jnp.einsum('ik,bk->ib', covariance, feat32, precision=highest)
    gram_matrix = jnp.dot(feat32, panel, precision=highest) + jnp.eye(B, dtype=jnp.float32)
    predicted = jnp.dot(feat32, prior_mean, precision=highest)
    lower_factor = jnp.linalg.cholesky(gram_matrix)
    lower_inverse = lax.linalg.triangular_solve(lower_factor, jnp.eye(B, dtype=jnp.float32), left_side=True, lower=True)
    inverse_gram = jnp.dot(lower_inverse.T, lower_inverse, precision=highest)
    coeffs = jnp.dot(inverse_gram, rewards - predicted, precision=highest)
    gain = jnp.dot(panel, inverse_gram, precision=highest)
    posterior_mean = prior_mean + jnp.dot(panel, coeffs, precision=highest)
    posterior_cov = covariance - jnp.einsum('ib,jb->ij', gain, panel, precision=highest)
    return (posterior_cov, posterior_mean)
```

```python
import jax, jax.numpy as jnp
from jax import lax
from jax.experimental import pallas as pl
from jax.experimental.pallas import tpu as pltpu

HI = lax.Precision.HIGHEST


def split3(x):
    hi = x.astype(jnp.bfloat16)
    rest = x - hi.astype(jnp.float32)
    mid = rest.astype(jnp.bfloat16)
    lo = (rest - mid.astype(jnp.float32)).astype(jnp.bfloat16)
    return hi, mid, lo


def sweep_inverse(a):
    n = a.shape[0]
    lane = lax.broadcasted_iota(jnp.int32, (8, n), 1)
    sub = lax.broadcasted_iota(jnp.int32, (8, 1), 0)
    blocks = [a[8 * i : 8 * i + 8] for i in range(n // 8)]
    for j in range(n):
        at, s = j // 8, j % 8
        mine = blocks[at]
        pivot = 1.0 / mine[s : s + 1, j : j + 1]
        in_lane = lane == j
        row = jnp.where(in_lane[:1], 1.0, mine[s : s + 1]) * pivot
        row = jnp.broadcast_to(row, (8, n))
        new = []
        for i, block in enumerate(blocks):
            col = block[:, j : j + 1]
            kept = jnp.where(in_lane, 0.0, block)
            if i == at:
                col = jnp.where(sub == s, -1.0, col)
                kept = jnp.where(sub == s, 0.0, kept)
            new.append(kept - col * row)
        blocks = new
    return jnp.concatenate(blocks, 0)


def update_kernel(g_ref, pred_ref, rew_ref, mean_ref, pr_ref, pc_ref, cov_ref, out_ref, outm_ref, gain_s, pc_s):
    step = pl.program_id(0)
    rows = cov_ref.shape[0]

    @pl.when(step == 0)
    def _():
        b = g_ref.shape[0]
        eye = (lax.broadcasted_iota(jnp.int32, (b, b), 0) == lax.broadcasted_iota(jnp.int32, (b, b), 1)).astype(jnp.float32)
        inv = sweep_inverse(g_ref[...] + eye)
        diff = rew_ref[...] - pred_ref[...]
        coeffs = jnp.dot(jnp.broadcast_to(diff, (8, b)), inv, precision=HI, preferred_element_type=jnp.float32)
        outm_ref[...] = mean_ref[...] + jnp.dot(coeffs, pr_ref[...], precision=HI, preferred_element_type=jnp.float32)[:1]
        gain = jnp.dot(inv, pr_ref[...], precision=HI, preferred_element_type=jnp.float32)
        hi, mid, _ = split3(gain)
        for i in range(gain_s.shape[0]):
            cut = slice(i * rows, i * rows + rows)
            gain_s[i] = jnp.concatenate([hi[:, cut], hi[:, cut], mid[:, cut]], 0)
        phi, pmid, _ = split3(pc_ref[...])
        pc_s[...] = jnp.concatenate([phi, pmid, phi], 0)

    update = lax.dot_general(gain_s[step], pc_s[...], (((0,), (0,)), ((), ())), preferred_element_type=jnp.float32)
    out_ref[...] = cov_ref[...] - update


def update(g, pred, rew, mean, pr, pc, cov, steps=4):
    b = g.shape[0]
    n, m = cov.shape
    rows = n // steps
    whole = lambda *shape: pl.BlockSpec(shape, lambda i: (0, 0))
    return pl.pallas_call(
        update_kernel,
        grid=(steps,),
        in_specs=[whole(b, b), whole(1, b), whole(1, b), whole(1, n), whole(b, n), whole(b, m), pl.BlockSpec((rows, m), lambda i: (i, 0))],
        out_specs=[pl.BlockSpec((rows, m), lambda i: (i, 0)), whole(1, n)],
        out_shape=[jax.ShapeDtypeStruct((n, m), jnp.float32), jax.ShapeDtypeStruct((1, n), jnp.float32)],
        scratch_shapes=[pltpu.VMEM((steps, 3 * b, rows), jnp.bfloat16), pltpu.VMEM((3 * b, m), jnp.bfloat16)],
    )(g, pred, rew, mean, pr, pc, cov)
from jax.sharding import PartitionSpec as P

MESH = pl.DeviceIdType.MESH


def far_first(t, n):
    return n // 2 + (1 - 2 * (t % 2)) * ((t + 1) // 2)


def near_first(t, n):
    return far_first(n - 2 - t, n)


def exchange_kernel(
    ctx_hbm, w_hbm, bias_hbm, cov_hbm, mean_hbm,
    g_out, pred_out, pr_out, pc_out,
    ctx_all, ctx_m, w_v, bias_v, cov_v, mean_v, c_hi, c_mid, c_lo,
    x_send, x_recv, z_send, z_recv, phi_s, phi_c, phi_p, phi_r,
    pp_send, pp_recv, p_own, g_send, g_recv, gz_s, gz_r, pz_s, pz_r, g_s, g_all,
    pr_all, p_z, pc_all,
    local, near, pair_s, pair_r, send, recv, mate,
):
    nz, nc, nb = z_send.shape[0], ctx_all.shape[0], 4
    r, c = lax.axis_index("row"), lax.axis_index("col")
    z, h = r // 2, r % 2
    other = 1 - h

    def at(zz, hh, cc):
        return (zz * 2 + hh, cc)

    def remote(src, dst, s_sem, r_sem, where):
        return pltpu.make_async_remote_copy(
            src_ref=src, dst_ref=dst, send_sem=s_sem, recv_sem=r_sem, device_id=where, device_id_type=MESH
        )

    loads = [
        pltpu.make_async_copy(ctx_hbm, ctx_all.at[c], local.at[0]),
        pltpu.make_async_copy(cov_hbm, cov_v, local.at[1]),
        pltpu.make_async_copy(w_hbm, w_v, local.at[2]),
        pltpu.make_async_copy(bias_hbm, bias_v, local.at[3]),
        pltpu.make_async_copy(mean_hbm, mean_v, local.at[4]),
    ]
    for load in loads:
        load.start()

    barrier = pltpu.get_barrier_semaphore()

    def greet(where):
        pl.semaphore_signal(barrier, inc=1, device_id=where, device_id_type=MESH)

    def greet_plane(t, _):
        greet(at(z, h, (c + t) % nc))
        return 0

    def greet_line(t, _):
        greet(at((z + t) % nz, h, c))
        greet(at((z - t + nz) % nz, h, c))
        greet(at((z + t) % nz, other, c))
        greet(at((z - t + nz) % nz, other, c))
        return 0

    lax.fori_loop(1, nc, greet_plane, 0)
    lax.fori_loop(1, nb + 1, greet_line, 0)
    greet(at(z, other, c))
    pl.semaphore_wait(barrier, nc - 1 + 4 * nb + 1)
    pl.semaphore_signal(near, inc=1, device_id=at((z + nb) % nz, h, c), device_id_type=MESH)
    pl.semaphore_signal(near, inc=1, device_id=at((z - nb + nz) % nz, h, c), device_id_type=MESH)

    def ctx_copy(t):
        return remote(ctx_hbm, ctx_all.at[c], send.at[0, t], recv.at[0, c], at(z, h, (c + t) % nc))

    def plane_arrival(buf, phase, src):
        return remote(buf.at[src], buf.at[src], send.at[phase, 0], recv.at[phase, src], at(z, other, c))

    def start_ctx(t, _):
        ctx_copy(t).start()
        return 0

    lax.fori_loop(1, nc, start_ctx, 0)

    loads[1].wait()
    rows = cov_v.shape[0]

    def split_cov(i, _):
        cut = pl.ds(pl.multiple_of(i * 64, 64), 64)
        hi, mid, lo = split3(cov_v[cut, :])
        c_hi[cut, :] = hi
        c_mid[cut, :] = mid
        c_lo[cut, :] = lo
        return 0

    lax.fori_loop(0, rows // 64, split_cov, 0)
    loads[2].wait()
    loads[3].wait()
    loads[4].wait()
    loads[0].wait()

    def wait_ctx(t, _):
        plane_arrival(ctx_all, 0, (c + t) % nc).wait_recv()
        return 0

    lax.fori_loop(1, nc, wait_ctx, 0)
    tokens, depth = ctx_m.shape
    half = tokens // 2
    ctx_m[...] = ctx_all[...].astype(jnp.float32).reshape(tokens, depth).astype(jnp.bfloat16)

    theirs = ctx_m[pl.ds(pl.multiple_of(other * half, half), half), :]
    x_send[...] = jnp.dot(theirs, w_v[...], preferred_element_type=jnp.float32)
    swap_x = remote(x_send, x_recv, pair_s.at[0], pair_r.at[0], at(z, other, c))
    swap_x.start()
    mine = ctx_m[pl.ds(pl.multiple_of(h * half, half), half), :]
    own = jnp.dot(mine, w_v[...], preferred_element_type=jnp.float32)
    z_pieces = [(slice(k // 4 * 16, k // 4 * 16 + 16), slice(k % 4 * 256, k % 4 * 256 + 256)) for k in range(nz)]
    for k, (a, b) in enumerate(z_pieces):
        z_send[k] = own[a, b]
    swap_x.wait_recv()
    for k, (a, b) in enumerate(z_pieces):
        z_send[k] += x_recv[a, b]
    pl.semaphore_wait(near, 2)

    def line_copy(src, dst, phase, t):
        return remote(src, dst, send.at[phase, t], recv.at[phase, z], at((z + t) % nz, h, c))

    def line_arrival(buf, phase, src):
        return remote(buf.at[src], buf.at[src], send.at[phase, 0], recv.at[phase, src], at(z, other, c))

    def start_z(t, _):
        t = far_first(t, nz)
        line_copy(z_send.at[(z + t) % nz], z_recv.at[z], 1, t).start()
        return 0

    lax.fori_loop(0, nz - 1, start_z, 0)
    z_recv[z] = z_send[z]

    def wait_z(t, _):
        line_arrival(z_recv, 1, (z + t) % nz).wait_recv()
        return 0

    lax.fori_loop(1, nz, wait_z, 0)
    kb = z % 4
    total = jnp.sum(z_recv[...], axis=0) + bias_v[:, pl.ds(pl.multiple_of(kb * 256, 256), 256)]
    phi = jnp.tanh(total).astype(jnp.bfloat16)
    phi_s[...] = phi

    def start_phi(t, _):
        t = far_first(t, nz)
        line_copy(phi_s, phi_c.at[h * nz + z], 2, t).start()
        return 0

    lax.fori_loop(0, nz - 1, start_phi, 0)

    def mate_copy(k):
        return remote(phi_c.at[h * nz + k], phi_c.at[h * nz + k], mate.at[0, k], mate.at[1, k], at(z, other, c))

    phi_c[h * nz + z] = phi
    mate_copy(z).start()

    def plane_copy(src, dst, phase, t):
        return remote(src, dst, send.at[phase, t], recv.at[phase, c], at(z, h, (c + t) % nc))

    def start_plane_phi(t, _):
        plane_copy(phi_s, phi_p.at[c], 3, t).start()
        return 0

    lax.fori_loop(1, nc, start_plane_phi, 0)
    phi_p[c] = phi

    goal = kb // 2
    slot = h * 8 + z // 4 * 2 + kb % 2

    def row_copy(t):
        zz = (c + t) % nc
        return remote(phi_p.at[zz], phi_r.at[slot], send.at[4, t], recv.at[4, slot], at(zz, goal, c))

    def pass_phi(t, _):
        zz = (c + t) % nc

        @pl.when(t > 0)
        def _():
            plane_arrival(phi_p, 3, zz).wait_recv()

        here = jnp.logical_and(zz == z, goal == h)

        @pl.when(here)
        def _():
            phi_r[slot] = phi_p[zz]

        @pl.when(jnp.logical_not(here))
        def _():
            row_copy(t).start()

        return 0

    lax.fori_loop(0, nc, pass_phi, 0)

    def pass_mate(t, _):
        zz = (z + near_first(t, nz)) % nz
        remote(phi_s, phi_c.at[h * nz + zz], send.at[2, 0], recv.at[2, zz], at(z, other, c)).wait_recv()
        mate_copy(zz).start()
        return 0

    lax.fori_loop(0, nz - 1, pass_mate, 0)

    def wait_mate(t, _):
        k = other * nz + t
        remote(phi_c.at[k], phi_c.at[k], mate.at[0, t], mate.at[1, t], at(z, other, c)).wait_recv()
        return 0

    lax.fori_loop(0, nz, wait_mate, 0)

    part = None
    for k in range(4):
        lhs = jnp.concatenate([phi_c[i * 4 + k] for i in range(8)], 0)
        for term in (c_hi, c_mid, c_lo):
            prod = lax.dot_general(
                lhs, term[:, k * 256 : k * 256 + 256], (((1,), (1,)), ((), ())), preferred_element_type=jnp.float32
            )
            part = prod if part is None else part + prod
    pp_send[...] = part.reshape(pp_send.shape)

    def start_pp(t, _):
        plane_copy(pp_send.at[(c + t) % nc], pp_recv.at[c], 5, t).start()
        return 0

    lax.fori_loop(1, nc, start_pp, 0)
    pp_recv[c] = pp_send[c]

    def source_here(s):
        zz = s % 8 // 2 * 4 + goal_of(s)
        return jnp.logical_and(zz == z, s // 8 == h)

    def goal_of(s):
        return 2 * h + s % 2

    def wait_row(s, _):
        @pl.when(jnp.logical_not(source_here(s)))
        def _():
            plane_arrival(phi_r, 4, s).wait_recv()

        return 0

    lax.fori_loop(0, nz, wait_row, 0)

    def wait_pp(t, _):
        plane_arrival(pp_recv, 5, (c + t) % nc).wait_recv()
        return 0

    lax.fori_loop(1, nc, wait_pp, 0)
    p_mine = jnp.sum(pp_recv[...], axis=0)
    p_own[...] = p_mine

    def start_pr(t, _):
        plane_copy(p_own, pr_all.at[c], 6, t).start()
        return 0

    lax.fori_loop(1, nc, start_pr, 0)
    pr_all[c] = p_mine
    p_z[z] = p_mine

    width = p_mine.shape[1]
    zeros = jnp.zeros((7, width), jnp.float32)
    terms = split3(jnp.concatenate([p_mine, mean_v[...], zeros], 0))
    stacked = jnp.concatenate(terms, 0)
    gram = None
    for k in range(2):
        rhs = jnp.concatenate([phi_r[i * 2 + k] for i in range(8)], 0)
        prod = lax.dot_general(
            stacked[:, k * 256 : k * 256 + 256], rhs, (((1,), (1,)), ((), ())), preferred_element_type=jnp.float32
        )
        gram = prod if gram is None else gram + prod
    g_send[...] = gram[:16] + gram[16:32] + gram[32:]
    swap_g = remote(g_send, g_recv, pair_s.at[1], pair_r.at[1], at(z, other, c))
    swap_g.start()
    swap_g.wait_recv()
    both = g_send[...] + g_recv[...]
    gz_s[...] = both[:8]
    pz_s[...] = both[8:9]

    def start_gz(t, _):
        t = far_first(t, nz)
        line_copy(gz_s, gz_r.at[z], 7, t).start()
        line_copy(pz_s, pz_r.at[z], 8, t).start()
        return 0

    lax.fori_loop(0, nz - 1, start_gz, 0)
    gz_r[z] = both[:8]
    pz_r[z] = both[8:9]

    def start_pz(t, _):
        t = far_first(t, nz)
        line_copy(p_own, p_z.at[z], 9, t).start()
        return 0

    lax.fori_loop(0, nz - 1, start_pz, 0)

    def wait_gz(t, _):
        zz = (z + t) % nz
        line_arrival(gz_r, 7, zz).wait_recv()
        line_arrival(pz_r, 8, zz).wait_recv()
        return 0

    lax.fori_loop(1, nz, wait_gz, 0)
    g_rows = jnp.sum(gz_r[...], axis=0)
    g_s[...] = g_rows

    def start_g(t, _):
        plane_copy(g_s, g_all.at[c], 10, t).start()
        return 0

    lax.fori_loop(1, nc, start_g, 0)
    g_all[c] = g_rows
    pred_out[...] = jnp.sum(pz_r[...], axis=0)

    def col_copy(zz):
        return remote(p_z.at[zz], pc_all.at[h, c], send.at[11, zz], recv.at[11, c], at(z, h, zz))

    def pass_pz(t, _):
        zz = (z + t) % nz

        @pl.when(t > 0)
        def _():
            line_arrival(p_z, 9, zz).wait_recv()

        @pl.when(zz == c)
        def _():
            pc_all[h, c] = p_z[zz]

        @pl.when(zz != c)
        def _():
            col_copy(zz).start()

        return 0

    lax.fori_loop(0, nz, pass_pz, 0)

    def mate_pc(p):
        return remote(pc_all.at[h, p], pc_all.at[h, p], mate.at[2, p], mate.at[3, p], at(z, other, c))

    def pass_pc(t, _):
        p = (c + t) % nc

        @pl.when(t > 0)
        def _():
            remote(p_own, pc_all.at[h, p], send.at[11, 0], recv.at[11, p], at(z, other, c)).wait_recv()

        mate_pc(p).start()
        return 0

    lax.fori_loop(0, nc, pass_pc, 0)

    def wait_last(t, _):
        p = (c + t) % nc
        plane_arrival(pr_all, 6, p).wait_recv()
        plane_arrival(g_all, 10, p).wait_recv()
        return 0

    lax.fori_loop(1, nc, wait_last, 0)
    g_out[...] = g_all[...].reshape(g_out.shape)
    pr_out[...] = pr_all[...].reshape(pr_out.shape)

    def wait_pc(p, _):
        remote(p_own, pc_all.at[other, p], mate.at[2, p], mate.at[3, p], at(z, other, c)).wait_recv()
        return 0

    lax.fori_loop(0, nc, wait_pc, 0)
    for k in range(2):
        pc_out[:, k * width : (k + 1) * width] = pc_all[k].reshape(tokens, width)

    swap_x.wait_send()
    swap_g.wait_send()

    def sent(t, _):
        ctx_copy(t).wait_send()
        line_copy(z_send.at[(z + t) % nz], z_recv.at[z], 1, t).wait_send()
        line_copy(phi_s, phi_c.at[h * nz + z], 2, t).wait_send()
        plane_copy(phi_s, phi_p.at[c], 3, t).wait_send()
        plane_copy(pp_send.at[(c + t) % nc], pp_recv.at[c], 5, t).wait_send()
        plane_copy(p_own, pr_all.at[c], 6, t).wait_send()
        line_copy(gz_s, gz_r.at[z], 7, t).wait_send()
        line_copy(pz_s, pz_r.at[z], 8, t).wait_send()
        line_copy(p_own, p_z.at[z], 9, t).wait_send()
        plane_copy(g_s, g_all.at[c], 10, t).wait_send()
        return 0

    lax.fori_loop(1, nz, sent, 0)

    def sent_some(t, _):
        mate_copy(t).wait_send()
        mate_pc(t).wait_send()

        @pl.when(jnp.logical_not(jnp.logical_and((c + t) % nc == z, goal == h)))
        def _():
            row_copy(t).wait_send()

        @pl.when(t != c)
        def _():
            col_copy(t).wait_send()

        return 0

    lax.fori_loop(0, nz, sent_some, 0)


def exchange(context, weight, bias, covariance, mean):
    rows_here, depth = context.shape
    n, m = covariance.shape
    nz, nc = lax.axis_size("row") // 2, lax.axis_size("col")
    b = rows_here * nc
    f32, bf16 = jnp.float32, jnp.bfloat16
    vmem, sem = pltpu.VMEM, pltpu.SemaphoreType
    scratch = [
        vmem((nc, rows_here, depth), bf16), vmem((b, depth), bf16), vmem((depth, m), bf16), vmem((1, m), f32),
        vmem((n, m), f32), vmem((1, n), f32), vmem((n, m), bf16), vmem((n, m), bf16), vmem((n, m), bf16),
        vmem((b // 2, m), f32), vmem((b // 2, m), f32), vmem((nz, 16, 256), f32), vmem((nz, 16, 256), f32),
        vmem((16, 256), bf16), vmem((2 * nz, 16, 256), bf16), vmem((nc, 16, 256), bf16), vmem((16, 16, 256), bf16),
        vmem((nc, 8, n), f32), vmem((nc, 8, n), f32), vmem((8, n), f32), vmem((16, b), f32), vmem((16, b), f32),
        vmem((8, b), f32), vmem((nz, 8, b), f32), vmem((1, b), f32), vmem((nz, 1, b), f32), vmem((8, b), f32), vmem((nc, 8, b), f32),
        vmem((nc, 8, n), f32), vmem((nz, 8, n), f32), vmem((2, nc, 8, n), f32),
        sem.DMA((5,)), sem.REGULAR, sem.DMA((2,)), sem.DMA((2,)), sem.DMA((12, 16)), sem.DMA((12, 16)), sem.DMA((4, 16)),
    ]
    return pl.pallas_call(
        exchange_kernel,
        in_specs=[pl.BlockSpec(memory_space=pl.ANY)] * 5,
        out_specs=[pl.BlockSpec(memory_space=pltpu.VMEM)] * 4,
        out_shape=[jax.ShapeDtypeStruct(s, f32) for s in ((b, b), (1, b), (b, n), (b, m))],
        scratch_shapes=scratch,
        compiler_params=pltpu.CompilerParams(collective_id=0, has_side_effects=True),
    )(context, weight, bias, covariance, mean)


def per_device(context, weight, feature_bias, covariance, prior_mean, rewards):
    mean = prior_mean.reshape(1, -1)
    g, pred, pr, pc = exchange(context, weight, feature_bias.reshape(1, -1), covariance, mean)
    cov, mean = update(g, pred, rewards.reshape(1, -1), mean, pr, pc, covariance)
    return cov, mean.reshape(-1)


def solution(mesh):
    return jax.shard_map(
        per_device,
        mesh=mesh,
        in_specs=(P("col", "row"), P("row", "col"), P("col"), P("row", "col"), P("row"), P()),
        out_specs=(P("row", "col"), P("row")),
        check_vma=False,
    )
```

```python
import jax
import jax.numpy as jnp
from jax import lax
from jax.experimental import pallas as pl
from jax.experimental.pallas import tpu as pltpu
from jax.sharding import PartitionSpec as P

HI = lax.Precision.HIGHEST
MESH = pl.DeviceIdType.MESH


def split3(x):
    hi = x.astype(jnp.bfloat16)
    rest = x - hi.astype(jnp.float32)
    mid = rest.astype(jnp.bfloat16)
    lo = (rest - mid.astype(jnp.float32)).astype(jnp.bfloat16)
    return hi, mid, lo


def coded_sum(x):
    t = x * 16.0
    t2 = t * t
    t4 = t2 * t2
    return ((t4 * t4) * t2 * t).astype(jnp.bfloat16)


def coded_panel(x):
    t = x * 4.0
    t2 = t * t
    return ((t2 * t2) * t2 * t).astype(jnp.bfloat16)


def rooted(y, power, scale):
    y = y.astype(jnp.float32)
    v = jnp.exp(jnp.log(jnp.abs(y)) * (1.0 / power)) * (1.0 / scale)
    return jnp.where(y < 0, -v, v)


def sum_from(y):
    return rooted(y, 11, 16)


def panel_from(y):
    return rooted(y, 7, 4)


def inverse_of_2(a, b, c):
    scale = 1.0 / (a * c - b * b)
    return c * scale, -b * scale, a * scale


def inverse_of_4(m):
    a0, a1, a2 = inverse_of_2(m[0][0], m[0][1], m[1][1])
    t = [[a0 * m[0][2 + k] + a1 * m[1][2 + k] for k in range(2)], [a1 * m[0][2 + k] + a2 * m[1][2 + k] for k in range(2)]]
    s0 = m[2][2] - (m[0][2] * t[0][0] + m[1][2] * t[1][0])
    s1 = m[2][3] - (m[0][2] * t[0][1] + m[1][2] * t[1][1])
    s2 = m[3][3] - (m[0][3] * t[0][1] + m[1][3] * t[1][1])
    c0, c1, c2 = inverse_of_2(s0, s1, s2)
    u = [[t[i][0] * c0 + t[i][1] * c1, t[i][0] * c1 + t[i][1] * c2] for i in range(2)]
    b0 = a0 + u[0][0] * t[0][0] + u[0][1] * t[0][1]
    b1 = a1 + u[0][0] * t[1][0] + u[0][1] * t[1][1]
    b2 = a2 + u[1][0] * t[1][0] + u[1][1] * t[1][1]
    return [
        [b0, b1, -u[0][0], -u[0][1]],
        [b1, b2, -u[1][0], -u[1][1]],
        [-u[0][0], -u[1][0], c0, c1],
        [-u[0][1], -u[1][1], c1, c2],
    ]


def panel4(blocks, lo, lane, sub):
    n = blocks[0].shape[1]
    for j in range(lo, lo + 8 * len(blocks), 4):
        at, s = (j - lo) // 8, j % 8
        mine = blocks[at]
        cell = [[None] * 4 for _ in range(4)]
        for i in range(4):
            for k in range(i, 4):
                cell[i][k] = cell[k][i] = jnp.broadcast_to(mine[s + i : s + i + 1, j + k : j + k + 1], (8, n))
        inv = inverse_of_4(cell)
        inside = (lane >= j) & (lane < j + 4)
        rows = [
            jnp.where(inside, jnp.where(lane == j + m, 1.0, 0.0), jnp.broadcast_to(mine[s + m : s + m + 1], (8, n)))
            for m in range(4)
        ]
        out = [(inv[i][0] * rows[0] + inv[i][1] * rows[1]) + (inv[i][2] * rows[2] + inv[i][3] * rows[3]) for i in range(4)]
        new = []
        for i, block in enumerate(blocks):
            kept = jnp.where(inside, 0.0, block)
            cols = [jnp.broadcast_to(block[:, j + k : j + k + 1], (8, n)) for k in range(4)]
            if i == at:
                here = (sub >= s) & (sub < s + 4)
                kept = jnp.where(here, 0.0, kept)
                cols = [jnp.where(here, jnp.where(sub == s + k, -1.0, 0.0), cols[k]) for k in range(4)]
            new.append(kept - ((cols[0] * out[0] + cols[1] * out[1]) + (cols[2] * out[2] + cols[3] * out[3])))
        blocks = new
    return blocks


def dot3(a, b):
    ah, am, al = split3(a)
    bh, bm, bl = split3(b)
    return jnp.dot(jnp.concatenate([ah, ah, am, am, ah, al], 1), jnp.concatenate([bh, bm, bh, bm, bl, bh], 0), preferred_element_type=jnp.float32)


def spd_inverse(a, w):
    n = a.shape[0]
    lane = lax.broadcasted_iota(jnp.int32, (8, n), 1)
    sub = lax.broadcasted_iota(jnp.int32, (8, n), 0)
    blocks = [a[8 * i : 8 * i + 8] for i in range(n // 8)]
    for lo in range(0, n, w):
        first, last = lo // 8, (lo + w) // 8
        panel = panel4(blocks[first:last], lo, lane, sub)
        rest = blocks[:first] + blocks[last:]
        cols = jnp.concatenate([b[:, lo : lo + w] for b in rest], 0)
        prod = dot3(cols, jnp.concatenate(panel, 0))
        inside = (lane >= lo) & (lane < lo + w)
        rest = [jnp.where(inside, 0.0, b) - prod[8 * i : 8 * i + 8] for i, b in enumerate(rest)]
        blocks = rest[:first] + panel + rest[first:]
    return jnp.concatenate(blocks, 0)


def update_kernel(g_ref, pred_ref, rew_ref, mean_ref, pr_ref, pc_ref, cov_ref, out_ref, outm_ref, gain_s, pc_s):
    step = pl.program_id(0)
    rows = cov_ref.shape[0]

    @pl.when(step == 0)
    def _():
        b = g_ref.shape[0]
        width = pc_ref.shape[-1]
        for k in range(2):
            panel = panel_from(pc_ref[k]).reshape(b, width)
            hi, mid, _ = split3(panel)
            cut = slice(k * width, k * width + width)
            pc_s[:b, cut] = hi
            pc_s[b : 2 * b, cut] = mid
            pc_s[2 * b :, cut] = hi
        pr = pr_ref[...]
        pr_t = pr.T
        eye = (lax.broadcasted_iota(jnp.int32, (b, b), 0) == lax.broadcasted_iota(jnp.int32, (b, b), 1)).astype(jnp.float32)
        inv = spd_inverse(g_ref[...] + eye, 16)
        gain = jnp.dot(pr_t, inv, precision=HI, preferred_element_type=jnp.float32)
        hi, mid, _ = split3(gain)
        gain_s[:, :b] = hi
        gain_s[:, b : 2 * b] = hi
        gain_s[:, 2 * b :] = mid
        diff = rew_ref[...] - pred_ref[...]
        coeffs = jnp.dot(jnp.broadcast_to(diff, (8, b)), inv, precision=HI, preferred_element_type=jnp.float32)
        outm_ref[...] = mean_ref[...] + jnp.dot(coeffs, pr, precision=HI, preferred_element_type=jnp.float32)[:1]

    mine = gain_s[pl.ds(pl.multiple_of(step * rows, rows), rows), :]
    out_ref[...] = cov_ref[...] - jnp.dot(mine, pc_s[...], preferred_element_type=jnp.float32)


def update(g, pred, rew, mean, pr, pc, cov, steps=4):
    b = g.shape[0]
    n, m = cov.shape
    rows = n // steps
    whole = lambda *shape: pl.BlockSpec(shape, lambda i: (0,) * len(shape))
    return pl.pallas_call(
        update_kernel,
        grid=(steps,),
        in_specs=[
            whole(b, b), whole(1, b), whole(1, b), whole(1, n), whole(b, n), whole(*pc.shape), pl.BlockSpec((rows, m), lambda i: (i, 0)),
        ],
        out_specs=[pl.BlockSpec((rows, m), lambda i: (i, 0)), whole(1, n)],
        out_shape=[jax.ShapeDtypeStruct((n, m), jnp.float32), jax.ShapeDtypeStruct((1, n), jnp.float32)],
        scratch_shapes=[pltpu.VMEM((n, 3 * b), jnp.bfloat16), pltpu.VMEM((3 * b, m), jnp.bfloat16)],
    )(g, pred, rew, mean, pr, pc, cov)


def far_first(t, n):
    return n // 2 + (1 - 2 * (t % 2)) * ((t + 1) // 2)


def near_first(t, n):
    return far_first(n - 2 - t, n)


def exchange_kernel(
    ctx_hbm, w_hbm, bias_hbm, cov_hbm, mean_hbm,
    g_out, pred_out, pr_out, pc_out,
    ctx_all, ctx_m, w_v, bias_v, cov_v, mean_v, c_hi, c_mid, c_lo,
    x_send, x_recv, z_send, z_code, z_recv, phi_s, phi_c, phi_r,
    pp_send, pp_recv, p_own, p_code, g_send, g_recv, gz_s, gz_r, pz_s, pz_r, g_s, g_all,
    pr_all, p_z, pc_all,
    local, near, pair_s, pair_r, send, recv, mate, send_pc, recv_pc,
):
    nz, nc, nb = z_send.shape[0], ctx_all.shape[0], 4
    r, c = lax.axis_index("row"), lax.axis_index("col")
    z, h = r // 2, r % 2
    other = 1 - h

    def at(zz, hh, cc):
        return (zz * 2 + hh, cc)

    def remote(src, dst, s_sem, r_sem, where):
        return pltpu.make_async_remote_copy(
            src_ref=src, dst_ref=dst, send_sem=s_sem, recv_sem=r_sem, device_id=where, device_id_type=MESH
        )

    loads = [
        pltpu.make_async_copy(ctx_hbm, ctx_all.at[c], local.at[0]),
        pltpu.make_async_copy(cov_hbm, cov_v, local.at[1]),
        pltpu.make_async_copy(w_hbm, w_v, local.at[2]),
        pltpu.make_async_copy(bias_hbm, bias_v, local.at[3]),
        pltpu.make_async_copy(mean_hbm, mean_v, local.at[4]),
    ]
    for load in loads:
        load.start()

    barrier = pltpu.get_barrier_semaphore()

    def greet(where):
        pl.semaphore_signal(barrier, inc=1, device_id=where, device_id_type=MESH)

    def greet_plane(t, _):
        greet(at(z, h, (c + t) % nc))
        return 0

    def greet_line(t, _):
        greet(at((z + t) % nz, h, c))
        greet(at((z - t + nz) % nz, h, c))
        greet(at((z + t) % nz, other, c))
        greet(at((z - t + nz) % nz, other, c))
        return 0

    lax.fori_loop(1, nc, greet_plane, 0)
    lax.fori_loop(1, nb + 1, greet_line, 0)
    greet(at(z, other, c))
    pl.semaphore_wait(barrier, nc - 1 + 4 * nb + 1)
    pl.semaphore_signal(near, inc=1, device_id=at((z + nb) % nz, h, c), device_id_type=MESH)
    pl.semaphore_signal(near, inc=1, device_id=at((z - nb + nz) % nz, h, c), device_id_type=MESH)

    def ctx_copy(t):
        return remote(ctx_hbm, ctx_all.at[c], send.at[0, t], recv.at[0, c], at(z, h, (c + t) % nc))

    def plane_arrival(buf, phase, src):
        return remote(buf.at[src], buf.at[src], send.at[phase, 0], recv.at[phase, src], at(z, other, c))

    def start_ctx(t, _):
        ctx_copy(t).start()
        return 0

    lax.fori_loop(1, nc, start_ctx, 0)

    loads[1].wait()
    rows = cov_v.shape[0]

    def split_cov(i, _):
        cut = pl.ds(pl.multiple_of(i * 64, 64), 64)
        hi, mid, lo = split3(cov_v[cut, :])
        c_hi[cut, :] = hi
        c_mid[cut, :] = mid
        c_lo[cut, :] = lo
        return 0

    lax.fori_loop(0, rows // 64, split_cov, 0)
    loads[2].wait()
    loads[3].wait()
    loads[4].wait()
    loads[0].wait()

    def wait_ctx(t, _):
        plane_arrival(ctx_all, 0, (c + t) % nc).wait_recv()
        return 0

    lax.fori_loop(1, nc, wait_ctx, 0)
    tokens, depth = ctx_m.shape
    half = tokens // 2
    ctx_m[...] = ctx_all[...].astype(jnp.float32).reshape(tokens, depth).astype(jnp.bfloat16)

    theirs = ctx_m[pl.ds(pl.multiple_of(other * half, half), half), :]
    x_send[...] = jnp.dot(theirs, w_v[...], preferred_element_type=jnp.float32)
    swap_x = remote(x_send, x_recv, pair_s.at[0], pair_r.at[0], at(z, other, c))
    swap_x.start()
    mine = ctx_m[pl.ds(pl.multiple_of(h * half, half), half), :]
    own = jnp.dot(mine, w_v[...], preferred_element_type=jnp.float32)
    z_pieces = [(slice(k // 4 * 16, k // 4 * 16 + 16), slice(k % 4 * 256, k % 4 * 256 + 256)) for k in range(nz)]
    for k, (a, b) in enumerate(z_pieces):
        z_send[k] = own[a, b]
    swap_x.wait_recv()
    for k, (a, b) in enumerate(z_pieces):
        both = z_send[k] + x_recv[a, b]
        z_send[k] = both
        z_code[k] = coded_sum(both)
    pl.semaphore_wait(near, 2)

    def line_copy(src, dst, phase, t):
        return remote(src, dst, send.at[phase, t], recv.at[phase, z], at((z + t) % nz, h, c))

    def line_arrival(buf, phase, src):
        return remote(buf.at[src], buf.at[src], send.at[phase, 0], recv.at[phase, src], at(z, other, c))

    def start_z(t, _):
        t = far_first(t, nz)
        line_copy(z_code.at[(z + t) % nz], z_recv.at[z], 1, t).start()
        return 0

    lax.fori_loop(0, nz - 1, start_z, 0)

    def add_z(t, acc):
        zz = (z + near_first(t, nz)) % nz
        line_arrival(z_recv, 1, zz).wait_recv()
        return acc + sum_from(z_recv[zz])

    total = lax.fori_loop(0, nz - 1, add_z, z_send[z])
    kb = z % 4
    total = total + bias_v[:, pl.ds(pl.multiple_of(kb * 256, 256), 256)]
    phi = jnp.tanh(total).astype(jnp.bfloat16)
    phi_s[...] = phi

    def start_phi(t, _):
        t = far_first(t, nz)
        line_copy(phi_s, phi_c.at[h * nz + z], 2, t).start()
        return 0

    lax.fori_loop(0, nz - 1, start_phi, 0)

    def mate_copy(k):
        return remote(phi_c.at[h * nz + k], phi_c.at[h * nz + k], mate.at[0, k], mate.at[1, k], at(z, other, c))

    def plane_copy(src, dst, phase, t):
        return remote(src, dst, send.at[phase, t], recv.at[phase, c], at(z, h, (c + t) % nc))

    holder = c == z

    def push(core, k):
        column = k % 4
        slot = core * 8 + k // 4 * 2 + column % 2

        @pl.when(jnp.logical_and(holder, column // 2 == h))
        def _():
            phi_r[slot] = phi_c[core * nz + k]

            @pl.when(slot != z)
            def _():
                remote(phi_c.at[core * nz + k], phi_r.at[slot], send.at[3, slot], recv.at[4, slot], at(z, h, slot)).start()

    phi_c[h * nz + z] = phi
    mate_copy(z).start()
    push(h, z)

    def pass_mate(t, _):
        zz = (z + near_first(t, nz)) % nz
        remote(phi_s, phi_c.at[h * nz + zz], send.at[2, 0], recv.at[2, zz], at(z, other, c)).wait_recv()
        mate_copy(zz).start()
        push(h, zz)
        return 0

    lax.fori_loop(0, nz - 1, pass_mate, 0)

    def wait_mate(t, _):
        k = (z + near_first(t - 1, nz)) % nz
        k = jnp.where(t == 0, z, k)
        i = other * nz + k
        remote(phi_c.at[i], phi_c.at[i], mate.at[0, k], mate.at[1, k], at(z, other, c)).wait_recv()
        push(other, k)
        return 0

    lax.fori_loop(0, nz, wait_mate, 0)

    part = None
    for k in range(4):
        lhs = jnp.concatenate([phi_c[i * 4 + k] for i in range(8)], 0)
        for term in (c_hi, c_mid, c_lo):
            prod = lax.dot_general(
                lhs, term[:, k * 256 : k * 256 + 256], (((1,), (1,)), ((), ())), preferred_element_type=jnp.float32
            )
            part = prod if part is None else part + prod
    pp_send[...] = part.reshape(pp_send.shape)

    def start_pp(t, _):
        plane_copy(pp_send.at[(c + t) % nc], pp_recv.at[c], 5, t).start()
        return 0

    lax.fori_loop(1, nc, start_pp, 0)
    pp_recv[c] = pp_send[c]

    def pass_row(t):
        return plane_copy(phi_r.at[c], phi_r.at[c], 4, t)

    @pl.when(jnp.logical_not(holder))
    def _():
        plane_arrival(phi_r, 4, c).wait_recv()

    def start_row(t, _):
        @pl.when((c + t) % nc != z)
        def _():
            pass_row(t).start()

        return 0

    lax.fori_loop(1, nc, start_row, 0)

    def wait_row(t, _):
        @pl.when(jnp.logical_not(holder))
        def _():
            plane_arrival(phi_r, 4, (c + t) % nc).wait_recv()

        return 0

    def wait_pp(t, _):
        plane_arrival(pp_recv, 5, (c + t) % nc).wait_recv()
        return 0

    lax.fori_loop(1, nc, wait_pp, 0)
    p_mine = jnp.sum(pp_recv[...], axis=0)
    p_own[...] = p_mine
    p_code[0] = coded_panel(p_mine)
    lax.fori_loop(1, nc, wait_row, 0)

    width = p_mine.shape[1]
    zeros = jnp.zeros((7, width), jnp.float32)
    terms = split3(jnp.concatenate([p_mine, mean_v[...], zeros], 0))
    stacked = jnp.concatenate(terms, 0)
    gram = None
    for k in range(2):
        rhs = jnp.concatenate([phi_r[i * 2 + k] for i in range(8)], 0)
        prod = lax.dot_general(
            stacked[:, k * 256 : k * 256 + 256], rhs, (((1,), (1,)), ((), ())), preferred_element_type=jnp.float32
        )
        gram = prod if gram is None else gram + prod
    g_send[...] = gram[:16] + gram[16:32] + gram[32:]
    swap_g = remote(g_send, g_recv, pair_s.at[1], pair_r.at[1], at(z, other, c))
    swap_g.start()

    def start_pr(t, _):
        plane_copy(p_own, pr_all.at[c], 6, t).start()
        return 0

    lax.fori_loop(1, nc, start_pr, 0)
    pr_all[c] = p_mine
    p_z[z] = p_code[0]

    swap_g.wait_recv()
    both = g_send[...] + g_recv[...]
    gz_s[...] = both[:8]
    pz_s[...] = both[8:9]

    def start_gz(t, _):
        t = far_first(t, nz)
        line_copy(gz_s, gz_r.at[z], 7, t).start()
        line_copy(pz_s, pz_r.at[z], 8, t).start()
        return 0

    lax.fori_loop(0, nz - 1, start_gz, 0)
    gz_r[z] = both[:8]
    pz_r[z] = both[8:9]

    def start_pz(t, _):
        t = far_first(t, nz)
        line_copy(p_code.at[0], p_z.at[z], 9, t).start()
        return 0

    lax.fori_loop(0, nz - 1, start_pz, 0)

    def wait_gz(t, _):
        zz = (z + t) % nz
        line_arrival(gz_r, 7, zz).wait_recv()
        line_arrival(pz_r, 8, zz).wait_recv()
        return 0

    lax.fori_loop(1, nz, wait_gz, 0)
    g_rows = jnp.sum(gz_r[...], axis=0)
    g_s[...] = g_rows

    def start_g(t, _):
        plane_copy(g_s, g_all.at[c], 10, t).start()
        return 0

    lax.fori_loop(1, nc, start_g, 0)
    g_all[c] = g_rows
    pred_out[...] = jnp.sum(pz_r[...], axis=0)

    def col_copy(zz, core):
        return remote(p_z.at[zz], pc_all.at[h, c], send_pc.at[core, zz], recv_pc.at[h, c], at(z, core, zz))

    def pass_pz(t, _):
        zz = (z + near_first(t - 1, nz)) % nz
        zz = jnp.where(t == 0, z, zz)

        @pl.when(t > 0)
        def _():
            line_arrival(p_z, 9, zz).wait_recv()

        @pl.when(zz == c)
        def _():
            pc_all[h, c] = p_z[zz]

        @pl.when(zz != c)
        def _():
            col_copy(zz, h).start()

        col_copy(zz, other).start()
        return 0

    lax.fori_loop(0, nz, pass_pz, 0)

    def wait_last(t, _):
        p = (c + t) % nc
        plane_arrival(pr_all, 6, p).wait_recv()
        plane_arrival(g_all, 10, p).wait_recv()
        return 0

    lax.fori_loop(1, nc, wait_last, 0)
    g_out[...] = g_all[...].reshape(g_out.shape)
    pr_out[...] = pr_all[...].reshape(pr_out.shape)

    def wait_pc(t, _):
        p = (c + t) % nc

        @pl.when(t > 0)
        def _():
            remote(p_code.at[0], pc_all.at[h, p], send_pc.at[0, 0], recv_pc.at[h, p], at(z, other, c)).wait_recv()

        remote(p_code.at[0], pc_all.at[other, p], send_pc.at[0, 0], recv_pc.at[other, p], at(z, other, c)).wait_recv()
        return 0

    lax.fori_loop(0, nc, wait_pc, 0)
    pc_out[...] = pc_all[...]

    swap_x.wait_send()
    swap_g.wait_send()

    def sent(t, _):
        ctx_copy(t).wait_send()
        line_copy(z_code.at[(z + t) % nz], z_recv.at[z], 1, t).wait_send()
        line_copy(phi_s, phi_c.at[h * nz + z], 2, t).wait_send()

        @pl.when((c + t) % nc != z)
        def _():
            pass_row(t).wait_send()

        plane_copy(pp_send.at[(c + t) % nc], pp_recv.at[c], 5, t).wait_send()
        plane_copy(p_own, pr_all.at[c], 6, t).wait_send()
        line_copy(gz_s, gz_r.at[z], 7, t).wait_send()
        line_copy(pz_s, pz_r.at[z], 8, t).wait_send()
        line_copy(p_code.at[0], p_z.at[z], 9, t).wait_send()
        plane_copy(g_s, g_all.at[c], 10, t).wait_send()
        return 0

    lax.fori_loop(1, nz, sent, 0)

    def sent_some(t, _):
        mate_copy(t).wait_send()
        col_copy(t, other).wait_send()

        @pl.when(t != c)
        def _():
            col_copy(t, h).wait_send()

        @pl.when(jnp.logical_and(holder, t != z))
        def _():
            remote(phi_r.at[t], phi_r.at[t], send.at[3, t], recv.at[4, t], at(z, h, t)).wait_send()

        return 0

    lax.fori_loop(0, nz, sent_some, 0)


def exchange(context, weight, bias, covariance, mean):
    rows_here, depth = context.shape
    n, m = covariance.shape
    nz, nc = lax.axis_size("row") // 2, lax.axis_size("col")
    b = rows_here * nc
    f32, bf16 = jnp.float32, jnp.bfloat16
    vmem, sem = pltpu.VMEM, pltpu.SemaphoreType
    scratch = [
        vmem((nc, rows_here, depth), bf16), vmem((b, depth), bf16), vmem((depth, m), bf16), vmem((1, m), f32),
        vmem((n, m), f32), vmem((1, n), f32), vmem((n, m), bf16), vmem((n, m), bf16), vmem((n, m), bf16),
        vmem((b // 2, m), f32), vmem((b // 2, m), f32), vmem((nz, 16, 256), f32), vmem((nz, 16, 256), bf16), vmem((nz, 16, 256), bf16),
        vmem((16, 256), bf16), vmem((2 * nz, 16, 256), bf16), vmem((16, 16, 256), bf16),
        vmem((nc, 8, n), f32), vmem((nc, 8, n), f32), vmem((8, n), f32), vmem((1, 8, n), bf16), vmem((16, b), f32), vmem((16, b), f32),
        vmem((8, b), f32), vmem((nz, 8, b), f32), vmem((1, b), f32), vmem((nz, 1, b), f32), vmem((8, b), f32), vmem((nc, 8, b), f32),
        vmem((nc, 8, n), f32), vmem((nz, 8, n), bf16), vmem((2, nc, 8, n), bf16),
        sem.DMA((5,)), sem.REGULAR, sem.DMA((2,)), sem.DMA((2,)), sem.DMA((11, 16)), sem.DMA((11, 16)), sem.DMA((2, 16)), sem.DMA((2, 16)), sem.DMA((2, 16)),
    ]
    return pl.pallas_call(
        exchange_kernel,
        in_specs=[pl.BlockSpec(memory_space=pl.ANY)] * 5,
        out_specs=[pl.BlockSpec(memory_space=pltpu.VMEM)] * 4,
        out_shape=[jax.ShapeDtypeStruct(s, f32) for s in ((b, b), (1, b), (b, n))] + [jax.ShapeDtypeStruct((2, nc, 8, n), bf16)],
        scratch_shapes=scratch,
        compiler_params=pltpu.CompilerParams(collective_id=0, has_side_effects=True),
    )(context, weight, bias, covariance, mean)


def per_device(context, weight, feature_bias, covariance, prior_mean, rewards):
    mean = prior_mean.reshape(1, -1)
    g, pred, pr, pc = exchange(context, weight, feature_bias.reshape(1, -1), covariance, mean)
    cov, mean = update(g, pred, rewards.reshape(1, -1), mean, pr, pc, covariance)
    return cov, mean.reshape(-1)


def solution(mesh):
    return jax.shard_map(
        per_device,
        mesh=mesh,
        in_specs=(P("col", "row"), P("row", "col"), P("col"), P("row", "col"), P("row"), P()),
        out_specs=(P("row", "col"), P("row")),
        check_vma=False,
    )
```

```python
import jax
import jax.numpy as jnp
from jax import lax
from jax.experimental import pallas as pl
from jax.experimental.pallas import tpu as pltpu
from jax.sharding import PartitionSpec as P

HI = lax.Precision.HIGHEST
MESH = pl.DeviceIdType.MESH


def split3(x):
    hi = x.astype(jnp.bfloat16)
    rest = x - hi.astype(jnp.float32)
    mid = rest.astype(jnp.bfloat16)
    lo = (rest - mid.astype(jnp.float32)).astype(jnp.bfloat16)
    return hi, mid, lo


def coded_sum(x):
    t = x * 16.0
    t2 = t * t
    t4 = t2 * t2
    return ((t4 * t4) * t2 * t).astype(jnp.bfloat16)


def coded_panel(x):
    t = x * 4.0
    t2 = t * t
    return ((t2 * t2) * t2 * t).astype(jnp.bfloat16)


def rooted(y, power, scale):
    y = y.astype(jnp.float32)
    v = jnp.exp(jnp.log(jnp.abs(y)) * (1.0 / power)) * (1.0 / scale)
    return jnp.where(y < 0, -v, v)


def sum_from(y):
    return rooted(y, 11, 16)


def panel_from(y):
    return rooted(y, 7, 4)


def inverse_of_2(a, b, c):
    scale = 1.0 / (a * c - b * b)
    return c * scale, -b * scale, a * scale


def inverse_of_4(m):
    a0, a1, a2 = inverse_of_2(m[0][0], m[0][1], m[1][1])
    t = [[a0 * m[0][2 + k] + a1 * m[1][2 + k] for k in range(2)], [a1 * m[0][2 + k] + a2 * m[1][2 + k] for k in range(2)]]
    s0 = m[2][2] - (m[0][2] * t[0][0] + m[1][2] * t[1][0])
    s1 = m[2][3] - (m[0][2] * t[0][1] + m[1][2] * t[1][1])
    s2 = m[3][3] - (m[0][3] * t[0][1] + m[1][3] * t[1][1])
    c0, c1, c2 = inverse_of_2(s0, s1, s2)
    u = [[t[i][0] * c0 + t[i][1] * c1, t[i][0] * c1 + t[i][1] * c2] for i in range(2)]
    b0 = a0 + u[0][0] * t[0][0] + u[0][1] * t[0][1]
    b1 = a1 + u[0][0] * t[1][0] + u[0][1] * t[1][1]
    b2 = a2 + u[1][0] * t[1][0] + u[1][1] * t[1][1]
    return [
        [b0, b1, -u[0][0], -u[0][1]],
        [b1, b2, -u[1][0], -u[1][1]],
        [-u[0][0], -u[1][0], c0, c1],
        [-u[0][1], -u[1][1], c1, c2],
    ]


def panel4(blocks, lo, lane, sub):
    n = blocks[0].shape[1]
    for j in range(lo, lo + 8 * len(blocks), 4):
        at, s = (j - lo) // 8, j % 8
        mine = blocks[at]
        cell = [[None] * 4 for _ in range(4)]
        for i in range(4):
            for k in range(i, 4):
                cell[i][k] = cell[k][i] = jnp.broadcast_to(mine[s + i : s + i + 1, j + k : j + k + 1], (8, n))
        inv = inverse_of_4(cell)
        inside = (lane >= j) & (lane < j + 4)
        rows = [
            jnp.where(inside, jnp.where(lane == j + m, 1.0, 0.0), jnp.broadcast_to(mine[s + m : s + m + 1], (8, n)))
            for m in range(4)
        ]
        out = [(inv[i][0] * rows[0] + inv[i][1] * rows[1]) + (inv[i][2] * rows[2] + inv[i][3] * rows[3]) for i in range(4)]
        new = []
        for i, block in enumerate(blocks):
            kept = jnp.where(inside, 0.0, block)
            cols = [jnp.broadcast_to(block[:, j + k : j + k + 1], (8, n)) for k in range(4)]
            if i == at:
                here = (sub >= s) & (sub < s + 4)
                kept = jnp.where(here, 0.0, kept)
                cols = [jnp.where(here, jnp.where(sub == s + k, -1.0, 0.0), cols[k]) for k in range(4)]
            new.append(kept - ((cols[0] * out[0] + cols[1] * out[1]) + (cols[2] * out[2] + cols[3] * out[3])))
        blocks = new
    return blocks


def dot3(a, b):
    ah, am, al = split3(a)
    bh, bm, bl = split3(b)
    return jnp.dot(jnp.concatenate([ah, ah, am, am, ah, al], 1), jnp.concatenate([bh, bm, bh, bm, bl, bh], 0), preferred_element_type=jnp.float32)


def eliminated(blocks, lo, w):
    n = blocks[0].shape[1]
    lane = lax.broadcasted_iota(jnp.int32, (8, n), 1)
    sub = lax.broadcasted_iota(jnp.int32, (8, n), 0)
    first, last = lo // 8, (lo + w) // 8
    panel = panel4(blocks[first:last], lo, lane, sub)
    rest = blocks[:first] + blocks[last:]
    cols = jnp.concatenate([b[:, lo : lo + w] for b in rest], 0)
    prod = dot3(cols, jnp.concatenate(panel, 0))
    inside = (lane >= lo) & (lane < lo + w)
    rest = [jnp.where(inside, 0.0, b) - prod[8 * i : 8 * i + 8] for i, b in enumerate(rest)]
    return rest[:first] + panel + rest[first:]


def update_kernel(gain_ref, pc_ref, shift_ref, mean_ref, cov_ref, out_ref, outm_ref):
    out_ref[...] = cov_ref[...] - jnp.dot(gain_ref[...], pc_ref[...], preferred_element_type=jnp.float32)

    @pl.when(pl.program_id(0) == 0)
    def _():
        outm_ref[...] = mean_ref[...] + shift_ref[...]


def update(gain, panel, shift, mean, cov, steps=4):
    n, m = cov.shape
    rows = n // steps
    whole = lambda *shape: pl.BlockSpec(shape, lambda i: (0,) * len(shape))
    cut = lambda width: pl.BlockSpec((rows, width), lambda i: (i, 0))
    return pl.pallas_call(
        update_kernel,
        grid=(steps,),
        in_specs=[cut(gain.shape[1]), whole(*panel.shape), whole(1, n), whole(1, n), cut(m)],
        out_specs=[cut(m), whole(1, n)],
        out_shape=[jax.ShapeDtypeStruct((n, m), jnp.float32), jax.ShapeDtypeStruct((1, n), jnp.float32)],
    )(gain, panel, shift, mean, cov)


def far_first(t, n):
    return n // 2 + (1 - 2 * (t % 2)) * ((t + 1) // 2)


def near_first(t, n):
    return far_first(n - 2 - t, n)


def exchange_kernel(
    ctx_hbm, w_hbm, bias_hbm, cov_hbm, mean_hbm, rew_hbm,
    gain_out, pc_out, shift_out,
    ctx_all, ctx_m, w_v, bias_v, cov_v, mean_v, rew_v, c_hi, c_mid,
    x_send, x_recv, z_send, z_code, z_recv, phi_s, phi_c, phi_r,
    pp_send, pp_recv, p_own, p_code, gz_s, gz_r, pz_s, pz_r, g_s, g_all, pred_s, pred_r,
    pr_all, p_z, pc_all,
    local, near, pair_s, pair_r, send, recv, mate, send_pc, recv_pc, send_g, recv_g,
):
    nz, nc, nb = z_recv.shape[0], ctx_all.shape[0], 4
    r, c = lax.axis_index("row"), lax.axis_index("col")
    z, h = r // 2, r % 2
    other = 1 - h

    def at(zz, hh, cc):
        return (zz * 2 + hh, cc)

    def remote(src, dst, s_sem, r_sem, where):
        return pltpu.make_async_remote_copy(
            src_ref=src, dst_ref=dst, send_sem=s_sem, recv_sem=r_sem, device_id=where, device_id_type=MESH
        )

    loads = [
        pltpu.make_async_copy(ctx_hbm, ctx_all.at[c], local.at[0]),
        pltpu.make_async_copy(cov_hbm, cov_v, local.at[1]),
        pltpu.make_async_copy(w_hbm, w_v, local.at[2]),
        pltpu.make_async_copy(bias_hbm, bias_v, local.at[3]),
        pltpu.make_async_copy(mean_hbm, mean_v, local.at[4]),
        pltpu.make_async_copy(rew_hbm, rew_v, local.at[5]),
    ]
    for load in loads:
        load.start()

    barrier = pltpu.get_barrier_semaphore()

    def greet(where):
        pl.semaphore_signal(barrier, inc=1, device_id=where, device_id_type=MESH)

    def greet_plane(t, _):
        greet(at(z, h, (c + t) % nc))
        return 0

    def greet_line(t, _):
        greet(at((z + t) % nz, h, c))
        greet(at((z - t + nz) % nz, h, c))
        greet(at((z + t) % nz, other, c))
        greet(at((z - t + nz) % nz, other, c))
        return 0

    lax.fori_loop(1, nc, greet_plane, 0)
    lax.fori_loop(1, nb + 1, greet_line, 0)
    greet(at(z, other, c))
    pl.semaphore_wait(barrier, nc - 1 + 4 * nb + 1)
    pl.semaphore_signal(near, inc=1, device_id=at((z + nb) % nz, h, c), device_id_type=MESH)
    pl.semaphore_signal(near, inc=1, device_id=at((z - nb + nz) % nz, h, c), device_id_type=MESH)

    def ctx_copy(t):
        return remote(ctx_hbm, ctx_all.at[c], send.at[0, t], recv.at[0, c], at(z, h, (c + t) % nc))

    def plane_arrival(buf, phase, src):
        return remote(buf.at[src], buf.at[src], send.at[phase, 0], recv.at[phase, src], at(z, other, c))

    def start_ctx(t, _):
        ctx_copy(t).start()
        return 0

    lax.fori_loop(1, nc, start_ctx, 0)

    loads[1].wait()
    rows = cov_v.shape[0]
    for i in range(rows // 128):
        cut = slice(i * 128, i * 128 + 128)
        hi, mid, _ = split3(cov_v[cut, :].T)
        c_hi[:, cut] = hi
        c_mid[:, cut] = mid
    for load in loads[:1] + loads[2:]:
        load.wait()

    def wait_ctx(t, _):
        plane_arrival(ctx_all, 0, (c + t) % nc).wait_recv()
        return 0

    lax.fori_loop(1, nc, wait_ctx, 0)
    tokens, depth = ctx_m.shape
    half = tokens // 2
    ctx_m[...] = ctx_all[...].astype(jnp.float32).reshape(tokens, depth).astype(jnp.bfloat16)

    theirs = ctx_m[pl.ds(pl.multiple_of(other * half, half), half), :]
    mine = ctx_m[pl.ds(pl.multiple_of(h * half, half), half), :]

    def line_copy(src, dst, phase, t):
        return remote(src, dst, send.at[phase, t], recv.at[phase, z], at((z + t) % nz, h, c))

    def line_arrival(buf, phase, src):
        return remote(buf.at[src], buf.at[src], send.at[phase, 0], recv.at[phase, src], at(z, other, c))

    def columns(block):
        return w_v[:, pl.ds(pl.multiple_of(block * 256, 256), 256)]

    def swap_x(block):
        return remote(x_send.at[block], x_recv.at[block], pair_s.at[block], pair_r.at[block], at(z, other, c))

    order = [(z + t) % 4 for t in (0, 1, 3, 2)]
    for block in order:
        x_send[block] = jnp.dot(theirs, columns(block), preferred_element_type=jnp.float32)
        swap_x(block).start()
    for t, block in zip((0, 1, 3, 2), order):
        z_send[block] = jnp.dot(mine, columns(block), preferred_element_type=jnp.float32)
    pl.semaphore_wait(near, 2)
    for t, block in zip((0, 1, 3, 2), order):
        swap_x(block).wait_recv()
        both = z_send[block] + x_recv[block]
        z_send[block] = both
        z_code[block] = coded_sum(both).reshape(4, 16, 256)

        def start_z(i, _):
            step = t + (i * 4 + 8) % nz
            row = (z + step) % nz // 4

            @pl.when(step > 0)
            def _():
                remote(
                    z_code.at[block, row], z_recv.at[z], send.at[1, step], recv.at[1, z], at((z + step) % nz, h, c)
                ).start()

            return 0

        lax.fori_loop(0, 4, start_z, 0)

    def add_z(t, acc):
        zz = (z + near_first(t, nz)) % nz
        line_arrival(z_recv, 1, zz).wait_recv()
        return acc + sum_from(z_recv[zz])

    kb = z % 4
    own = z_send[kb, pl.ds(pl.multiple_of(z // 4 * 16, 16), 16), :]
    total = lax.fori_loop(0, nz - 1, add_z, own)
    total = total + bias_v[:, pl.ds(pl.multiple_of(kb * 256, 256), 256)]
    phi = jnp.tanh(total).astype(jnp.bfloat16)
    phi_s[...] = phi

    def start_phi(t, _):
        t = far_first(t, nz)
        line_copy(phi_s, phi_c.at[h * nz + z], 2, t).start()
        return 0

    lax.fori_loop(0, nz - 1, start_phi, 0)

    def mate_copy(k):
        return remote(phi_c.at[h * nz + k], phi_c.at[h * nz + k], mate.at[0, k], mate.at[1, k], at(z, other, c))

    def plane_copy(src, dst, phase, t):
        return remote(src, dst, send.at[phase, t], recv.at[phase, c], at(z, h, (c + t) % nc))

    holder = c == z

    def push(core, k):
        column = k % 4
        slot = core * 8 + k // 4 * 2 + column % 2

        @pl.when(jnp.logical_and(holder, column // 2 == h))
        def _():
            phi_r[slot] = phi_c[core * nz + k]

            @pl.when(slot != z)
            def _():
                remote(phi_c.at[core * nz + k], phi_r.at[slot], send.at[3, slot], recv.at[4, slot], at(z, h, slot)).start()

    phi_c[h * nz + z] = phi
    mate_copy(z).start()
    push(h, z)

    def pass_mate(t, _):
        zz = (z + near_first(t, nz)) % nz
        remote(phi_s, phi_c.at[h * nz + zz], send.at[2, 0], recv.at[2, zz], at(z, other, c)).wait_recv()
        mate_copy(zz).start()
        push(h, zz)
        return 0

    lax.fori_loop(0, nz - 1, pass_mate, 0)

    def wait_mate(t, _):
        k = (z + near_first(t - 1, nz)) % nz
        k = jnp.where(t == 0, z, k)
        i = other * nz + k
        remote(phi_c.at[i], phi_c.at[i], mate.at[0, k], mate.at[1, k], at(z, other, c)).wait_recv()
        push(other, k)
        return 0

    lax.fori_loop(0, nz, wait_mate, 0)

    part = None
    for k in range(4):
        lhs = jnp.concatenate([phi_c[i * 4 + k] for i in range(8)], 0)
        for term in (c_hi, c_mid):
            prod = jnp.dot(lhs, term[k * 256 : k * 256 + 256, :], preferred_element_type=jnp.float32)
            part = prod if part is None else part + prod
    pp_send[...] = part.reshape(pp_send.shape)

    def start_pp(t, _):
        plane_copy(pp_send.at[(c + t) % nc], pp_recv.at[c], 5, t).start()
        return 0

    lax.fori_loop(1, nc, start_pp, 0)
    pp_recv[c] = pp_send[c]

    def pass_row(t):
        return plane_copy(phi_r.at[c], phi_r.at[c], 4, t)

    @pl.when(jnp.logical_not(holder))
    def _():
        plane_arrival(phi_r, 4, c).wait_recv()

    def start_row(t, _):
        @pl.when((c + t) % nc != z)
        def _():
            pass_row(t).start()

        return 0

    lax.fori_loop(1, nc, start_row, 0)

    def wait_row(t, _):
        @pl.when(jnp.logical_not(holder))
        def _():
            plane_arrival(phi_r, 4, (c + t) % nc).wait_recv()

        return 0

    def wait_pp(t, _):
        plane_arrival(pp_recv, 5, (c + t) % nc).wait_recv()
        return 0

    lax.fori_loop(1, nc, wait_pp, 0)
    p_mine = jnp.sum(pp_recv[...], axis=0)
    p_own[...] = p_mine
    p_code[0] = coded_panel(p_mine)
    lax.fori_loop(1, nc, wait_row, 0)

    width = p_mine.shape[1]
    zeros = jnp.zeros((7, width), jnp.float32)
    terms = split3(jnp.concatenate([p_mine, mean_v[...], zeros], 0))
    stacked = jnp.concatenate(terms, 0)
    gram = None
    for k in range(2):
        rhs = jnp.concatenate([phi_r[i * 2 + k] for i in range(8)], 0)
        prod = lax.dot_general(
            stacked[:, k * 256 : k * 256 + 256], rhs, (((1,), (1,)), ((), ())), preferred_element_type=jnp.float32
        )
        gram = prod if gram is None else gram + prod
    both = gram[:16] + gram[16:32] + gram[32:]
    gz_s[...] = both[:8]
    pz_s[...] = both[8:9]
    p_z[z] = p_code[0]

    def start_gz(t, _):
        t = far_first(t, nz)
        line_copy(gz_s, gz_r.at[z], 7, t).start()
        line_copy(pz_s, pz_r.at[z], 8, t).start()
        return 0

    lax.fori_loop(0, nz - 1, start_gz, 0)
    gz_r[z] = both[:8]
    pz_r[z] = both[8:9]

    def start_pz(t, _):
        t = far_first(t, nz)
        line_copy(p_code.at[0], p_z.at[z], 9, t).start()
        return 0

    lax.fori_loop(0, nz - 1, start_pz, 0)

    def wait_gz(t, _):
        zz = (z + t) % nz
        line_arrival(gz_r, 7, zz).wait_recv()
        line_arrival(pz_r, 8, zz).wait_recv()
        return 0

    lax.fori_loop(1, nz, wait_gz, 0)
    g_s[...] = jnp.sum(gz_r[...], axis=0)
    pred_s[...] = jnp.sum(pz_r[...], axis=0)
    swap_pred = remote(pred_s, pred_r, pair_s.at[4], pair_r.at[4], at(z, other, c))
    swap_pred.start()

    def g_copy(t, core):
        return remote(g_s, g_all.at[h, c], send_g.at[core, t], recv_g.at[h, c], at(z, core, (c + t) % nc))

    def g_arrival(core, p):
        return remote(g_s, g_all.at[core, p], send_g.at[0, 0], recv_g.at[core, p], at(z, other, c))

    def start_g(t, _):
        @pl.when(t > 0)
        def _():
            g_copy(t, h).start()

        g_copy(t, other).start()
        return 0

    lax.fori_loop(0, nc, start_g, 0)
    g_all[h, c] = g_s[...]

    def start_pr(t, _):
        plane_copy(p_own, pr_all.at[c], 6, t).start()
        return 0

    lax.fori_loop(1, nc, start_pr, 0)
    pr_all[c] = p_own[...]

    def wait_g(t, _):
        p = (c + t) % nc

        @pl.when(t > 0)
        def _():
            g_arrival(h, p).wait_recv()

        g_arrival(other, p).wait_recv()
        return 0

    lax.fori_loop(0, nc, wait_g, 0)
    eye = (lax.broadcasted_iota(jnp.int32, (tokens, tokens), 0) == lax.broadcasted_iota(jnp.int32, (tokens, tokens), 1)).astype(jnp.float32)
    g = (g_all[0] + g_all[1]).reshape(tokens, tokens) + eye
    blocks = [g[8 * i : 8 * i + 8] for i in range(tokens // 8)]
    for lo in range(0, 48, 16):
        blocks = eliminated(blocks, lo, 16)

    def col_copy(zz, core):
        return remote(p_z.at[zz], pc_all.at[h, c], send_pc.at[core, zz], recv_pc.at[h, c], at(z, core, zz))

    def pass_pz(t, _):
        zz = (z + near_first(t - 1, nz)) % nz
        zz = jnp.where(t == 0, z, zz)

        @pl.when(t > 0)
        def _():
            line_arrival(p_z, 9, zz).wait_recv()

        @pl.when(zz == c)
        def _():
            pc_all[h, c] = p_z[zz]

        @pl.when(zz != c)
        def _():
            col_copy(zz, h).start()

        col_copy(zz, other).start()
        return 0

    lax.fori_loop(0, nz, pass_pz, 0)

    for lo in range(48, 96, 16):
        blocks = eliminated(blocks, lo, 16)

    def wait_last(t, _):
        p = (c + t) % nc
        plane_arrival(pr_all, 6, p).wait_recv()
        return 0

    lax.fori_loop(1, nc, wait_last, 0)

    def wait_pc(t, _):
        p = (c + t) % nc

        @pl.when(t > 0)
        def _():
            remote(p_code.at[0], pc_all.at[h, p], send_pc.at[0, 0], recv_pc.at[h, p], at(z, other, c)).wait_recv()

        remote(p_code.at[0], pc_all.at[other, p], send_pc.at[0, 0], recv_pc.at[other, p], at(z, other, c)).wait_recv()
        return 0

    lax.fori_loop(0, nc, wait_pc, 0)
    swap_pred.wait()

    for k in range(2):
        panel = panel_from(pc_all[k]).reshape(tokens, width)
        hi, mid, _ = split3(panel)
        cut = slice(k * width, k * width + width)
        pc_out[:tokens, cut] = hi
        pc_out[tokens : 2 * tokens, cut] = mid
        pc_out[2 * tokens :, cut] = hi
    pr = pr_all[...].reshape(tokens, width)
    pr_t = pr.T
    for lo in range(96, 128, 16):
        blocks = eliminated(blocks, lo, 16)
    inv = jnp.concatenate(blocks, 0)
    gain = jnp.dot(pr_t, inv, precision=HI, preferred_element_type=jnp.float32)
    hi, mid, _ = split3(gain)
    gain_out[:, :tokens] = hi
    gain_out[:, tokens : 2 * tokens] = hi
    gain_out[:, 2 * tokens :] = mid
    diff = rew_v[...] - (pred_s[...] + pred_r[...])
    coeffs = jnp.dot(jnp.broadcast_to(diff, (8, tokens)), inv, precision=HI, preferred_element_type=jnp.float32)
    shift_out[...] = jnp.dot(coeffs, pr, precision=HI, preferred_element_type=jnp.float32)[:1]

    for block in range(4):
        swap_x(block).wait_send()

    def sent(t, _):
        ctx_copy(t).wait_send()
        remote(phi_s, z_recv.at[z], send.at[1, t], recv.at[1, z], at((z + t) % nz, h, c)).wait_send()
        line_copy(phi_s, phi_c.at[h * nz + z], 2, t).wait_send()

        @pl.when((c + t) % nc != z)
        def _():
            pass_row(t).wait_send()

        plane_copy(pp_send.at[(c + t) % nc], pp_recv.at[c], 5, t).wait_send()
        plane_copy(p_own, pr_all.at[c], 6, t).wait_send()
        line_copy(gz_s, gz_r.at[z], 7, t).wait_send()
        line_copy(pz_s, pz_r.at[z], 8, t).wait_send()
        line_copy(p_code.at[0], p_z.at[z], 9, t).wait_send()
        g_copy(t, h).wait_send()
        return 0

    lax.fori_loop(1, nz, sent, 0)

    def sent_some(t, _):
        mate_copy(t).wait_send()
        col_copy(t, other).wait_send()
        g_copy(t, other).wait_send()

        @pl.when(t != c)
        def _():
            col_copy(t, h).wait_send()

        @pl.when(jnp.logical_and(holder, t != z))
        def _():
            remote(phi_r.at[t], phi_r.at[t], send.at[3, t], recv.at[4, t], at(z, h, t)).wait_send()

        return 0

    lax.fori_loop(0, nz, sent_some, 0)


def exchange(context, weight, bias, covariance, mean, rewards):
    rows_here, depth = context.shape
    n, m = covariance.shape
    nz, nc = lax.axis_size("row") // 2, lax.axis_size("col")
    b = rows_here * nc
    f32, bf16 = jnp.float32, jnp.bfloat16
    vmem, sem = pltpu.VMEM, pltpu.SemaphoreType
    scratch = [
        vmem((nc, rows_here, depth), bf16), vmem((b, depth), bf16), vmem((depth, m), bf16), vmem((1, m), f32),
        vmem((n, m), f32), vmem((1, n), f32), vmem((1, b), f32), vmem((m, n), bf16), vmem((m, n), bf16),
        vmem((4, b // 2, 256), f32), vmem((4, b // 2, 256), f32), vmem((4, b // 2, 256), f32),
        vmem((4, 4, 16, 256), bf16), vmem((nz, 16, 256), bf16),
        vmem((16, 256), bf16), vmem((2 * nz, 16, 256), bf16), vmem((16, 16, 256), bf16),
        vmem((nc, 8, n), f32), vmem((nc, 8, n), f32), vmem((8, n), f32), vmem((1, 8, n), bf16),
        vmem((8, b), f32), vmem((nz, 8, b), f32), vmem((1, b), f32), vmem((nz, 1, b), f32), vmem((8, b), f32), vmem((2, nc, 8, b), f32),
        vmem((1, b), f32), vmem((1, b), f32),
        vmem((nc, 8, n), f32), vmem((nz, 8, n), bf16), vmem((2, nc, 8, n), bf16),
        sem.DMA((6,)), sem.REGULAR, sem.DMA((5,)), sem.DMA((5,)), sem.DMA((10, 16)), sem.DMA((10, 16)), sem.DMA((2, 16)),
        sem.DMA((2, 16)), sem.DMA((2, 16)), sem.DMA((2, 16)), sem.DMA((2, 16)),
    ]
    return pl.pallas_call(
        exchange_kernel,
        in_specs=[pl.BlockSpec(memory_space=pl.ANY)] * 6,
        out_specs=[pl.BlockSpec(memory_space=pltpu.VMEM)] * 3,
        out_shape=[
            jax.ShapeDtypeStruct((n, 3 * b), bf16), jax.ShapeDtypeStruct((3 * b, m), bf16), jax.ShapeDtypeStruct((1, n), f32),
        ],
        scratch_shapes=scratch,
        compiler_params=pltpu.CompilerParams(collective_id=0, has_side_effects=True),
    )(context, weight, bias, covariance, mean, rewards)


def per_device(context, weight, feature_bias, covariance, prior_mean, rewards):
    mean = prior_mean.reshape(1, -1)
    gain, panel, shift = exchange(context, weight, feature_bias.reshape(1, -1), covariance, mean, rewards.reshape(1, -1))
    cov, mean = update(gain, panel, shift, mean, covariance)
    return cov, mean.reshape(-1)


def solution(mesh):
    return jax.shard_map(
        per_device,
        mesh=mesh,
        in_specs=(P("col", "row"), P("row", "col"), P("col"), P("row", "col"), P("row"), P()),
        out_specs=(P("row", "col"), P("row")),
        check_vma=False,
    )
```

```python
import jax
import jax.numpy as jnp
from jax import lax
from jax.experimental import pallas as pl
from jax.experimental.pallas import tpu as pltpu
from jax.sharding import PartitionSpec as P

HI = lax.Precision.HIGHEST
MESH = pl.DeviceIdType.MESH


def split3(x):
    hi = x.astype(jnp.bfloat16)
    rest = x - hi.astype(jnp.float32)
    mid = rest.astype(jnp.bfloat16)
    lo = (rest - mid.astype(jnp.float32)).astype(jnp.bfloat16)
    return hi, mid, lo


def coded_sum(x):
    t = x * 16.0
    t2 = t * t
    t4 = t2 * t2
    return ((t4 * t4) * t2 * t).astype(jnp.bfloat16)


def coded_panel(x):
    t = x * 4.0
    t2 = t * t
    return ((t2 * t2) * t2 * t).astype(jnp.bfloat16)


def rooted(y, power, scale):
    y = y.astype(jnp.float32)
    v = jnp.exp(jnp.log(jnp.abs(y)) * (1.0 / power)) * (1.0 / scale)
    return jnp.where(y < 0, -v, v)


def sum_from(y):
    return rooted(y, 11, 16)


def panel_from(y):
    return rooted(y, 7, 4)


def inverse_of_2(a, b, c):
    scale = 1.0 / (a * c - b * b)
    return c * scale, -b * scale, a * scale


def inverse_of_4(m):
    a0, a1, a2 = inverse_of_2(m[0][0], m[0][1], m[1][1])
    t = [[a0 * m[0][2 + k] + a1 * m[1][2 + k] for k in range(2)], [a1 * m[0][2 + k] + a2 * m[1][2 + k] for k in range(2)]]
    s0 = m[2][2] - (m[0][2] * t[0][0] + m[1][2] * t[1][0])
    s1 = m[2][3] - (m[0][2] * t[0][1] + m[1][2] * t[1][1])
    s2 = m[3][3] - (m[0][3] * t[0][1] + m[1][3] * t[1][1])
    c0, c1, c2 = inverse_of_2(s0, s1, s2)
    u = [[t[i][0] * c0 + t[i][1] * c1, t[i][0] * c1 + t[i][1] * c2] for i in range(2)]
    b0 = a0 + u[0][0] * t[0][0] + u[0][1] * t[0][1]
    b1 = a1 + u[0][0] * t[1][0] + u[0][1] * t[1][1]
    b2 = a2 + u[1][0] * t[1][0] + u[1][1] * t[1][1]
    return [
        [b0, b1, -u[0][0], -u[0][1]],
        [b1, b2, -u[1][0], -u[1][1]],
        [-u[0][0], -u[1][0], c0, c1],
        [-u[0][1], -u[1][1], c1, c2],
    ]


def panel4(blocks, lo, lane, sub):
    n = blocks[0].shape[1]
    for j in range(lo, lo + 8 * len(blocks), 4):
        at, s = (j - lo) // 8, j % 8
        mine = blocks[at]
        cell = [[None] * 4 for _ in range(4)]
        for i in range(4):
            for k in range(i, 4):
                cell[i][k] = cell[k][i] = jnp.broadcast_to(mine[s + i : s + i + 1, j + k : j + k + 1], (8, n))
        inv = inverse_of_4(cell)
        inside = (lane >= j) & (lane < j + 4)
        rows = [
            jnp.where(inside, jnp.where(lane == j + m, 1.0, 0.0), jnp.broadcast_to(mine[s + m : s + m + 1], (8, n)))
            for m in range(4)
        ]
        out = [(inv[i][0] * rows[0] + inv[i][1] * rows[1]) + (inv[i][2] * rows[2] + inv[i][3] * rows[3]) for i in range(4)]
        new = []
        for i, block in enumerate(blocks):
            kept = jnp.where(inside, 0.0, block)
            cols = [jnp.broadcast_to(block[:, j + k : j + k + 1], (8, n)) for k in range(4)]
            if i == at:
                here = (sub >= s) & (sub < s + 4)
                kept = jnp.where(here, 0.0, kept)
                cols = [jnp.where(here, jnp.where(sub == s + k, -1.0, 0.0), cols[k]) for k in range(4)]
            new.append(kept - ((cols[0] * out[0] + cols[1] * out[1]) + (cols[2] * out[2] + cols[3] * out[3])))
        blocks = new
    return blocks


def dot3(a, b):
    ah, am, al = split3(a)
    bh, bm, bl = split3(b)
    return jnp.dot(jnp.concatenate([ah, ah, am, am, ah, al], 1), jnp.concatenate([bh, bm, bh, bm, bl, bh], 0), preferred_element_type=jnp.float32)


def eliminated(blocks, lo, w):
    n = blocks[0].shape[1]
    lane = lax.broadcasted_iota(jnp.int32, (8, n), 1)
    sub = lax.broadcasted_iota(jnp.int32, (8, n), 0)
    first, last = lo // 8, (lo + w) // 8
    panel = panel4(blocks[first:last], lo, lane, sub)
    rest = blocks[:first] + blocks[last:]
    cols = jnp.concatenate([b[:, lo : lo + w] for b in rest], 0)
    prod = dot3(cols, jnp.concatenate(panel, 0))
    inside = (lane >= lo) & (lane < lo + w)
    rest = [jnp.where(inside, 0.0, b) - prod[8 * i : 8 * i + 8] for i, b in enumerate(rest)]
    return rest[:first] + panel + rest[first:]


def update_kernel(gain_ref, pc_ref, shift_ref, mean_ref, cov_ref, out_ref, outm_ref):
    out_ref[...] = cov_ref[...] - jnp.dot(gain_ref[...], pc_ref[...], preferred_element_type=jnp.float32)

    @pl.when(pl.program_id(0) == 0)
    def _():
        outm_ref[...] = mean_ref[...] + shift_ref[...]


def update(gain, panel, shift, mean, cov, steps=4):
    n, m = cov.shape
    width = m // steps
    whole = lambda *shape: pl.BlockSpec(shape, lambda i: (0,) * len(shape))
    cut = lambda rows: pl.BlockSpec((rows, width), lambda i: (0, i))
    return pl.pallas_call(
        update_kernel,
        grid=(steps,),
        in_specs=[whole(*gain.shape), cut(panel.shape[0]), whole(1, n), whole(1, n), cut(n)],
        out_specs=[cut(n), whole(1, n)],
        out_shape=[jax.ShapeDtypeStruct((n, m), jnp.float32), jax.ShapeDtypeStruct((1, n), jnp.float32)],
    )(gain, panel, shift, mean, cov)


def far_first(t, n):
    return n // 2 + (1 - 2 * (t % 2)) * ((t + 1) // 2)


def near_first(t, n):
    return far_first(n - 2 - t, n)


def exchange_kernel(
    ctx_hbm, w_hbm, bias_hbm, cov_hbm, mean_hbm, rew_hbm,
    gain_out, pc_out, shift_out,
    ctx_all, ctx_m, w_v, bias_v, cov_v, mean_v, rew_v, c_hi, c_mid,
    x_send, x_recv, z_send, z_code, z_recv, phi_s, phi_c, phi_r,
    pp_send, pp_recv, p_own, p_code, gz_s, gz_r, pz_s, pz_r, g_s, g_all, pred_s, pred_r,
    pr_all, p_z, pc_all,
    local, near, pair_s, pair_r, send, recv, mate, send_pc, recv_pc, send_g, recv_g,
):
    nz, nc, nb = z_recv.shape[0], ctx_all.shape[0], 4
    r, c = lax.axis_index("row"), lax.axis_index("col")
    z, h = r // 2, r % 2
    other = 1 - h

    def at(zz, hh, cc):
        return (zz * 2 + hh, cc)

    def remote(src, dst, s_sem, r_sem, where):
        return pltpu.make_async_remote_copy(
            src_ref=src, dst_ref=dst, send_sem=s_sem, recv_sem=r_sem, device_id=where, device_id_type=MESH
        )

    loads = [
        pltpu.make_async_copy(ctx_hbm, ctx_all.at[c], local.at[0]),
        pltpu.make_async_copy(cov_hbm, cov_v, local.at[1]),
        pltpu.make_async_copy(w_hbm, w_v, local.at[2]),
        pltpu.make_async_copy(bias_hbm, bias_v, local.at[3]),
        pltpu.make_async_copy(mean_hbm, mean_v, local.at[4]),
        pltpu.make_async_copy(rew_hbm, rew_v, local.at[5]),
    ]
    for load in loads:
        load.start()

    barrier = pltpu.get_barrier_semaphore()

    def greet(where):
        pl.semaphore_signal(barrier, inc=1, device_id=where, device_id_type=MESH)

    def greet_plane(t, _):
        greet(at(z, h, (c + t) % nc))
        return 0

    def greet_line(t, _):
        greet(at((z + t) % nz, h, c))
        greet(at((z - t + nz) % nz, h, c))
        greet(at((z + t) % nz, other, c))
        greet(at((z - t + nz) % nz, other, c))
        return 0

    lax.fori_loop(1, nc, greet_plane, 0)
    lax.fori_loop(1, nb + 1, greet_line, 0)
    greet(at(z, other, c))
    pl.semaphore_wait(barrier, nc - 1 + 4 * nb + 1)
    pl.semaphore_signal(near, inc=1, device_id=at((z + nb) % nz, h, c), device_id_type=MESH)
    pl.semaphore_signal(near, inc=1, device_id=at((z - nb + nz) % nz, h, c), device_id_type=MESH)

    def ctx_copy(t):
        return remote(ctx_hbm, ctx_all.at[c], send.at[0, t], recv.at[0, c], at(z, h, (c + t) % nc))

    def plane_arrival(buf, phase, src):
        return remote(buf.at[src], buf.at[src], send.at[phase, 0], recv.at[phase, src], at(z, other, c))

    def start_ctx(t, _):
        ctx_copy(t).start()
        return 0

    lax.fori_loop(1, nc, start_ctx, 0)

    for load in loads[:1] + loads[2:]:
        load.wait()

    def wait_ctx(t, _):
        plane_arrival(ctx_all, 0, (c + t) % nc).wait_recv()
        return 0

    lax.fori_loop(1, nc, wait_ctx, 0)
    tokens, depth = ctx_m.shape
    half = tokens // 2
    ctx_m[...] = ctx_all[...].astype(jnp.float32).reshape(tokens, depth).astype(jnp.bfloat16)

    def line_copy(src, dst, phase, t):
        return remote(src, dst, send.at[phase, t], recv.at[phase, z], at((z + t) % nz, h, c))

    def line_arrival(buf, phase, src):
        return remote(buf.at[src], buf.at[src], send.at[phase, 0], recv.at[phase, src], at(z, other, c))

    def swap_x(block):
        theirs = pl.ds(pl.multiple_of(other * half, half), half)
        return remote(x_send.at[block, theirs], x_recv.at[block], pair_s.at[block], pair_r.at[block], at(z, other, c))

    for block in range(4):
        x_send[block] = jnp.dot(ctx_m[...], w_v[:, block * 256 : block * 256 + 256], preferred_element_type=jnp.float32)
        swap_x(block).start()
    own_rows = pl.ds(pl.multiple_of(h * half, half), half)
    for block in range(4):
        swap_x(block).wait_recv()
        both = x_send[block, own_rows, :] + x_recv[block]
        z_send[block] = both
        z_code[block] = coded_sum(both).reshape(4, 16, 256)
    pl.semaphore_wait(near, 2)

    def start_z(t, _):
        t = far_first(t, nz)
        k = (z + t) % nz
        line_copy(z_code.at[k % 4, k // 4], z_recv.at[z], 1, t).start()
        return 0

    lax.fori_loop(0, nz - 1, start_z, 0)

    loads[1].wait()
    rows = cov_v.shape[0]
    for i in range(rows // 128):
        cut = slice(i * 128, i * 128 + 128)
        hi, mid, _ = split3(cov_v[cut, :].T)
        c_hi[:, cut] = hi
        c_mid[:, cut] = mid

    def add_z(t, acc):
        zz = (z + near_first(t, nz)) % nz
        line_arrival(z_recv, 1, zz).wait_recv()
        return acc + sum_from(z_recv[zz])

    kb = z % 4
    own = z_send[kb, pl.ds(pl.multiple_of(z // 4 * 16, 16), 16), :]
    total = lax.fori_loop(0, nz - 1, add_z, own)
    total = total + bias_v[:, pl.ds(pl.multiple_of(kb * 256, 256), 256)]
    phi = jnp.tanh(total).astype(jnp.bfloat16)
    phi_s[...] = phi

    def start_phi(t, _):
        t = far_first(t, nz)
        line_copy(phi_s, phi_c.at[h * nz + z], 2, t).start()
        return 0

    lax.fori_loop(0, nz - 1, start_phi, 0)

    def mate_copy(k):
        return remote(phi_c.at[h * nz + k], phi_c.at[h * nz + k], mate.at[0, k], mate.at[1, k], at(z, other, c))

    def plane_copy(src, dst, phase, t):
        return remote(src, dst, send.at[phase, t], recv.at[phase, c], at(z, h, (c + t) % nc))

    holder = c == z

    def push(core, k):
        column = k % 4
        slot = core * 8 + k // 4 * 2 + column % 2

        @pl.when(jnp.logical_and(holder, column // 2 == h))
        def _():
            phi_r[slot] = phi_c[core * nz + k]

            @pl.when(slot != z)
            def _():
                remote(phi_c.at[core * nz + k], phi_r.at[slot], send.at[3, slot], recv.at[4, slot], at(z, h, slot)).start()

    phi_c[h * nz + z] = phi
    mate_copy(z).start()
    push(h, z)

    def pass_mate(t, _):
        zz = (z + near_first(t, nz)) % nz
        remote(phi_s, phi_c.at[h * nz + zz], send.at[2, 0], recv.at[2, zz], at(z, other, c)).wait_recv()
        mate_copy(zz).start()
        push(h, zz)
        return 0

    lax.fori_loop(0, nz - 1, pass_mate, 0)

    def wait_mate(t, _):
        k = (z + near_first(t - 1, nz)) % nz
        k = jnp.where(t == 0, z, k)
        i = other * nz + k
        remote(phi_c.at[i], phi_c.at[i], mate.at[0, k], mate.at[1, k], at(z, other, c)).wait_recv()
        push(other, k)
        return 0

    lax.fori_loop(0, nz, wait_mate, 0)

    part = None
    for k in range(4):
        lhs = jnp.concatenate([phi_c[i * 4 + k] for i in range(8)], 0)
        for term in (c_hi, c_mid):
            prod = jnp.dot(lhs, term[k * 256 : k * 256 + 256, :], preferred_element_type=jnp.float32)
            part = prod if part is None else part + prod
    pp_send[...] = part.reshape(pp_send.shape)

    def start_pp(t, _):
        plane_copy(pp_send.at[(c + t) % nc], pp_recv.at[c], 5, t).start()
        return 0

    lax.fori_loop(1, nc, start_pp, 0)
    pp_recv[c] = pp_send[c]

    def pass_row(t):
        return plane_copy(phi_r.at[c], phi_r.at[c], 4, t)

    @pl.when(jnp.logical_not(holder))
    def _():
        plane_arrival(phi_r, 4, c).wait_recv()

    def start_row(t, _):
        @pl.when((c + t) % nc != z)
        def _():
            pass_row(t).start()

        return 0

    lax.fori_loop(1, nc, start_row, 0)

    def wait_row(t, _):
        @pl.when(jnp.logical_not(holder))
        def _():
            plane_arrival(phi_r, 4, (c + t) % nc).wait_recv()

        return 0

    def wait_pp(t, _):
        plane_arrival(pp_recv, 5, (c + t) % nc).wait_recv()
        return 0

    lax.fori_loop(1, nc, wait_pp, 0)
    p_mine = jnp.sum(pp_recv[...], axis=0)
    p_own[...] = p_mine
    p_code[0] = coded_panel(p_mine)
    lax.fori_loop(1, nc, wait_row, 0)

    width = p_mine.shape[1]
    zeros = jnp.zeros((7, width), jnp.float32)
    terms = split3(jnp.concatenate([p_mine, mean_v[...], zeros], 0))
    stacked = jnp.concatenate(terms, 0)
    gram = None
    for k in range(2):
        rhs = jnp.concatenate([phi_r[i * 2 + k] for i in range(8)], 0)
        prod = lax.dot_general(
            stacked[:, k * 256 : k * 256 + 256], rhs, (((1,), (1,)), ((), ())), preferred_element_type=jnp.float32
        )
        gram = prod if gram is None else gram + prod
    both = gram[:16] + gram[16:32] + gram[32:]
    gz_s[...] = both[:8]
    pz_s[...] = both[8:9]
    p_z[z] = p_code[0]

    def start_gz(t, _):
        t = far_first(t, nz)
        line_copy(gz_s, gz_r.at[z], 7, t).start()
        line_copy(pz_s, pz_r.at[z], 8, t).start()
        return 0

    lax.fori_loop(0, nz - 1, start_gz, 0)
    gz_r[z] = both[:8]
    pz_r[z] = both[8:9]

    def start_pz(t, _):
        t = far_first(t, nz)
        line_copy(p_code.at[0], p_z.at[z], 9, t).start()
        return 0

    lax.fori_loop(0, nz - 1, start_pz, 0)

    def wait_gz(t, _):
        zz = (z + t) % nz
        line_arrival(gz_r, 7, zz).wait_recv()
        line_arrival(pz_r, 8, zz).wait_recv()
        return 0

    lax.fori_loop(1, nz, wait_gz, 0)
    g_s[...] = jnp.sum(gz_r[...], axis=0)
    pred_s[...] = jnp.sum(pz_r[...], axis=0)
    swap_pred = remote(pred_s, pred_r, pair_s.at[4], pair_r.at[4], at(z, other, c))
    swap_pred.start()

    def g_copy(t, core):
        return remote(g_s, g_all.at[h, c], send_g.at[core, t], recv_g.at[h, c], at(z, core, (c + t) % nc))

    def g_arrival(core, p):
        return remote(g_s, g_all.at[core, p], send_g.at[0, 0], recv_g.at[core, p], at(z, other, c))

    def start_g(t, _):
        @pl.when(t > 0)
        def _():
            g_copy(t, h).start()

        g_copy(t, other).start()
        return 0

    lax.fori_loop(0, nc, start_g, 0)
    g_all[h, c] = g_s[...]

    def start_pr(t, _):
        plane_copy(p_own, pr_all.at[c], 6, t).start()
        return 0

    lax.fori_loop(1, nc, start_pr, 0)
    pr_all[c] = p_own[...]

    def wait_g(t, _):
        p = (c + t) % nc

        @pl.when(t > 0)
        def _():
            g_arrival(h, p).wait_recv()

        g_arrival(other, p).wait_recv()
        return 0

    lax.fori_loop(0, nc, wait_g, 0)
    eye = (lax.broadcasted_iota(jnp.int32, (tokens, tokens), 0) == lax.broadcasted_iota(jnp.int32, (tokens, tokens), 1)).astype(jnp.float32)
    g = (g_all[0] + g_all[1]).reshape(tokens, tokens) + eye
    blocks = [g[8 * i : 8 * i + 8] for i in range(tokens // 8)]
    for lo in range(0, 48, 16):
        blocks = eliminated(blocks, lo, 16)

    def col_copy(zz, core):
        return remote(p_z.at[zz], pc_all.at[h, c], send_pc.at[core, zz], recv_pc.at[h, c], at(z, core, zz))

    def pass_pz(t, _):
        zz = (z + near_first(t - 1, nz)) % nz
        zz = jnp.where(t == 0, z, zz)

        @pl.when(t > 0)
        def _():
            line_arrival(p_z, 9, zz).wait_recv()

        @pl.when(zz == c)
        def _():
            pc_all[h, c] = p_z[zz]

        @pl.when(zz != c)
        def _():
            col_copy(zz, h).start()

        col_copy(zz, other).start()
        return 0

    lax.fori_loop(0, nz, pass_pz, 0)

    for lo in range(48, 96, 16):
        blocks = eliminated(blocks, lo, 16)

    def wait_last(t, _):
        p = (c + t) % nc
        plane_arrival(pr_all, 6, p).wait_recv()
        return 0

    lax.fori_loop(1, nc, wait_last, 0)

    def wait_pc(t, _):
        p = (c + t) % nc

        @pl.when(t > 0)
        def _():
            remote(p_code.at[0], pc_all.at[h, p], send_pc.at[0, 0], recv_pc.at[h, p], at(z, other, c)).wait_recv()

        remote(p_code.at[0], pc_all.at[other, p], send_pc.at[0, 0], recv_pc.at[other, p], at(z, other, c)).wait_recv()
        return 0

    lax.fori_loop(0, nc, wait_pc, 0)
    swap_pred.wait()

    for k in range(2):
        panel = panel_from(pc_all[k]).reshape(tokens, width)
        hi, mid, _ = split3(panel)
        cut = slice(k * width, k * width + width)
        pc_out[:tokens, cut] = hi
        pc_out[tokens : 2 * tokens, cut] = mid
        pc_out[2 * tokens :, cut] = hi
    pr = pr_all[...].reshape(tokens, width)
    rh, rm, _ = split3(pr.T)
    pr_t = jnp.concatenate([rh, rh, rm], 1)
    for lo in range(96, 128, 16):
        blocks = eliminated(blocks, lo, 16)
    inv = jnp.concatenate(blocks, 0)
    ih, im, _ = split3(inv)
    gain = jnp.dot(pr_t, jnp.concatenate([ih, im, ih], 0), preferred_element_type=jnp.float32)
    hi, mid, _ = split3(gain)
    gain_out[:, :tokens] = hi
    gain_out[:, tokens : 2 * tokens] = hi
    gain_out[:, 2 * tokens :] = mid
    diff = rew_v[...] - (pred_s[...] + pred_r[...])
    coeffs = jnp.dot(jnp.broadcast_to(diff, (8, tokens)), inv, precision=HI, preferred_element_type=jnp.float32)
    shift_out[...] = jnp.dot(coeffs, pr, precision=HI, preferred_element_type=jnp.float32)[:1]

    for block in range(4):
        swap_x(block).wait_send()

    def sent(t, _):
        ctx_copy(t).wait_send()
        remote(phi_s, z_recv.at[z], send.at[1, t], recv.at[1, z], at((z + t) % nz, h, c)).wait_send()
        line_copy(phi_s, phi_c.at[h * nz + z], 2, t).wait_send()

        @pl.when((c + t) % nc != z)
        def _():
            pass_row(t).wait_send()

        plane_copy(pp_send.at[(c + t) % nc], pp_recv.at[c], 5, t).wait_send()
        plane_copy(p_own, pr_all.at[c], 6, t).wait_send()
        line_copy(gz_s, gz_r.at[z], 7, t).wait_send()
        line_copy(pz_s, pz_r.at[z], 8, t).wait_send()
        line_copy(p_code.at[0], p_z.at[z], 9, t).wait_send()
        g_copy(t, h).wait_send()
        return 0

    lax.fori_loop(1, nz, sent, 0)

    def sent_some(t, _):
        mate_copy(t).wait_send()
        col_copy(t, other).wait_send()
        g_copy(t, other).wait_send()

        @pl.when(t != c)
        def _():
            col_copy(t, h).wait_send()

        @pl.when(jnp.logical_and(holder, t != z))
        def _():
            remote(phi_r.at[t], phi_r.at[t], send.at[3, t], recv.at[4, t], at(z, h, t)).wait_send()

        return 0

    lax.fori_loop(0, nz, sent_some, 0)


def exchange(context, weight, bias, covariance, mean, rewards):
    rows_here, depth = context.shape
    n, m = covariance.shape
    nz, nc = lax.axis_size("row") // 2, lax.axis_size("col")
    b = rows_here * nc
    f32, bf16 = jnp.float32, jnp.bfloat16
    vmem, sem = pltpu.VMEM, pltpu.SemaphoreType
    scratch = [
        vmem((nc, rows_here, depth), bf16), vmem((b, depth), bf16), vmem((depth, m), bf16), vmem((1, m), f32),
        vmem((n, m), f32), vmem((1, n), f32), vmem((1, b), f32), vmem((m, n), bf16), vmem((m, n), bf16),
        vmem((4, b, 256), f32), vmem((4, b // 2, 256), f32), vmem((4, b // 2, 256), f32),
        vmem((4, 4, 16, 256), bf16), vmem((nz, 16, 256), bf16),
        vmem((16, 256), bf16), vmem((2 * nz, 16, 256), bf16), vmem((16, 16, 256), bf16),
        vmem((nc, 8, n), f32), vmem((nc, 8, n), f32), vmem((8, n), f32), vmem((1, 8, n), bf16),
        vmem((8, b), f32), vmem((nz, 8, b), f32), vmem((1, b), f32), vmem((nz, 1, b), f32), vmem((8, b), f32), vmem((2, nc, 8, b), f32),
        vmem((1, b), f32), vmem((1, b), f32),
        vmem((nc, 8, n), f32), vmem((nz, 8, n), bf16), vmem((2, nc, 8, n), bf16),
        sem.DMA((6,)), sem.REGULAR, sem.DMA((5,)), sem.DMA((5,)), sem.DMA((10, 16)), sem.DMA((10, 16)), sem.DMA((2, 16)),
        sem.DMA((2, 16)), sem.DMA((2, 16)), sem.DMA((2, 16)), sem.DMA((2, 16)),
    ]
    return pl.pallas_call(
        exchange_kernel,
        in_specs=[pl.BlockSpec(memory_space=pl.ANY)] * 6,
        out_specs=[pl.BlockSpec(memory_space=pltpu.VMEM)] * 3,
        out_shape=[
            jax.ShapeDtypeStruct((n, 3 * b), bf16), jax.ShapeDtypeStruct((3 * b, m), bf16), jax.ShapeDtypeStruct((1, n), f32),
        ],
        scratch_shapes=scratch,
        compiler_params=pltpu.CompilerParams(collective_id=0, has_side_effects=True),
    )(context, weight, bias, covariance, mean, rewards)


def per_device(context, weight, feature_bias, covariance, prior_mean, rewards):
    mean = prior_mean.reshape(1, -1)
    gain, panel, shift = exchange(context, weight, feature_bias.reshape(1, -1), covariance, mean, rewards.reshape(1, -1))
    cov, mean = update(gain, panel, shift, mean, covariance)
    return cov, mean.reshape(-1)


def solution(mesh):
    return jax.shard_map(
        per_device,
        mesh=mesh,
        in_specs=(P("col", "row"), P("row", "col"), P("col"), P("row", "col"), P("row"), P()),
        out_specs=(P("row", "col"), P("row")),
        check_vma=False,
    )
```

```python
import jax
import jax.numpy as jnp
from jax import lax
from jax.experimental import pallas as pl
from jax.experimental.pallas import tpu as pltpu
from jax.sharding import PartitionSpec as P

HI = lax.Precision.HIGHEST
MESH = pl.DeviceIdType.MESH


def split3(x):
    hi = x.astype(jnp.bfloat16)
    rest = x - hi.astype(jnp.float32)
    mid = rest.astype(jnp.bfloat16)
    lo = (rest - mid.astype(jnp.float32)).astype(jnp.bfloat16)
    return hi, mid, lo


def coded_sum(x):
    t = x * 16.0
    t2 = t * t
    t4 = t2 * t2
    return ((t4 * t4) * t2 * t).astype(jnp.bfloat16)


def coded_panel(x):
    t = x * 4.0
    t2 = t * t
    return ((t2 * t2) * t2 * t).astype(jnp.bfloat16)


def rooted(y, power, scale):
    y = y.astype(jnp.float32)
    v = jnp.exp(jnp.log(jnp.abs(y)) * (1.0 / power)) * (1.0 / scale)
    return jnp.where(y < 0, -v, v)


def sum_from(y):
    return rooted(y, 11, 16)


def panel_from(y):
    return rooted(y, 7, 4)


def inverse_of_2(a, b, c):
    scale = 1.0 / (a * c - b * b)
    return c * scale, -b * scale, a * scale


def inverse_of_4(m):
    a0, a1, a2 = inverse_of_2(m[0][0], m[0][1], m[1][1])
    t = [[a0 * m[0][2 + k] + a1 * m[1][2 + k] for k in range(2)], [a1 * m[0][2 + k] + a2 * m[1][2 + k] for k in range(2)]]
    s0 = m[2][2] - (m[0][2] * t[0][0] + m[1][2] * t[1][0])
    s1 = m[2][3] - (m[0][2] * t[0][1] + m[1][2] * t[1][1])
    s2 = m[3][3] - (m[0][3] * t[0][1] + m[1][3] * t[1][1])
    c0, c1, c2 = inverse_of_2(s0, s1, s2)
    u = [[t[i][0] * c0 + t[i][1] * c1, t[i][0] * c1 + t[i][1] * c2] for i in range(2)]
    b0 = a0 + u[0][0] * t[0][0] + u[0][1] * t[0][1]
    b1 = a1 + u[0][0] * t[1][0] + u[0][1] * t[1][1]
    b2 = a2 + u[1][0] * t[1][0] + u[1][1] * t[1][1]
    return [
        [b0, b1, -u[0][0], -u[0][1]],
        [b1, b2, -u[1][0], -u[1][1]],
        [-u[0][0], -u[1][0], c0, c1],
        [-u[0][1], -u[1][1], c1, c2],
    ]


def panel4(blocks, lo, lane, sub):
    n = blocks[0].shape[1]
    for j in range(lo, lo + 8 * len(blocks), 4):
        at, s = (j - lo) // 8, j % 8
        mine = blocks[at]
        cell = [[None] * 4 for _ in range(4)]
        for i in range(4):
            for k in range(i, 4):
                cell[i][k] = cell[k][i] = jnp.broadcast_to(mine[s + i : s + i + 1, j + k : j + k + 1], (8, n))
        inv = inverse_of_4(cell)
        inside = (lane >= j) & (lane < j + 4)
        rows = [
            jnp.where(inside, jnp.where(lane == j + m, 1.0, 0.0), jnp.broadcast_to(mine[s + m : s + m + 1], (8, n)))
            for m in range(4)
        ]
        out = [(inv[i][0] * rows[0] + inv[i][1] * rows[1]) + (inv[i][2] * rows[2] + inv[i][3] * rows[3]) for i in range(4)]
        new = []
        for i, block in enumerate(blocks):
            kept = jnp.where(inside, 0.0, block)
            cols = [jnp.broadcast_to(block[:, j + k : j + k + 1], (8, n)) for k in range(4)]
            if i == at:
                here = (sub >= s) & (sub < s + 4)
                kept = jnp.where(here, 0.0, kept)
                cols = [jnp.where(here, jnp.where(sub == s + k, -1.0, 0.0), cols[k]) for k in range(4)]
            new.append(kept - ((cols[0] * out[0] + cols[1] * out[1]) + (cols[2] * out[2] + cols[3] * out[3])))
        blocks = new
    return blocks


def dot3(a, b):
    ah, am, al = split3(a)
    bh, bm, bl = split3(b)
    return jnp.dot(jnp.concatenate([ah, ah, am, am, ah, al], 1), jnp.concatenate([bh, bm, bh, bm, bl, bh], 0), preferred_element_type=jnp.float32)


def eliminated(blocks, lo, w):
    n = blocks[0].shape[1]
    lane = lax.broadcasted_iota(jnp.int32, (8, n), 1)
    sub = lax.broadcasted_iota(jnp.int32, (8, n), 0)
    first, last = lo // 8, (lo + w) // 8
    panel = panel4(blocks[first:last], lo, lane, sub)
    rest = blocks[:first] + blocks[last:]
    cols = jnp.concatenate([b[:, lo : lo + w] for b in rest], 0)
    prod = dot3(cols, jnp.concatenate(panel, 0))
    inside = (lane >= lo) & (lane < lo + w)
    rest = [jnp.where(inside, 0.0, b) - prod[8 * i : 8 * i + 8] for i, b in enumerate(rest)]
    return rest[:first] + panel + rest[first:]


def update_kernel(gain_ref, pc_ref, shift_ref, mean_ref, cov_ref, out_ref, outm_ref):
    out_ref[...] = cov_ref[...] - jnp.dot(gain_ref[...], pc_ref[...], preferred_element_type=jnp.float32)

    @pl.when(pl.program_id(0) == 0)
    def _():
        outm_ref[...] = mean_ref[...] + shift_ref[...]


def update(gain, panel, shift, mean, cov, steps=4):
    n, m = cov.shape
    width = m // steps
    whole = lambda *shape: pl.BlockSpec(shape, lambda i: (0,) * len(shape))
    cut = lambda rows: pl.BlockSpec((rows, width), lambda i: (0, i))
    return pl.pallas_call(
        update_kernel,
        grid=(steps,),
        in_specs=[whole(*gain.shape), cut(panel.shape[0]), whole(1, n), whole(1, n), cut(n)],
        out_specs=[cut(n), whole(1, n)],
        out_shape=[jax.ShapeDtypeStruct((n, m), jnp.float32), jax.ShapeDtypeStruct((1, n), jnp.float32)],
    )(gain, panel, shift, mean, cov)


def far_first(t, n):
    return n // 2 + (1 - 2 * lax.rem(t, 2)) * lax.div(t + 1, 2)


def near_first(t, n):
    return far_first(n - 2 - t, n)


def exchange_kernel(
    ctx_hbm, w_hbm, bias_hbm, cov_hbm, mean_hbm, rew_hbm,
    gain_out, pc_out, shift_out,
    ctx_all, ctx_m, w_v, bias_v, cov_v, mean_v, rew_v, c_hi, c_mid,
    x_send, x_recv, z_send, z_code, z_recv, phi_s, phi_c, phi_r,
    pp_send, pp_recv, p_code, gz_s, gz_r, pz_s, pz_r, g_s, g_all, pred_s, pred_r,
    pr_all, p_z, pc_all,
    local, near, pair_s, pair_r, send, recv, mate, send_pc, recv_pc, send_g, recv_g,
):
    nz, nc, nb = z_recv.shape[0], ctx_all.shape[0], 4
    r, c = lax.axis_index("row"), lax.axis_index("col")
    z, h = lax.div(r, 2), lax.rem(r, 2)
    other = 1 - h

    def at(zz, hh, cc):
        return (zz * 2 + hh, cc)

    def remote(src, dst, s_sem, r_sem, where):
        return pltpu.make_async_remote_copy(
            src_ref=src, dst_ref=dst, send_sem=s_sem, recv_sem=r_sem, device_id=where, device_id_type=MESH
        )

    loads = [
        pltpu.make_async_copy(ctx_hbm, ctx_all.at[c], local.at[0]),
        pltpu.make_async_copy(cov_hbm, cov_v, local.at[1]),
        pltpu.make_async_copy(w_hbm, w_v, local.at[2]),
        pltpu.make_async_copy(bias_hbm, bias_v, local.at[3]),
        pltpu.make_async_copy(mean_hbm, mean_v, local.at[4]),
        pltpu.make_async_copy(rew_hbm, rew_v, local.at[5]),
    ]
    for load in loads:
        load.start()

    barrier = pltpu.get_barrier_semaphore()

    def greet(where):
        pl.semaphore_signal(barrier, inc=1, device_id=where, device_id_type=MESH)

    def greet_plane(t, _):
        greet(at(z, h, lax.rem(c + t, nc)))
        return 0

    def greet_line(t, _):
        greet(at(lax.rem(z + t, nz), h, c))
        greet(at(lax.rem(z - t + nz, nz), h, c))
        greet(at(lax.rem(z + t, nz), other, c))
        greet(at(lax.rem(z - t + nz, nz), other, c))
        return 0

    lax.fori_loop(1, nc, greet_plane, 0)
    lax.fori_loop(1, nb + 1, greet_line, 0)
    greet(at(z, other, c))
    pl.semaphore_wait(barrier, nc - 1 + 4 * nb + 1)
    pl.semaphore_signal(near, inc=1, device_id=at(lax.rem(z + nb, nz), h, c), device_id_type=MESH)
    pl.semaphore_signal(near, inc=1, device_id=at(lax.rem(z - nb + nz, nz), h, c), device_id_type=MESH)

    def ctx_copy(t):
        return remote(ctx_hbm, ctx_all.at[c], send.at[0, t], recv.at[0, c], at(z, h, lax.rem(c + t, nc)))

    def plane_arrival(buf, phase, src):
        return remote(buf.at[src], buf.at[src], send.at[phase, 0], recv.at[phase, src], at(z, other, c))

    def start_ctx(t, _):
        ctx_copy(t).start()
        return 0

    lax.fori_loop(1, nc, start_ctx, 0)

    for load in loads[:1] + loads[2:]:
        load.wait()

    def wait_ctx(t, _):
        plane_arrival(ctx_all, 0, lax.rem(c + t, nc)).wait_recv()
        return 0

    lax.fori_loop(1, nc, wait_ctx, 0)
    tokens, depth = ctx_m.shape
    half = tokens // 2
    ctx_m[...] = ctx_all[...].astype(jnp.float32).reshape(tokens, depth).astype(jnp.bfloat16)

    def line_copy(src, dst, phase, t):
        return remote(src, dst, send.at[phase, t], recv.at[phase, z], at(lax.rem(z + t, nz), h, c))

    def line_arrival(buf, phase, src):
        return remote(buf.at[src], buf.at[src], send.at[phase, 0], recv.at[phase, src], at(z, other, c))

    def swap_x(block):
        theirs = pl.ds(pl.multiple_of(other * half, half), half)
        return remote(x_send.at[block, theirs], x_recv.at[block], pair_s.at[block], pair_r.at[block], at(z, other, c))

    for block in range(4):
        x_send[block] = jnp.dot(ctx_m[...], w_v[:, block * 256 : block * 256 + 256], preferred_element_type=jnp.float32)
        swap_x(block).start()
    own_rows = pl.ds(pl.multiple_of(h * half, half), half)
    for block in range(4):
        swap_x(block).wait_recv()
        both = x_send[block, own_rows, :] + x_recv[block]
        z_send[block] = both
        z_code[block] = coded_sum(both).reshape(4, 16, 256)
    pl.semaphore_wait(near, 2)

    def start_z(t, _):
        t = far_first(t, nz)
        k = lax.rem(z + t, nz)
        line_copy(z_code.at[lax.rem(k, 4), lax.div(k, 4)], z_recv.at[z], 1, t).start()
        return 0

    lax.fori_loop(0, nz - 1, start_z, 0)

    loads[1].wait()
    rows = cov_v.shape[0]
    for i in range(rows // 128):
        cut = slice(i * 128, i * 128 + 128)
        hi, mid, _ = split3(cov_v[cut, :].T)
        c_hi[:, cut] = hi
        c_mid[:, cut] = mid

    def add_z(t, acc):
        zz = lax.rem(z + near_first(t, nz), nz)
        line_arrival(z_recv, 1, zz).wait_recv()
        return acc + sum_from(z_recv[zz])

    kb = lax.rem(z, 4)
    own = z_send[kb, pl.ds(pl.multiple_of(lax.div(z, 4) * 16, 16), 16), :]
    total = lax.fori_loop(0, nz - 1, add_z, own)
    total = total + bias_v[:, pl.ds(pl.multiple_of(kb * 256, 256), 256)]
    phi = jnp.tanh(total).astype(jnp.bfloat16)
    phi_s[...] = phi

    def start_phi(t, _):
        t = far_first(t, nz)
        line_copy(phi_s, phi_c.at[h * nz + z], 2, t).start()
        return 0

    lax.fori_loop(0, nz - 1, start_phi, 0)

    def mate_copy(k):
        return remote(phi_c.at[h * nz + k], phi_c.at[h * nz + k], mate.at[0, k], mate.at[1, k], at(z, other, c))

    def plane_copy(src, dst, phase, t):
        return remote(src, dst, send.at[phase, t], recv.at[phase, c], at(z, h, lax.rem(c + t, nc)))

    holder = c == z

    def push(core, k):
        column = lax.rem(k, 4)
        slot = core * 8 + lax.div(k, 4) * 2 + lax.rem(column, 2)

        @pl.when(jnp.logical_and(holder, lax.div(column, 2) == h))
        def _():
            phi_r[slot] = phi_c[core * nz + k]

            @pl.when(slot != z)
            def _():
                remote(phi_c.at[core * nz + k], phi_r.at[slot], send.at[3, slot], recv.at[4, slot], at(z, h, slot)).start()

    phi_c[h * nz + z] = phi
    mate_copy(z).start()
    push(h, z)

    def pass_mate(t, _):
        zz = lax.rem(z + near_first(t, nz), nz)
        remote(phi_s, phi_c.at[h * nz + zz], send.at[2, 0], recv.at[2, zz], at(z, other, c)).wait_recv()
        mate_copy(zz).start()
        push(h, zz)
        return 0

    lax.fori_loop(0, nz - 1, pass_mate, 0)

    def wait_mate(t, _):
        k = lax.rem(z + near_first(t - 1, nz), nz)
        i = other * nz + k
        remote(phi_c.at[i], phi_c.at[i], mate.at[0, k], mate.at[1, k], at(z, other, c)).wait_recv()
        push(other, k)
        return 0

    lax.fori_loop(0, nz, wait_mate, 0)

    part = None
    for k in range(4):
        lhs = jnp.concatenate([phi_c[i * 4 + k] for i in range(8)], 0)
        for term in (c_hi, c_mid):
            prod = jnp.dot(lhs, term[k * 256 : k * 256 + 256, :], preferred_element_type=jnp.float32)
            part = prod if part is None else part + prod
    pp_send[...] = coded_panel(part).reshape(pp_send.shape)

    def start_pp(t, _):
        plane_copy(pp_send.at[lax.rem(c + t, nc)], pp_recv.at[c], 5, t).start()
        return 0

    lax.fori_loop(1, nc, start_pp, 0)
    pp_recv[c] = pp_send[c]

    def pass_row(t):
        return plane_copy(phi_r.at[c], phi_r.at[c], 4, t)

    @pl.when(jnp.logical_not(holder))
    def _():
        plane_arrival(phi_r, 4, c).wait_recv()

    def start_row(t, _):
        @pl.when(lax.rem(c + t, nc) != z)
        def _():
            pass_row(t).start()

        return 0

    lax.fori_loop(1, nc, start_row, 0)

    def wait_row(t, _):
        @pl.when(jnp.logical_not(holder))
        def _():
            plane_arrival(phi_r, 4, lax.rem(c + t, nc)).wait_recv()

        return 0

    def wait_pp(t, _):
        plane_arrival(pp_recv, 5, lax.rem(c + t, nc)).wait_recv()
        return 0

    lax.fori_loop(1, nc, wait_pp, 0)
    p_mine = jnp.sum(panel_from(pp_recv[...]), axis=0)
    p_code[0] = coded_panel(p_mine)
    lax.fori_loop(1, nc, wait_row, 0)

    width = p_mine.shape[1]
    zeros = jnp.zeros((7, width), jnp.float32)
    terms = split3(jnp.concatenate([p_mine, mean_v[...], zeros], 0))
    stacked = jnp.concatenate(terms, 0)
    gram = None
    for k in range(2):
        rhs = jnp.concatenate([phi_r[i * 2 + k] for i in range(8)], 0)
        prod = lax.dot_general(
            stacked[:, k * 256 : k * 256 + 256], rhs, (((1,), (1,)), ((), ())), preferred_element_type=jnp.float32
        )
        gram = prod if gram is None else gram + prod
    both = gram[:16] + gram[16:32] + gram[32:]
    gz_s[...] = both[:8]
    pz_s[...] = both[8:9]
    p_z[z] = p_code[0]

    def start_gz(t, _):
        t = far_first(t, nz)
        line_copy(gz_s, gz_r.at[z], 7, t).start()
        line_copy(pz_s, pz_r.at[z], 8, t).start()
        return 0

    lax.fori_loop(0, nz - 1, start_gz, 0)
    gz_r[z] = both[:8]
    pz_r[z] = both[8:9]

    def start_pz(t, _):
        t = far_first(t, nz)
        line_copy(p_code.at[0], p_z.at[z], 9, t).start()
        return 0

    lax.fori_loop(0, nz - 1, start_pz, 0)

    def wait_gz(t, _):
        zz = lax.rem(z + t, nz)
        line_arrival(gz_r, 7, zz).wait_recv()
        line_arrival(pz_r, 8, zz).wait_recv()
        return 0

    lax.fori_loop(1, nz, wait_gz, 0)
    g_s[...] = jnp.sum(gz_r[...], axis=0)
    pred_s[...] = jnp.sum(pz_r[...], axis=0)
    swap_pred = remote(pred_s, pred_r, pair_s.at[4], pair_r.at[4], at(z, other, c))
    swap_pred.start()

    def g_copy(t, core):
        return remote(g_s, g_all.at[h, c], send_g.at[core, t], recv_g.at[h, c], at(z, core, lax.rem(c + t, nc)))

    def g_arrival(core, p):
        return remote(g_s, g_all.at[core, p], send_g.at[0, 0], recv_g.at[core, p], at(z, other, c))

    def start_g(t, _):
        @pl.when(t > 0)
        def _():
            g_copy(t, h).start()

        g_copy(t, other).start()
        return 0

    lax.fori_loop(0, nc, start_g, 0)
    g_all[h, c] = g_s[...]

    def start_pr(t, _):
        plane_copy(p_code.at[0], pr_all.at[c], 6, t).start()
        return 0

    lax.fori_loop(1, nc, start_pr, 0)
    pr_all[c] = p_code[0]

    def wait_g(t, _):
        p = lax.rem(c + t, nc)

        @pl.when(t > 0)
        def _():
            g_arrival(h, p).wait_recv()

        g_arrival(other, p).wait_recv()
        return 0

    lax.fori_loop(0, nc, wait_g, 0)
    eye = (lax.broadcasted_iota(jnp.int32, (tokens, tokens), 0) == lax.broadcasted_iota(jnp.int32, (tokens, tokens), 1)).astype(jnp.float32)
    g = (g_all[0] + g_all[1]).reshape(tokens, tokens) + eye
    blocks = [g[8 * i : 8 * i + 8] for i in range(tokens // 8)]
    for lo in range(0, 32, 16):
        blocks = eliminated(blocks, lo, 16)

    def col_copy(zz, core):
        return remote(p_z.at[zz], pc_all.at[h, c], send_pc.at[core, zz], recv_pc.at[h, c], at(z, core, zz))

    def pass_pz(t, _):
        zz = lax.rem(z + near_first(t - 1, nz), nz)

        @pl.when(t > 0)
        def _():
            line_arrival(p_z, 9, zz).wait_recv()

        @pl.when(zz == c)
        def _():
            pc_all[h, c] = p_z[zz]

        @pl.when(zz != c)
        def _():
            col_copy(zz, h).start()

        col_copy(zz, other).start()
        return 0

    lax.fori_loop(0, nz, pass_pz, 0)

    for lo in range(32, 96, 16):
        blocks = eliminated(blocks, lo, 16)

    def wait_last(t, _):
        p = lax.rem(c + t, nc)
        plane_arrival(pr_all, 6, p).wait_recv()
        return 0

    lax.fori_loop(1, nc, wait_last, 0)

    def wait_pc(t, _):
        p = lax.rem(c + t, nc)

        @pl.when(t > 0)
        def _():
            remote(p_code.at[0], pc_all.at[h, p], send_pc.at[0, 0], recv_pc.at[h, p], at(z, other, c)).wait_recv()

        remote(p_code.at[0], pc_all.at[other, p], send_pc.at[0, 0], recv_pc.at[other, p], at(z, other, c)).wait_recv()
        return 0

    lax.fori_loop(0, nc, wait_pc, 0)
    swap_pred.wait()

    for k in range(2):
        panel = panel_from(pc_all[k]).reshape(tokens, width)
        hi, mid, _ = split3(panel)
        cut = slice(k * width, k * width + width)
        pc_out[:tokens, cut] = hi
        pc_out[tokens : 2 * tokens, cut] = mid
        pc_out[2 * tokens :, cut] = hi
    pr = panel_from(pr_all[...]).reshape(tokens, width)
    rh, rm, _ = split3(pr.T)
    pr_t = jnp.concatenate([rh, rh, rm], 1)
    for lo in range(96, 128, 16):
        blocks = eliminated(blocks, lo, 16)
    inv = jnp.concatenate(blocks, 0)
    ih, im, _ = split3(inv)
    gain = jnp.dot(pr_t, jnp.concatenate([ih, im, ih], 0), preferred_element_type=jnp.float32)
    hi, mid, _ = split3(gain)
    gain_out[:, :tokens] = hi
    gain_out[:, tokens : 2 * tokens] = hi
    gain_out[:, 2 * tokens :] = mid
    diff = rew_v[...] - (pred_s[...] + pred_r[...])
    coeffs = jnp.dot(jnp.broadcast_to(diff, (8, tokens)), inv, precision=HI, preferred_element_type=jnp.float32)
    shift_out[...] = jnp.dot(coeffs, pr, precision=HI, preferred_element_type=jnp.float32)[:1]

    for block in range(4):
        swap_x(block).wait_send()

    def sent(t, _):
        ctx_copy(t).wait_send()
        remote(phi_s, z_recv.at[z], send.at[1, t], recv.at[1, z], at(lax.rem(z + t, nz), h, c)).wait_send()
        line_copy(phi_s, phi_c.at[h * nz + z], 2, t).wait_send()

        @pl.when(lax.rem(c + t, nc) != z)
        def _():
            pass_row(t).wait_send()

        plane_copy(pp_send.at[lax.rem(c + t, nc)], pp_recv.at[c], 5, t).wait_send()
        plane_copy(p_code.at[0], pr_all.at[c], 6, t).wait_send()
        line_copy(gz_s, gz_r.at[z], 7, t).wait_send()
        line_copy(pz_s, pz_r.at[z], 8, t).wait_send()
        line_copy(p_code.at[0], p_z.at[z], 9, t).wait_send()
        g_copy(t, h).wait_send()
        return 0

    lax.fori_loop(1, nz, sent, 0)

    def sent_some(t, _):
        mate_copy(t).wait_send()
        col_copy(t, other).wait_send()
        g_copy(t, other).wait_send()

        @pl.when(t != c)
        def _():
            col_copy(t, h).wait_send()

        @pl.when(jnp.logical_and(holder, t != z))
        def _():
            remote(phi_r.at[t], phi_r.at[t], send.at[3, t], recv.at[4, t], at(z, h, t)).wait_send()

        return 0

    lax.fori_loop(0, nz, sent_some, 0)


def exchange(context, weight, bias, covariance, mean, rewards):
    rows_here, depth = context.shape
    n, m = covariance.shape
    nz, nc = lax.axis_size("row") // 2, lax.axis_size("col")
    b = rows_here * nc
    f32, bf16 = jnp.float32, jnp.bfloat16
    vmem, sem = pltpu.VMEM, pltpu.SemaphoreType
    scratch = [
        vmem((nc, rows_here, depth), bf16), vmem((b, depth), bf16), vmem((depth, m), bf16), vmem((1, m), f32),
        vmem((n, m), f32), vmem((1, n), f32), vmem((1, b), f32), vmem((m, n), bf16), vmem((m, n), bf16),
        vmem((4, b, 256), f32), vmem((4, b // 2, 256), f32), vmem((4, b // 2, 256), f32),
        vmem((4, 4, 16, 256), bf16), vmem((nz, 16, 256), bf16),
        vmem((16, 256), bf16), vmem((2 * nz, 16, 256), bf16), vmem((16, 16, 256), bf16),
        vmem((nc, 8, n), bf16), vmem((nc, 8, n), bf16), vmem((1, 8, n), bf16),
        vmem((8, b), f32), vmem((nz, 8, b), f32), vmem((1, b), f32), vmem((nz, 1, b), f32), vmem((8, b), f32), vmem((2, nc, 8, b), f32),
        vmem((1, b), f32), vmem((1, b), f32),
        vmem((nc, 8, n), bf16), vmem((nz, 8, n), bf16), vmem((2, nc, 8, n), bf16),
        sem.DMA((6,)), sem.REGULAR, sem.DMA((5,)), sem.DMA((5,)), sem.DMA((10, 16)), sem.DMA((10, 16)), sem.DMA((2, 16)),
        sem.DMA((2, 16)), sem.DMA((2, 16)), sem.DMA((2, 16)), sem.DMA((2, 16)),
    ]
    return pl.pallas_call(
        exchange_kernel,
        in_specs=[pl.BlockSpec(memory_space=pl.ANY)] * 6,
        out_specs=[pl.BlockSpec(memory_space=pltpu.VMEM)] * 3,
        out_shape=[
            jax.ShapeDtypeStruct((n, 3 * b), bf16), jax.ShapeDtypeStruct((3 * b, m), bf16), jax.ShapeDtypeStruct((1, n), f32),
        ],
        scratch_shapes=scratch,
        compiler_params=pltpu.CompilerParams(collective_id=0, has_side_effects=True),
    )(context, weight, bias, covariance, mean, rewards)


def per_device(context, weight, feature_bias, covariance, prior_mean, rewards):
    mean = prior_mean.reshape(1, -1)
    gain, panel, shift = exchange(context, weight, feature_bias.reshape(1, -1), covariance, mean, rewards.reshape(1, -1))
    cov, mean = update(gain, panel, shift, mean, covariance)
    return cov, mean.reshape(-1)


def solution(mesh):
    return jax.shard_map(
        per_device,
        mesh=mesh,
        in_specs=(P("col", "row"), P("row", "col"), P("col"), P("row", "col"), P("row"), P()),
        out_specs=(P("row", "col"), P("row")),
        check_vma=False,
    )
```

```python
import jax
import jax.numpy as jnp
from jax import lax
from jax.experimental import pallas as pl
from jax.experimental.pallas import tpu as pltpu
from jax.sharding import PartitionSpec as P

HI = lax.Precision.HIGHEST
MESH = pl.DeviceIdType.MESH


def split3(x):
    hi = x.astype(jnp.bfloat16)
    rest = x - hi.astype(jnp.float32)
    mid = rest.astype(jnp.bfloat16)
    lo = (rest - mid.astype(jnp.float32)).astype(jnp.bfloat16)
    return hi, mid, lo


def coded_sum(x):
    t = x * 16.0
    t2 = t * t
    t4 = t2 * t2
    return ((t4 * t4) * t2 * t).astype(jnp.bfloat16)


def coded_panel(x):
    t = x * 4.0
    t2 = t * t
    return ((t2 * t2) * t2 * t).astype(jnp.bfloat16)


def rooted(y, power, scale):
    y = y.astype(jnp.float32)
    v = jnp.exp(jnp.log(jnp.abs(y)) * (1.0 / power)) * (1.0 / scale)
    return jnp.where(y < 0, -v, v)


def sum_from(y):
    return rooted(y, 11, 16)


def panel_from(y):
    return rooted(y, 7, 4)


def inverse_of_2(a, b, c):
    scale = 1.0 / (a * c - b * b)
    return c * scale, -b * scale, a * scale


def inverse_of_4(m):
    a0, a1, a2 = inverse_of_2(m[0][0], m[0][1], m[1][1])
    t = [[a0 * m[0][2 + k] + a1 * m[1][2 + k] for k in range(2)], [a1 * m[0][2 + k] + a2 * m[1][2 + k] for k in range(2)]]
    s0 = m[2][2] - (m[0][2] * t[0][0] + m[1][2] * t[1][0])
    s1 = m[2][3] - (m[0][2] * t[0][1] + m[1][2] * t[1][1])
    s2 = m[3][3] - (m[0][3] * t[0][1] + m[1][3] * t[1][1])
    c0, c1, c2 = inverse_of_2(s0, s1, s2)
    u = [[t[i][0] * c0 + t[i][1] * c1, t[i][0] * c1 + t[i][1] * c2] for i in range(2)]
    b0 = a0 + u[0][0] * t[0][0] + u[0][1] * t[0][1]
    b1 = a1 + u[0][0] * t[1][0] + u[0][1] * t[1][1]
    b2 = a2 + u[1][0] * t[1][0] + u[1][1] * t[1][1]
    return [
        [b0, b1, -u[0][0], -u[0][1]],
        [b1, b2, -u[1][0], -u[1][1]],
        [-u[0][0], -u[1][0], c0, c1],
        [-u[0][1], -u[1][1], c1, c2],
    ]


def panel4(blocks, lo, lane, sub):
    n = blocks[0].shape[1]
    for j in range(lo, lo + 8 * len(blocks), 4):
        at, s = (j - lo) // 8, j % 8
        mine = blocks[at]
        cell = [[None] * 4 for _ in range(4)]
        for i in range(4):
            for k in range(i, 4):
                cell[i][k] = cell[k][i] = jnp.broadcast_to(mine[s + i : s + i + 1, j + k : j + k + 1], (8, n))
        inv = inverse_of_4(cell)
        inside = (lane >= j) & (lane < j + 4)
        rows = [
            jnp.where(inside, jnp.where(lane == j + m, 1.0, 0.0), jnp.broadcast_to(mine[s + m : s + m + 1], (8, n)))
            for m in range(4)
        ]
        out = [(inv[i][0] * rows[0] + inv[i][1] * rows[1]) + (inv[i][2] * rows[2] + inv[i][3] * rows[3]) for i in range(4)]
        new = []
        for i, block in enumerate(blocks):
            kept = jnp.where(inside, 0.0, block)
            cols = [jnp.broadcast_to(block[:, j + k : j + k + 1], (8, n)) for k in range(4)]
            if i == at:
                here = (sub >= s) & (sub < s + 4)
                kept = jnp.where(here, 0.0, kept)
                cols = [jnp.where(here, jnp.where(sub == s + k, -1.0, 0.0), cols[k]) for k in range(4)]
            new.append(kept - ((cols[0] * out[0] + cols[1] * out[1]) + (cols[2] * out[2] + cols[3] * out[3])))
        blocks = new
    return blocks


def dot3(a, b):
    ah, am, al = split3(a)
    bh, bm, bl = split3(b)
    return jnp.dot(jnp.concatenate([ah, ah, am, am, ah, al], 1), jnp.concatenate([bh, bm, bh, bm, bl, bh], 0), preferred_element_type=jnp.float32)


def eliminated(blocks, lo, w):
    n = blocks[0].shape[1]
    lane = lax.broadcasted_iota(jnp.int32, (8, n), 1)
    sub = lax.broadcasted_iota(jnp.int32, (8, n), 0)
    first, last = lo // 8, (lo + w) // 8
    panel = panel4(blocks[first:last], lo, lane, sub)
    rest = blocks[:first] + blocks[last:]
    cols = jnp.concatenate([b[:, lo : lo + w] for b in rest], 0)
    prod = dot3(cols, jnp.concatenate(panel, 0))
    inside = (lane >= lo) & (lane < lo + w)
    rest = [jnp.where(inside, 0.0, b) - prod[8 * i : 8 * i + 8] for i, b in enumerate(rest)]
    return rest[:first] + panel + rest[first:]


def update_kernel(gain_ref, pc_ref, shift_ref, mean_ref, cov_ref, out_ref, outm_ref):
    out_ref[...] = cov_ref[...] - jnp.dot(gain_ref[...], pc_ref[...], preferred_element_type=jnp.float32)

    @pl.when(pl.program_id(0) == 0)
    def _():
        outm_ref[...] = mean_ref[...] + shift_ref[...]


def update(gain, panel, shift, mean, cov, steps=2):
    n, m = cov.shape
    width = m // steps
    whole = lambda *shape: pl.BlockSpec(shape, lambda i: (0,) * len(shape))
    cut = lambda rows: pl.BlockSpec((rows, width), lambda i: (0, i))
    return pl.pallas_call(
        update_kernel,
        grid=(steps,),
        in_specs=[whole(*gain.shape), cut(panel.shape[0]), whole(1, n), whole(1, n), cut(n)],
        out_specs=[cut(n), whole(1, n)],
        out_shape=[jax.ShapeDtypeStruct((n, m), jnp.float32), jax.ShapeDtypeStruct((1, n), jnp.float32)],
        compiler_params=pltpu.CompilerParams(vmem_limit_bytes=16 << 20),
    )(gain, panel, shift, mean, cov)


def far_first(t, n):
    return n // 2 + (1 - 2 * lax.rem(t, 2)) * lax.div(t + 1, 2)


def near_first(t, n):
    return far_first(n - 2 - t, n)


def exchange_kernel(
    ctx_hbm, w_hbm, bias_hbm, cov_hbm, mean_hbm, rew_hbm,
    gain_out, pc_out, shift_out,
    ctx_all, ctx_m, w_v, bias_v, cov_v, mean_v, rew_v, c_hi, c_mid,
    x_send, x_recv, z_send, z_code, z_recv, phi_s, phi_c, phi_r,
    pp_send, pp_recv, p_code, gz_s, gz_r, pz_s, pz_r, g_s, g_all, pred_s, pred_r,
    pr_all, p_z, pc_all,
    local, near, pair_s, pair_r, send, recv, mate, send_pc, recv_pc, send_g, recv_g,
):
    nz, nc, nb = z_recv.shape[0], ctx_all.shape[0], 4
    r, c = lax.axis_index("row"), lax.axis_index("col")
    z, h = lax.div(r, 2), lax.rem(r, 2)
    other = 1 - h

    def at(zz, hh, cc):
        return (zz * 2 + hh, cc)

    def remote(src, dst, s_sem, r_sem, where):
        return pltpu.make_async_remote_copy(
            src_ref=src, dst_ref=dst, send_sem=s_sem, recv_sem=r_sem, device_id=where, device_id_type=MESH
        )

    loads = [
        pltpu.make_async_copy(ctx_hbm, ctx_all.at[c], local.at[0]),
        pltpu.make_async_copy(cov_hbm, cov_v, local.at[1]),
        pltpu.make_async_copy(w_hbm, w_v, local.at[2]),
        pltpu.make_async_copy(bias_hbm, bias_v, local.at[3]),
        pltpu.make_async_copy(mean_hbm, mean_v, local.at[4]),
        pltpu.make_async_copy(rew_hbm, rew_v, local.at[5]),
    ]
    for load in loads:
        load.start()

    barrier = pltpu.get_barrier_semaphore()

    def greet(where):
        pl.semaphore_signal(barrier, inc=1, device_id=where, device_id_type=MESH)

    def greet_plane(t, _):
        greet(at(z, h, lax.rem(c + t, nc)))
        return 0

    def greet_line(t, _):
        greet(at(lax.rem(z + t, nz), h, c))
        greet(at(lax.rem(z - t + nz, nz), h, c))
        return 0

    lax.fori_loop(1, nc, greet_plane, 0)
    lax.fori_loop(1, nb + 1, greet_line, 0)
    greet(at(z, other, c))
    pl.semaphore_wait(barrier, nc - 1 + 2 * nb + 1)
    pl.semaphore_signal(near, inc=1, device_id=at(lax.rem(z + nb, nz), h, c), device_id_type=MESH)
    pl.semaphore_signal(near, inc=1, device_id=at(lax.rem(z - nb + nz, nz), h, c), device_id_type=MESH)

    def ctx_copy(t):
        return remote(ctx_hbm, ctx_all.at[c], send.at[0, t], recv.at[0, c], at(z, h, lax.rem(c + t, nc)))

    def plane_arrival(buf, phase, src):
        return remote(buf.at[src], buf.at[src], send.at[phase, 0], recv.at[phase, src], at(z, other, c))

    def start_ctx(t, _):
        ctx_copy(t).start()
        return 0

    lax.fori_loop(1, nc, start_ctx, 0)

    def covariance_terms(first, last):
        for i in range(first, last):
            cut = slice(i * 128, i * 128 + 128)
            hi, mid, _ = split3(cov_v[cut, :].T)
            c_hi[:, cut] = hi
            c_mid[:, cut] = mid

    loads[1].wait()
    covariance_terms(0, 2)
    for load in loads[:1] + loads[2:]:
        load.wait()

    def wait_ctx(t, _):
        plane_arrival(ctx_all, 0, lax.rem(c + t, nc)).wait_recv()
        return 0

    lax.fori_loop(1, nc, wait_ctx, 0)
    tokens, depth = ctx_m.shape
    half = tokens // 2
    ctx_m[...] = ctx_all[...].astype(jnp.float32).reshape(tokens, depth).astype(jnp.bfloat16)

    def line_copy(src, dst, phase, t):
        return remote(src, dst, send.at[phase, t], recv.at[phase, z], at(lax.rem(z + t, nz), h, c))

    def line_arrival(buf, phase, src):
        return remote(buf.at[src], buf.at[src], send.at[phase, 0], recv.at[phase, src], at(z, other, c))

    def swap_x(block):
        theirs = pl.ds(pl.multiple_of(other * half, half), half)
        return remote(x_send.at[block, theirs], x_recv.at[block], pair_s.at[block], pair_r.at[block], at(z, other, c))

    for block in range(4):
        x_send[block] = jnp.dot(ctx_m[...], w_v[:, block * 256 : block * 256 + 256], preferred_element_type=jnp.float32)
        swap_x(block).start()
    own_rows = pl.ds(pl.multiple_of(h * half, half), half)
    for block in range(4):
        swap_x(block).wait_recv()
        both = x_send[block, own_rows, :] + x_recv[block]
        z_send[block] = both
        z_code[block] = coded_sum(both).reshape(4, 16, 256)
    pl.semaphore_wait(near, 2)

    def start_z(t, _):
        t = far_first(t, nz)
        k = lax.rem(z + t, nz)
        line_copy(z_code.at[lax.rem(k, 4), lax.div(k, 4)], z_recv.at[z], 1, t).start()
        return 0

    lax.fori_loop(0, nz - 1, start_z, 0)

    covariance_terms(2, 4)

    def add_z(t, acc):
        zz = lax.rem(z + near_first(t, nz), nz)
        line_arrival(z_recv, 1, zz).wait_recv()
        return acc + sum_from(z_recv[zz])

    kb = lax.rem(z, 4)
    own = z_send[kb, pl.ds(pl.multiple_of(lax.div(z, 4) * 16, 16), 16), :]
    total = lax.fori_loop(0, nz - 1, add_z, own)
    total = total + bias_v[:, pl.ds(pl.multiple_of(kb * 256, 256), 256)]
    phi = jnp.tanh(total).astype(jnp.bfloat16)
    phi_s[...] = phi

    def start_phi(t, _):
        t = far_first(t, nz)
        line_copy(phi_s, phi_c.at[h * nz + z], 2, t).start()
        return 0

    lax.fori_loop(0, nz - 1, start_phi, 0)

    def mate_copy(k):
        return remote(phi_c.at[h * nz + k], phi_c.at[h * nz + k], mate.at[0, k], mate.at[1, k], at(z, other, c))

    def plane_copy(src, dst, phase, t):
        return remote(src, dst, send.at[phase, t], recv.at[phase, c], at(z, h, lax.rem(c + t, nc)))

    holder = c == z

    def push(core, k):
        column = lax.rem(k, 4)
        slot = core * 8 + lax.div(k, 4) * 2 + lax.rem(column, 2)

        @pl.when(jnp.logical_and(holder, lax.div(column, 2) == h))
        def _():
            phi_r[slot] = phi_c[core * nz + k]

            @pl.when(slot != z)
            def _():
                remote(phi_c.at[core * nz + k], phi_r.at[slot], send.at[3, slot], recv.at[4, slot], at(z, h, slot)).start()

    phi_c[h * nz + z] = phi
    mate_copy(z).start()
    push(h, z)

    def pass_mate(t, _):
        zz = lax.rem(z + near_first(t, nz), nz)
        remote(phi_s, phi_c.at[h * nz + zz], send.at[2, 0], recv.at[2, zz], at(z, other, c)).wait_recv()
        mate_copy(zz).start()
        push(h, zz)
        return 0

    lax.fori_loop(0, nz - 1, pass_mate, 0)

    def wait_mate(t, _):
        k = lax.rem(z + near_first(t - 1, nz), nz)
        i = other * nz + k
        remote(phi_c.at[i], phi_c.at[i], mate.at[0, k], mate.at[1, k], at(z, other, c)).wait_recv()
        push(other, k)
        return 0

    lax.fori_loop(0, nz, wait_mate, 0)

    part = None
    for k in range(4):
        lhs = jnp.concatenate([phi_c[i * 4 + k] for i in range(8)], 0)
        for term in (c_hi, c_mid):
            prod = jnp.dot(lhs, term[k * 256 : k * 256 + 256, :], preferred_element_type=jnp.float32)
            part = prod if part is None else part + prod
    pp_send[...] = coded_panel(part).reshape(pp_send.shape)

    def start_pp(t, _):
        plane_copy(pp_send.at[lax.rem(c + t, nc)], pp_recv.at[c], 5, t).start()
        return 0

    lax.fori_loop(1, nc, start_pp, 0)
    pp_recv[c] = pp_send[c]

    def pass_row(t):
        return plane_copy(phi_r.at[c], phi_r.at[c], 4, t)

    @pl.when(jnp.logical_not(holder))
    def _():
        plane_arrival(phi_r, 4, c).wait_recv()

    def start_row(t, _):
        @pl.when(lax.rem(c + t, nc) != z)
        def _():
            pass_row(t).start()

        return 0

    lax.fori_loop(1, nc, start_row, 0)

    def wait_row(t, _):
        @pl.when(jnp.logical_not(holder))
        def _():
            plane_arrival(phi_r, 4, lax.rem(c + t, nc)).wait_recv()

        return 0

    def wait_pp(t, _):
        plane_arrival(pp_recv, 5, lax.rem(c + t, nc)).wait_recv()
        return 0

    lax.fori_loop(1, nc, wait_pp, 0)
    p_mine = jnp.sum(panel_from(pp_recv[...]), axis=0)
    p_code[0] = coded_panel(p_mine)
    lax.fori_loop(1, nc, wait_row, 0)

    width = p_mine.shape[1]
    zeros = jnp.zeros((7, width), jnp.float32)
    terms = split3(jnp.concatenate([p_mine, mean_v[...], zeros], 0))
    stacked = jnp.concatenate(terms, 0)
    gram = None
    for k in range(2):
        rhs = jnp.concatenate([phi_r[i * 2 + k] for i in range(8)], 0)
        prod = lax.dot_general(
            stacked[:, k * 256 : k * 256 + 256], rhs, (((1,), (1,)), ((), ())), preferred_element_type=jnp.float32
        )
        gram = prod if gram is None else gram + prod
    both = gram[:16] + gram[16:32] + gram[32:]
    gz_s[...] = both[:8]
    pz_s[...] = both[8:9]
    p_z[z] = p_code[0]

    def start_gz(t, _):
        t = far_first(t, nz)
        line_copy(gz_s, gz_r.at[z], 7, t).start()
        line_copy(pz_s, pz_r.at[z], 8, t).start()
        return 0

    lax.fori_loop(0, nz - 1, start_gz, 0)
    gz_r[z] = both[:8]
    pz_r[z] = both[8:9]

    def start_pz(t, _):
        t = far_first(t, nz)
        line_copy(p_code.at[0], p_z.at[z], 9, t).start()
        return 0

    lax.fori_loop(0, nz - 1, start_pz, 0)

    def wait_gz(t, _):
        zz = lax.rem(z + t, nz)
        line_arrival(gz_r, 7, zz).wait_recv()
        line_arrival(pz_r, 8, zz).wait_recv()
        return 0

    lax.fori_loop(1, nz, wait_gz, 0)
    g_s[...] = jnp.sum(gz_r[...], axis=0)
    pred_s[...] = jnp.sum(pz_r[...], axis=0)
    swap_pred = remote(pred_s, pred_r, pair_s.at[4], pair_r.at[4], at(z, other, c))
    swap_pred.start()

    def g_copy(t, core):
        return remote(g_s, g_all.at[h, c], send_g.at[core, t], recv_g.at[h, c], at(z, core, lax.rem(c + t, nc)))

    def g_arrival(core, p):
        return remote(g_s, g_all.at[core, p], send_g.at[0, 0], recv_g.at[core, p], at(z, other, c))

    def start_g(t, _):
        @pl.when(t > 0)
        def _():
            g_copy(t, h).start()

        g_copy(t, other).start()
        return 0

    lax.fori_loop(0, nc, start_g, 0)
    g_all[h, c] = g_s[...]

    def start_pr(t, _):
        plane_copy(p_code.at[0], pr_all.at[c], 6, t).start()
        return 0

    lax.fori_loop(1, nc, start_pr, 0)
    pr_all[c] = p_code[0]

    def col_copy(zz, core):
        return remote(p_z.at[zz], pc_all.at[h, c], send_pc.at[core, zz], recv_pc.at[h, c], at(z, core, zz))

    def pass_pz(t, _):
        zz = lax.rem(z + near_first(t - 1, nz), nz)

        @pl.when(t > 0)
        def _():
            line_arrival(p_z, 9, zz).wait_recv()

        @pl.when(zz == c)
        def _():
            pc_all[h, c] = p_z[zz]

        @pl.when(zz != c)
        def _():
            col_copy(zz, h).start()

        col_copy(zz, other).start()
        return 0

    lax.fori_loop(0, nz, pass_pz, 0)

    def wait_g(t, _):
        p = lax.rem(c + t, nc)

        @pl.when(t > 0)
        def _():
            g_arrival(h, p).wait_recv()

        g_arrival(other, p).wait_recv()
        return 0

    lax.fori_loop(0, nc, wait_g, 0)
    eye = (lax.broadcasted_iota(jnp.int32, (tokens, tokens), 0) == lax.broadcasted_iota(jnp.int32, (tokens, tokens), 1)).astype(jnp.float32)
    g = (g_all[0] + g_all[1]).reshape(tokens, tokens) + eye
    blocks = [g[8 * i : 8 * i + 8] for i in range(tokens // 8)]
    for lo in range(0, 32, 16):
        blocks = eliminated(blocks, lo, 16)

    for lo in range(32, 96, 16):
        blocks = eliminated(blocks, lo, 16)

    def wait_last(t, _):
        p = lax.rem(c + t, nc)
        plane_arrival(pr_all, 6, p).wait_recv()
        return 0

    lax.fori_loop(1, nc, wait_last, 0)

    def wait_pc(t, _):
        p = lax.rem(c + t, nc)

        @pl.when(t > 0)
        def _():
            remote(p_code.at[0], pc_all.at[h, p], send_pc.at[0, 0], recv_pc.at[h, p], at(z, other, c)).wait_recv()

        remote(p_code.at[0], pc_all.at[other, p], send_pc.at[0, 0], recv_pc.at[other, p], at(z, other, c)).wait_recv()
        return 0

    lax.fori_loop(0, nc, wait_pc, 0)
    swap_pred.wait()

    for k in range(2):
        panel = panel_from(pc_all[k]).reshape(tokens, width)
        hi, mid, _ = split3(panel)
        cut = slice(k * width, k * width + width)
        pc_out[:tokens, cut] = hi
        pc_out[tokens : 2 * tokens, cut] = mid
        pc_out[2 * tokens :, cut] = hi
    pr = panel_from(pr_all[...]).reshape(tokens, width)
    rh, rm, _ = split3(pr.T)
    pr_t = jnp.concatenate([rh, rh, rm], 1)
    for lo in range(96, 128, 16):
        blocks = eliminated(blocks, lo, 16)
    inv = jnp.concatenate(blocks, 0)
    ih, im, _ = split3(inv)
    gain = jnp.dot(pr_t, jnp.concatenate([ih, im, ih], 0), preferred_element_type=jnp.float32)
    hi, mid, _ = split3(gain)
    gain_out[:, :tokens] = hi
    gain_out[:, tokens : 2 * tokens] = hi
    gain_out[:, 2 * tokens :] = mid
    diff = rew_v[...] - (pred_s[...] + pred_r[...])
    coeffs = jnp.dot(jnp.broadcast_to(diff, (8, tokens)), inv, precision=HI, preferred_element_type=jnp.float32)
    shift_out[...] = jnp.dot(coeffs, pr, precision=HI, preferred_element_type=jnp.float32)[:1]

    for block in range(4):
        swap_x(block).wait_send()

    def sent(t, _):
        ctx_copy(t).wait_send()
        remote(phi_s, z_recv.at[z], send.at[1, t], recv.at[1, z], at(lax.rem(z + t, nz), h, c)).wait_send()
        line_copy(phi_s, phi_c.at[h * nz + z], 2, t).wait_send()

        @pl.when(lax.rem(c + t, nc) != z)
        def _():
            pass_row(t).wait_send()

        plane_copy(pp_send.at[lax.rem(c + t, nc)], pp_recv.at[c], 5, t).wait_send()
        plane_copy(p_code.at[0], pr_all.at[c], 6, t).wait_send()
        line_copy(gz_s, gz_r.at[z], 7, t).wait_send()
        line_copy(pz_s, pz_r.at[z], 8, t).wait_send()
        line_copy(p_code.at[0], p_z.at[z], 9, t).wait_send()
        g_copy(t, h).wait_send()
        return 0

    lax.fori_loop(1, nz, sent, 0)

    def sent_some(t, _):
        mate_copy(t).wait_send()
        col_copy(t, other).wait_send()
        g_copy(t, other).wait_send()

        @pl.when(t != c)
        def _():
            col_copy(t, h).wait_send()

        @pl.when(jnp.logical_and(holder, t != z))
        def _():
            remote(phi_r.at[t], phi_r.at[t], send.at[3, t], recv.at[4, t], at(z, h, t)).wait_send()

        return 0

    lax.fori_loop(0, nz, sent_some, 0)


def exchange(context, weight, bias, covariance, mean, rewards):
    rows_here, depth = context.shape
    n, m = covariance.shape
    nz, nc = lax.axis_size("row") // 2, lax.axis_size("col")
    b = rows_here * nc
    f32, bf16 = jnp.float32, jnp.bfloat16
    vmem, sem = pltpu.VMEM, pltpu.SemaphoreType
    scratch = [
        vmem((nc, rows_here, depth), bf16), vmem((b, depth), bf16), vmem((depth, m), bf16), vmem((1, m), f32),
        vmem((n, m), f32), vmem((1, n), f32), vmem((1, b), f32), vmem((m, n), bf16), vmem((m, n), bf16),
        vmem((4, b, 256), f32), vmem((4, b // 2, 256), f32), vmem((4, b // 2, 256), f32),
        vmem((4, 4, 16, 256), bf16), vmem((nz, 16, 256), bf16),
        vmem((16, 256), bf16), vmem((2 * nz, 16, 256), bf16), vmem((16, 16, 256), bf16),
        vmem((nc, 8, n), bf16), vmem((nc, 8, n), bf16), vmem((1, 8, n), bf16),
        vmem((8, b), f32), vmem((nz, 8, b), f32), vmem((1, b), f32), vmem((nz, 1, b), f32), vmem((8, b), f32), vmem((2, nc, 8, b), f32),
        vmem((1, b), f32), vmem((1, b), f32),
        vmem((nc, 8, n), bf16), vmem((nz, 8, n), bf16), vmem((2, nc, 8, n), bf16),
        sem.DMA((6,)), sem.REGULAR, sem.DMA((5,)), sem.DMA((5,)), sem.DMA((10, 16)), sem.DMA((10, 16)), sem.DMA((2, 16)),
        sem.DMA((2, 16)), sem.DMA((2, 16)), sem.DMA((2, 16)), sem.DMA((2, 16)),
    ]
    return pl.pallas_call(
        exchange_kernel,
        in_specs=[pl.BlockSpec(memory_space=pltpu.HBM)] * 6,
        out_specs=[pl.BlockSpec(memory_space=pltpu.VMEM)] * 3,
        out_shape=[
            jax.ShapeDtypeStruct((n, 3 * b), bf16), jax.ShapeDtypeStruct((3 * b, m), bf16), jax.ShapeDtypeStruct((1, n), f32),
        ],
        scratch_shapes=scratch,
        compiler_params=pltpu.CompilerParams(collective_id=0, has_side_effects=True, vmem_limit_bytes=28 << 20),
    )(*(pltpu.with_memory_space_constraint(x, pltpu.HBM) for x in (context, weight, bias, covariance, mean, rewards)))


def per_device(context, weight, feature_bias, covariance, prior_mean, rewards):
    mean = prior_mean.reshape(1, -1)
    gain, panel, shift = exchange(context, weight, feature_bias.reshape(1, -1), covariance, mean, rewards.reshape(1, -1))
    cov, mean = update(gain, panel, shift, mean, pltpu.with_memory_space_constraint(covariance, pltpu.HBM))
    return cov, mean.reshape(-1)


def solution(mesh):
    return jax.shard_map(
        per_device,
        mesh=mesh,
        in_specs=(P("col", "row"), P("row", "col"), P("col"), P("row", "col"), P("row"), P()),
        out_specs=(P("row", "col"), P("row")),
        check_vma=False,
    )
```

```python
import jax
import jax.numpy as jnp
from jax import lax
from jax.experimental import pallas as pl
from jax.experimental.pallas import tpu as pltpu
from jax.sharding import PartitionSpec as P

HI = lax.Precision.HIGHEST
MESH = pl.DeviceIdType.MESH


def split3(x):
    hi = x.astype(jnp.bfloat16)
    rest = x - hi.astype(jnp.float32)
    mid = rest.astype(jnp.bfloat16)
    lo = (rest - mid.astype(jnp.float32)).astype(jnp.bfloat16)
    return hi, mid, lo


def coded_sum(x):
    t = x * 16.0
    t2 = t * t
    t4 = t2 * t2
    return ((t4 * t4) * t2 * t).astype(jnp.bfloat16)


def coded_panel(x):
    t = x * 4.0
    t2 = t * t
    return ((t2 * t2) * t2 * t).astype(jnp.bfloat16)


def rooted(y, power, scale):
    y = y.astype(jnp.float32)
    v = jnp.exp(jnp.log(jnp.abs(y)) * (1.0 / power)) * (1.0 / scale)
    return jnp.where(y < 0, -v, v)


def sum_from(y):
    return rooted(y, 11, 16)


def panel_from(y):
    return rooted(y, 7, 4)


def inverse_of_2(a, b, c):
    scale = 1.0 / (a * c - b * b)
    return c * scale, -b * scale, a * scale


def inverse_of_4(m):
    a0, a1, a2 = inverse_of_2(m[0][0], m[0][1], m[1][1])
    t = [[a0 * m[0][2 + k] + a1 * m[1][2 + k] for k in range(2)], [a1 * m[0][2 + k] + a2 * m[1][2 + k] for k in range(2)]]
    s0 = m[2][2] - (m[0][2] * t[0][0] + m[1][2] * t[1][0])
    s1 = m[2][3] - (m[0][2] * t[0][1] + m[1][2] * t[1][1])
    s2 = m[3][3] - (m[0][3] * t[0][1] + m[1][3] * t[1][1])
    c0, c1, c2 = inverse_of_2(s0, s1, s2)
    u = [[t[i][0] * c0 + t[i][1] * c1, t[i][0] * c1 + t[i][1] * c2] for i in range(2)]
    b0 = a0 + u[0][0] * t[0][0] + u[0][1] * t[0][1]
    b1 = a1 + u[0][0] * t[1][0] + u[0][1] * t[1][1]
    b2 = a2 + u[1][0] * t[1][0] + u[1][1] * t[1][1]
    return [
        [b0, b1, -u[0][0], -u[0][1]],
        [b1, b2, -u[1][0], -u[1][1]],
        [-u[0][0], -u[1][0], c0, c1],
        [-u[0][1], -u[1][1], c1, c2],
    ]


def panel4(blocks, lo, lane, sub):
    n = blocks[0].shape[1]
    for j in range(lo, lo + 8 * len(blocks), 4):
        at, s = (j - lo) // 8, j % 8
        mine = blocks[at]
        cell = [[None] * 4 for _ in range(4)]
        for i in range(4):
            for k in range(i, 4):
                cell[i][k] = cell[k][i] = jnp.broadcast_to(mine[s + i : s + i + 1, j + k : j + k + 1], (8, n))
        inv = inverse_of_4(cell)
        inside = (lane >= j) & (lane < j + 4)
        rows = [
            jnp.where(inside, jnp.where(lane == j + m, 1.0, 0.0), jnp.broadcast_to(mine[s + m : s + m + 1], (8, n)))
            for m in range(4)
        ]
        out = [(inv[i][0] * rows[0] + inv[i][1] * rows[1]) + (inv[i][2] * rows[2] + inv[i][3] * rows[3]) for i in range(4)]
        new = []
        for i, block in enumerate(blocks):
            kept = jnp.where(inside, 0.0, block)
            cols = [jnp.broadcast_to(block[:, j + k : j + k + 1], (8, n)) for k in range(4)]
            if i == at:
                here = (sub >= s) & (sub < s + 4)
                kept = jnp.where(here, 0.0, kept)
                cols = [jnp.where(here, jnp.where(sub == s + k, -1.0, 0.0), cols[k]) for k in range(4)]
            new.append(kept - ((cols[0] * out[0] + cols[1] * out[1]) + (cols[2] * out[2] + cols[3] * out[3])))
        blocks = new
    return blocks


def dot3(a, b):
    ah, am, al = split3(a)
    bh, bm, bl = split3(b)
    return jnp.dot(jnp.concatenate([ah, ah, am, am, ah, al], 1), jnp.concatenate([bh, bm, bh, bm, bl, bh], 0), preferred_element_type=jnp.float32)


def eliminated(blocks, lo, w):
    n = blocks[0].shape[1]
    lane = lax.broadcasted_iota(jnp.int32, (8, n), 1)
    sub = lax.broadcasted_iota(jnp.int32, (8, n), 0)
    first, last = lo // 8, (lo + w) // 8
    panel = panel4(blocks[first:last], lo, lane, sub)
    rest = blocks[:first] + blocks[last:]
    cols = jnp.concatenate([b[:, lo : lo + w] for b in rest], 0)
    prod = dot3(cols, jnp.concatenate(panel, 0))
    inside = (lane >= lo) & (lane < lo + w)
    rest = [jnp.where(inside, 0.0, b) - prod[8 * i : 8 * i + 8] for i, b in enumerate(rest)]
    return rest[:first] + panel + rest[first:]


def update_kernel(gain_ref, pc_ref, shift_ref, mean_ref, cov_ref, out_ref, outm_ref):
    out_ref[...] = cov_ref[...] - jnp.dot(gain_ref[...], pc_ref[...], preferred_element_type=jnp.float32)

    @pl.when(pl.program_id(0) == 0)
    def _():
        outm_ref[...] = mean_ref[...] + shift_ref[...]


def update(gain, panel, shift, mean, cov, steps=2):
    n, m = cov.shape
    width = m // steps
    whole = lambda *shape: pl.BlockSpec(shape, lambda i: (0,) * len(shape))
    cut = lambda rows: pl.BlockSpec((rows, width), lambda i: (0, i))
    return pl.pallas_call(
        update_kernel,
        grid=(steps,),
        in_specs=[whole(*gain.shape), cut(panel.shape[0]), whole(1, n), whole(1, n), cut(n)],
        out_specs=[cut(n), whole(1, n)],
        out_shape=[jax.ShapeDtypeStruct((n, m), jnp.float32), jax.ShapeDtypeStruct((1, n), jnp.float32)],
        compiler_params=pltpu.CompilerParams(vmem_limit_bytes=16 << 20),
    )(gain, panel, shift, mean, cov)


def far_first(t, n):
    return n // 2 + (1 - 2 * lax.rem(t, 2)) * lax.div(t + 1, 2)


def near_first(t, n):
    return far_first(n - 2 - t, n)


def exchange_kernel(
    ctx_hbm, w_hbm, bias_hbm, cov_hbm, mean_hbm, rew_hbm,
    gain_out, pc_out, shift_out,
    ctx_all, ctx_m, w_v, bias_v, cov_v, mean_v, rew_v, c_hi, c_mid,
    x_send, x_recv, z_send, z_code, z_recv, phi_s, phi_c, phi_r,
    pp_send, pp_recv, p_code, gz_s, gz_r, pz_s, pz_r, g_s, g_all, pred_s, pred_r,
    pr_all, p_z, pc_all,
    local, near, pair_s, pair_r, send, recv, mate, send_pc, recv_pc, send_g, recv_g,
):
    nz, nc, nb = z_recv.shape[0], ctx_all.shape[0], 4
    r, c = lax.axis_index("row"), lax.axis_index("col")
    z, h = lax.div(r, 2), lax.rem(r, 2)
    other = 1 - h

    def at(zz, hh, cc):
        return (zz * 2 + hh, cc)

    def remote(src, dst, s_sem, r_sem, where):
        return pltpu.make_async_remote_copy(
            src_ref=src, dst_ref=dst, send_sem=s_sem, recv_sem=r_sem, device_id=where, device_id_type=MESH
        )

    loads = [
        pltpu.make_async_copy(ctx_hbm, ctx_all.at[c], local.at[0]),
        pltpu.make_async_copy(cov_hbm, cov_v, local.at[1]),
        pltpu.make_async_copy(w_hbm, w_v, local.at[2]),
        pltpu.make_async_copy(bias_hbm, bias_v, local.at[3]),
        pltpu.make_async_copy(mean_hbm, mean_v, local.at[4]),
        pltpu.make_async_copy(rew_hbm, rew_v, local.at[5]),
    ]
    for load in loads:
        load.start()

    barrier = pltpu.get_barrier_semaphore()

    def greet(where):
        pl.semaphore_signal(barrier, inc=1, device_id=where, device_id_type=MESH)

    def greet_plane(t, _):
        greet(at(z, h, lax.rem(c + t, nc)))
        return 0

    def greet_line(t, _):
        greet(at(lax.rem(z + t, nz), h, c))
        greet(at(lax.rem(z - t + nz, nz), h, c))
        return 0

    lax.fori_loop(1, nc, greet_plane, 0)
    lax.fori_loop(1, nb + 1, greet_line, 0)
    greet(at(z, other, c))
    pl.semaphore_wait(barrier, nc - 1 + 2 * nb + 1)
    pl.semaphore_signal(near, inc=1, device_id=at(lax.rem(z + nb, nz), h, c), device_id_type=MESH)
    pl.semaphore_signal(near, inc=1, device_id=at(lax.rem(z - nb + nz, nz), h, c), device_id_type=MESH)

    def ctx_copy(t):
        return remote(ctx_hbm, ctx_all.at[c], send.at[0, t], recv.at[0, c], at(z, h, lax.rem(c + t, nc)))

    def plane_arrival(buf, phase, src):
        return remote(buf.at[src], buf.at[src], send.at[phase, 0], recv.at[phase, src], at(z, other, c))

    def start_ctx(t, _):
        ctx_copy(t).start()
        return 0

    lax.fori_loop(1, nc, start_ctx, 0)

    def covariance_terms(first, last):
        for i in range(first, last):
            cut = slice(i * 128, i * 128 + 128)
            hi, mid, _ = split3(cov_v[cut, :].T)
            c_hi[:, cut] = hi
            c_mid[:, cut] = mid

    for load in loads[:1] + loads[2:]:
        load.wait()

    def wait_ctx(t, _):
        plane_arrival(ctx_all, 0, lax.rem(c + t, nc)).wait_recv()
        return 0

    lax.fori_loop(1, nc, wait_ctx, 0)
    tokens, depth = ctx_m.shape
    half = tokens // 2
    ctx_m[...] = ctx_all[...].astype(jnp.float32).reshape(tokens, depth).astype(jnp.bfloat16)

    def line_copy(src, dst, phase, t):
        return remote(src, dst, send.at[phase, t], recv.at[phase, z], at(lax.rem(z + t, nz), h, c))

    def line_arrival(buf, phase, src):
        return remote(buf.at[src], buf.at[src], send.at[phase, 0], recv.at[phase, src], at(z, other, c))

    def swap_x(block):
        theirs = pl.ds(pl.multiple_of(other * half, half), half)
        return remote(x_send.at[block, theirs], x_recv.at[block], pair_s.at[block], pair_r.at[block], at(z, other, c))

    for block in range(4):
        x_send[block] = jnp.dot(ctx_m[...], w_v[:, block * 256 : block * 256 + 256], preferred_element_type=jnp.float32)
        swap_x(block).start()
    own_rows = pl.ds(pl.multiple_of(h * half, half), half)
    for block in range(4):
        swap_x(block).wait_recv()
        both = x_send[block, own_rows, :] + x_recv[block]
        z_send[block] = both
        z_code[block] = coded_sum(both).reshape(4, 16, 256)
    pl.semaphore_wait(near, 2)

    def start_z(t, _):
        t = far_first(t, nz)
        k = lax.rem(z + t, nz)
        line_copy(z_code.at[lax.rem(k, 4), lax.div(k, 4)], z_recv.at[z], 1, t).start()
        return 0

    lax.fori_loop(0, nz - 1, start_z, 0)

    loads[1].wait()
    covariance_terms(0, 4)

    def add_z(t, acc):
        zz = lax.rem(z + near_first(t, nz), nz)
        line_arrival(z_recv, 1, zz).wait_recv()
        return acc + sum_from(z_recv[zz])

    kb = lax.rem(z, 4)
    own = z_send[kb, pl.ds(pl.multiple_of(lax.div(z, 4) * 16, 16), 16), :]
    total = lax.fori_loop(0, nz - 1, add_z, own)
    total = total + bias_v[:, pl.ds(pl.multiple_of(kb * 256, 256), 256)]
    phi = jnp.tanh(total).astype(jnp.bfloat16)
    phi_s[...] = phi

    def start_phi(t, _):
        t = far_first(t, nz)
        line_copy(phi_s, phi_c.at[h * nz + z], 2, t).start()
        return 0

    lax.fori_loop(0, nz - 1, start_phi, 0)

    def mate_copy(k):
        return remote(phi_c.at[h * nz + k], phi_c.at[h * nz + k], mate.at[0, k], mate.at[1, k], at(z, other, c))

    def plane_copy(src, dst, phase, t):
        return remote(src, dst, send.at[phase, t], recv.at[phase, c], at(z, h, lax.rem(c + t, nc)))

    holder = c == z

    def push(core, k):
        column = lax.rem(k, 4)
        slot = core * 8 + lax.div(k, 4) * 2 + lax.rem(column, 2)

        @pl.when(jnp.logical_and(holder, lax.div(column, 2) == h))
        def _():
            phi_r[slot] = phi_c[core * nz + k]

            @pl.when(slot != z)
            def _():
                remote(phi_c.at[core * nz + k], phi_r.at[slot], send.at[3, slot], recv.at[4, slot], at(z, h, slot)).start()

    phi_c[h * nz + z] = phi
    mate_copy(z).start()
    push(h, z)

    def pass_mate(t, _):
        zz = lax.rem(z + near_first(t, nz), nz)
        remote(phi_s, phi_c.at[h * nz + zz], send.at[2, 0], recv.at[2, zz], at(z, other, c)).wait_recv()
        mate_copy(zz).start()
        push(h, zz)
        return 0

    lax.fori_loop(0, nz - 1, pass_mate, 0)

    def wait_mate(t, _):
        k = lax.rem(z + near_first(t - 1, nz), nz)
        i = other * nz + k
        remote(phi_c.at[i], phi_c.at[i], mate.at[0, k], mate.at[1, k], at(z, other, c)).wait_recv()
        push(other, k)
        return 0

    lax.fori_loop(0, nz, wait_mate, 0)

    part = None
    for k in range(4):
        lhs = jnp.concatenate([phi_c[i * 4 + k] for i in range(8)], 0)
        for term in (c_hi, c_mid):
            prod = jnp.dot(lhs, term[k * 256 : k * 256 + 256, :], preferred_element_type=jnp.float32)
            part = prod if part is None else part + prod
    pp_send[...] = coded_panel(part).reshape(pp_send.shape)

    def start_pp(t, _):
        plane_copy(pp_send.at[lax.rem(c + t, nc)], pp_recv.at[c], 5, t).start()
        return 0

    lax.fori_loop(1, nc, start_pp, 0)
    pp_recv[c] = pp_send[c]

    def pass_row(t):
        return plane_copy(phi_r.at[c], phi_r.at[c], 4, t)

    @pl.when(jnp.logical_not(holder))
    def _():
        plane_arrival(phi_r, 4, c).wait_recv()

    def start_row(t, _):
        @pl.when(lax.rem(c + t, nc) != z)
        def _():
            pass_row(t).start()

        return 0

    lax.fori_loop(1, nc, start_row, 0)

    def wait_row(t, _):
        @pl.when(jnp.logical_not(holder))
        def _():
            plane_arrival(phi_r, 4, lax.rem(c + t, nc)).wait_recv()

        return 0

    def wait_pp(t, _):
        plane_arrival(pp_recv, 5, lax.rem(c + t, nc)).wait_recv()
        return 0

    lax.fori_loop(1, nc, wait_pp, 0)
    p_mine = jnp.sum(panel_from(pp_recv[...]), axis=0)
    p_code[0] = coded_panel(p_mine)
    lax.fori_loop(1, nc, wait_row, 0)

    width = p_mine.shape[1]
    zeros = jnp.zeros((7, width), jnp.float32)
    terms = split3(jnp.concatenate([p_mine, mean_v[...], zeros], 0))
    stacked = jnp.concatenate(terms, 0)
    gram = None
    for k in range(2):
        rhs = jnp.concatenate([phi_r[i * 2 + k] for i in range(8)], 0)
        prod = lax.dot_general(
            stacked[:, k * 256 : k * 256 + 256], rhs, (((1,), (1,)), ((), ())), preferred_element_type=jnp.float32
        )
        gram = prod if gram is None else gram + prod
    both = gram[:16] + gram[16:32] + gram[32:]
    gz_s[...] = both[:8]
    pz_s[...] = both[8:9]
    p_z[z] = p_code[0]

    def start_gz(t, _):
        t = far_first(t, nz)
        line_copy(gz_s, gz_r.at[z], 7, t).start()
        line_copy(pz_s, pz_r.at[z], 8, t).start()
        return 0

    lax.fori_loop(0, nz - 1, start_gz, 0)
    gz_r[z] = both[:8]
    pz_r[z] = both[8:9]

    def start_pz(t, _):
        t = far_first(t, nz)
        line_copy(p_code.at[0], p_z.at[z], 9, t).start()
        return 0

    lax.fori_loop(0, nz - 1, start_pz, 0)

    def start_pr(t, _):
        plane_copy(p_code.at[0], pr_all.at[c], 6, t).start()
        return 0

    lax.fori_loop(1, nc, start_pr, 0)
    pr_all[c] = p_code[0]

    def wait_gz(t, _):
        zz = lax.rem(z + t, nz)
        line_arrival(gz_r, 7, zz).wait_recv()
        line_arrival(pz_r, 8, zz).wait_recv()
        return 0

    lax.fori_loop(1, nz, wait_gz, 0)
    g_s[...] = jnp.sum(gz_r[...], axis=0)
    pred_s[...] = jnp.sum(pz_r[...], axis=0)
    swap_pred = remote(pred_s, pred_r, pair_s.at[4], pair_r.at[4], at(z, other, c))
    swap_pred.start()

    def g_copy(t, core):
        return remote(g_s, g_all.at[h, c], send_g.at[core, t], recv_g.at[h, c], at(z, core, lax.rem(c + t, nc)))

    def g_arrival(core, p):
        return remote(g_s, g_all.at[core, p], send_g.at[0, 0], recv_g.at[core, p], at(z, other, c))

    def start_g(t, _):
        @pl.when(t > 0)
        def _():
            g_copy(t, h).start()

        g_copy(t, other).start()
        return 0

    lax.fori_loop(0, nc, start_g, 0)
    g_all[h, c] = g_s[...]

    def col_copy(zz, core):
        return remote(p_z.at[zz], pc_all.at[h, c], send_pc.at[core, zz], recv_pc.at[h, c], at(z, core, zz))

    def pass_pz(t, _):
        zz = lax.rem(z + near_first(t - 1, nz), nz)

        @pl.when(t > 0)
        def _():
            line_arrival(p_z, 9, zz).wait_recv()

        @pl.when(zz == c)
        def _():
            pc_all[h, c] = p_z[zz]

        @pl.when(zz != c)
        def _():
            col_copy(zz, h).start()

        col_copy(zz, other).start()
        return 0

    lax.fori_loop(0, nz, pass_pz, 0)

    def wait_g(t, _):
        p = lax.rem(c + t, nc)

        @pl.when(t > 0)
        def _():
            g_arrival(h, p).wait_recv()

        g_arrival(other, p).wait_recv()
        return 0

    lax.fori_loop(0, nc, wait_g, 0)
    eye = (lax.broadcasted_iota(jnp.int32, (tokens, tokens), 0) == lax.broadcasted_iota(jnp.int32, (tokens, tokens), 1)).astype(jnp.float32)
    g = (g_all[0] + g_all[1]).reshape(tokens, tokens) + eye
    blocks = [g[8 * i : 8 * i + 8] for i in range(tokens // 8)]
    for lo in range(0, 32, 16):
        blocks = eliminated(blocks, lo, 16)

    for lo in range(32, 96, 16):
        blocks = eliminated(blocks, lo, 16)

    def wait_last(t, _):
        p = lax.rem(c + t, nc)
        plane_arrival(pr_all, 6, p).wait_recv()
        return 0

    lax.fori_loop(1, nc, wait_last, 0)

    def wait_pc(t, _):
        p = lax.rem(c + t, nc)

        @pl.when(t > 0)
        def _():
            remote(p_code.at[0], pc_all.at[h, p], send_pc.at[0, 0], recv_pc.at[h, p], at(z, other, c)).wait_recv()

        remote(p_code.at[0], pc_all.at[other, p], send_pc.at[0, 0], recv_pc.at[other, p], at(z, other, c)).wait_recv()
        return 0

    lax.fori_loop(0, nc, wait_pc, 0)
    swap_pred.wait()

    for k in range(2):
        panel = panel_from(pc_all[k]).reshape(tokens, width)
        hi, mid, _ = split3(panel)
        cut = slice(k * width, k * width + width)
        pc_out[:tokens, cut] = hi
        pc_out[tokens : 2 * tokens, cut] = mid
        pc_out[2 * tokens :, cut] = hi
    pr = panel_from(pr_all[...]).reshape(tokens, width)
    rh, rm, _ = split3(pr.T)
    pr_t = jnp.concatenate([rh, rh, rm], 1)
    for lo in range(96, 128, 16):
        blocks = eliminated(blocks, lo, 16)
    inv = jnp.concatenate(blocks, 0)
    ih, im, _ = split3(inv)
    gain = jnp.dot(pr_t, jnp.concatenate([ih, im, ih], 0), preferred_element_type=jnp.float32)
    hi, mid, _ = split3(gain)
    gain_out[:, :tokens] = hi
    gain_out[:, tokens : 2 * tokens] = hi
    gain_out[:, 2 * tokens :] = mid
    diff = rew_v[...] - (pred_s[...] + pred_r[...])
    coeffs = jnp.dot(jnp.broadcast_to(diff, (8, tokens)), inv, precision=HI, preferred_element_type=jnp.float32)
    shift_out[...] = jnp.dot(coeffs, pr, precision=HI, preferred_element_type=jnp.float32)[:1]

    for block in range(4):
        swap_x(block).wait_send()

    def sent(t, _):
        ctx_copy(t).wait_send()
        remote(phi_s, z_recv.at[z], send.at[1, t], recv.at[1, z], at(lax.rem(z + t, nz), h, c)).wait_send()
        line_copy(phi_s, phi_c.at[h * nz + z], 2, t).wait_send()

        @pl.when(lax.rem(c + t, nc) != z)
        def _():
            pass_row(t).wait_send()

        plane_copy(pp_send.at[lax.rem(c + t, nc)], pp_recv.at[c], 5, t).wait_send()
        plane_copy(p_code.at[0], pr_all.at[c], 6, t).wait_send()
        line_copy(gz_s, gz_r.at[z], 7, t).wait_send()
        line_copy(pz_s, pz_r.at[z], 8, t).wait_send()
        line_copy(p_code.at[0], p_z.at[z], 9, t).wait_send()
        g_copy(t, h).wait_send()
        return 0

    lax.fori_loop(1, nz, sent, 0)

    def sent_some(t, _):
        mate_copy(t).wait_send()
        col_copy(t, other).wait_send()
        g_copy(t, other).wait_send()

        @pl.when(t != c)
        def _():
            col_copy(t, h).wait_send()

        @pl.when(jnp.logical_and(holder, t != z))
        def _():
            remote(phi_r.at[t], phi_r.at[t], send.at[3, t], recv.at[4, t], at(z, h, t)).wait_send()

        return 0

    lax.fori_loop(0, nz, sent_some, 0)


def exchange(context, weight, bias, covariance, mean, rewards):
    rows_here, depth = context.shape
    n, m = covariance.shape
    nz, nc = lax.axis_size("row") // 2, lax.axis_size("col")
    b = rows_here * nc
    f32, bf16 = jnp.float32, jnp.bfloat16
    vmem, sem = pltpu.VMEM, pltpu.SemaphoreType
    scratch = [
        vmem((nc, rows_here, depth), bf16), vmem((b, depth), bf16), vmem((depth, m), bf16), vmem((1, m), f32),
        vmem((n, m), f32), vmem((1, n), f32), vmem((1, b), f32), vmem((m, n), bf16), vmem((m, n), bf16),
        vmem((4, b, 256), f32), vmem((4, b // 2, 256), f32), vmem((4, b // 2, 256), f32),
        vmem((4, 4, 16, 256), bf16), vmem((nz, 16, 256), bf16),
        vmem((16, 256), bf16), vmem((2 * nz, 16, 256), bf16), vmem((16, 16, 256), bf16),
        vmem((nc, 8, n), bf16), vmem((nc, 8, n), bf16), vmem((1, 8, n), bf16),
        vmem((8, b), f32), vmem((nz, 8, b), f32), vmem((1, b), f32), vmem((nz, 1, b), f32), vmem((8, b), f32), vmem((2, nc, 8, b), f32),
        vmem((1, b), f32), vmem((1, b), f32),
        vmem((nc, 8, n), bf16), vmem((nz, 8, n), bf16), vmem((2, nc, 8, n), bf16),
        sem.DMA((6,)), sem.REGULAR, sem.DMA((5,)), sem.DMA((5,)), sem.DMA((10, 16)), sem.DMA((10, 16)), sem.DMA((2, 16)),
        sem.DMA((2, 16)), sem.DMA((2, 16)), sem.DMA((2, 16)), sem.DMA((2, 16)),
    ]
    return pl.pallas_call(
        exchange_kernel,
        in_specs=[pl.BlockSpec(memory_space=pltpu.HBM)] * 6,
        out_specs=[pl.BlockSpec(memory_space=pltpu.VMEM)] * 3,
        out_shape=[
            jax.ShapeDtypeStruct((n, 3 * b), bf16), jax.ShapeDtypeStruct((3 * b, m), bf16), jax.ShapeDtypeStruct((1, n), f32),
        ],
        scratch_shapes=scratch,
        compiler_params=pltpu.CompilerParams(collective_id=0, has_side_effects=True, vmem_limit_bytes=28 << 20),
    )(*(pltpu.with_memory_space_constraint(x, pltpu.HBM) for x in (context, weight, bias, covariance, mean, rewards)))


def per_device(context, weight, feature_bias, covariance, prior_mean, rewards):
    mean = prior_mean.reshape(1, -1)
    gain, panel, shift = exchange(context, weight, feature_bias.reshape(1, -1), covariance, mean, rewards.reshape(1, -1))
    cov, mean = update(gain, panel, shift, mean, pltpu.with_memory_space_constraint(covariance, pltpu.HBM))
    return cov, mean.reshape(-1)


def solution(mesh):
    return jax.shard_map(
        per_device,
        mesh=mesh,
        in_specs=(P("col", "row"), P("row", "col"), P("col"), P("row", "col"), P("row"), P()),
        out_specs=(P("row", "col"), P("row")),
        check_vma=False,
    )
```

```python
import jax
import jax.numpy as jnp
from jax import lax
from jax.experimental import pallas as pl
from jax.experimental.pallas import tpu as pltpu
from jax.sharding import PartitionSpec as P

HI = lax.Precision.HIGHEST
MESH = pl.DeviceIdType.MESH


def split3(x):
    hi = x.astype(jnp.bfloat16)
    rest = x - hi.astype(jnp.float32)
    mid = rest.astype(jnp.bfloat16)
    lo = (rest - mid.astype(jnp.float32)).astype(jnp.bfloat16)
    return hi, mid, lo


def coded_sum(x):
    t = x * 16.0
    t2 = t * t
    t4 = t2 * t2
    return ((t4 * t4) * t2 * t).astype(jnp.bfloat16)


def coded_panel(x):
    t = x * 4.0
    t2 = t * t
    return ((t2 * t2) * t2 * t).astype(jnp.bfloat16)


def rooted(y, power, scale):
    y = y.astype(jnp.float32)
    v = jnp.exp(jnp.log(jnp.abs(y)) * (1.0 / power)) * (1.0 / scale)
    return jnp.where(y < 0, -v, v)


def sum_from(y):
    return rooted(y, 11, 16)


def panel_from(y):
    return rooted(y, 7, 4)


def inverse_of_2(a, b, c):
    scale = 1.0 / (a * c - b * b)
    return c * scale, -b * scale, a * scale


def inverse_of_4(m):
    a0, a1, a2 = inverse_of_2(m[0][0], m[0][1], m[1][1])
    t = [[a0 * m[0][2 + k] + a1 * m[1][2 + k] for k in range(2)], [a1 * m[0][2 + k] + a2 * m[1][2 + k] for k in range(2)]]
    s0 = m[2][2] - (m[0][2] * t[0][0] + m[1][2] * t[1][0])
    s1 = m[2][3] - (m[0][2] * t[0][1] + m[1][2] * t[1][1])
    s2 = m[3][3] - (m[0][3] * t[0][1] + m[1][3] * t[1][1])
    c0, c1, c2 = inverse_of_2(s0, s1, s2)
    u = [[t[i][0] * c0 + t[i][1] * c1, t[i][0] * c1 + t[i][1] * c2] for i in range(2)]
    b0 = a0 + u[0][0] * t[0][0] + u[0][1] * t[0][1]
    b1 = a1 + u[0][0] * t[1][0] + u[0][1] * t[1][1]
    b2 = a2 + u[1][0] * t[1][0] + u[1][1] * t[1][1]
    return [
        [b0, b1, -u[0][0], -u[0][1]],
        [b1, b2, -u[1][0], -u[1][1]],
        [-u[0][0], -u[1][0], c0, c1],
        [-u[0][1], -u[1][1], c1, c2],
    ]


def panel4(blocks, lo, lane, sub):
    n = blocks[0].shape[1]
    for j in range(lo, lo + 8 * len(blocks), 4):
        at, s = (j - lo) // 8, j % 8
        mine = blocks[at]
        cell = [[None] * 4 for _ in range(4)]
        for i in range(4):
            for k in range(i, 4):
                cell[i][k] = cell[k][i] = jnp.broadcast_to(mine[s + i : s + i + 1, j + k : j + k + 1], (8, n))
        inv = inverse_of_4(cell)
        inside = (lane >= j) & (lane < j + 4)
        rows = [
            jnp.where(inside, jnp.where(lane == j + m, 1.0, 0.0), jnp.broadcast_to(mine[s + m : s + m + 1], (8, n)))
            for m in range(4)
        ]
        out = [(inv[i][0] * rows[0] + inv[i][1] * rows[1]) + (inv[i][2] * rows[2] + inv[i][3] * rows[3]) for i in range(4)]
        new = []
        for i, block in enumerate(blocks):
            kept = jnp.where(inside, 0.0, block)
            cols = [jnp.broadcast_to(block[:, j + k : j + k + 1], (8, n)) for k in range(4)]
            if i == at:
                here = (sub >= s) & (sub < s + 4)
                kept = jnp.where(here, 0.0, kept)
                cols = [jnp.where(here, jnp.where(sub == s + k, -1.0, 0.0), cols[k]) for k in range(4)]
            new.append(kept - ((cols[0] * out[0] + cols[1] * out[1]) + (cols[2] * out[2] + cols[3] * out[3])))
        blocks = new
    return blocks


def dot3(a, b):
    ah, am, al = split3(a)
    bh, bm, bl = split3(b)
    return jnp.dot(jnp.concatenate([ah, ah, am, am, ah, al], 1), jnp.concatenate([bh, bm, bh, bm, bl, bh], 0), preferred_element_type=jnp.float32)


def eliminated(blocks, lo, w):
    n = blocks[0].shape[1]
    lane = lax.broadcasted_iota(jnp.int32, (8, n), 1)
    sub = lax.broadcasted_iota(jnp.int32, (8, n), 0)
    first, last = lo // 8, (lo + w) // 8
    panel = panel4(blocks[first:last], lo, lane, sub)
    rest = blocks[:first] + blocks[last:]
    cols = jnp.concatenate([b[:, lo : lo + w] for b in rest], 0)
    prod = dot3(cols, jnp.concatenate(panel, 0))
    inside = (lane >= lo) & (lane < lo + w)
    rest = [jnp.where(inside, 0.0, b) - prod[8 * i : 8 * i + 8] for i, b in enumerate(rest)]
    return rest[:first] + panel + rest[first:]


def update_kernel(gain_ref, pc_ref, shift_ref, mean_ref, cov_ref, out_ref, outm_ref):
    out_ref[...] = cov_ref[...] - jnp.dot(gain_ref[...], pc_ref[...], preferred_element_type=jnp.float32)

    @pl.when(pl.program_id(0) == 0)
    def _():
        outm_ref[...] = mean_ref[...] + shift_ref[...]


def update(gain, panel, shift, mean, cov, steps=2):
    n, m = cov.shape
    width = m // steps
    whole = lambda *shape: pl.BlockSpec(shape, lambda i: (0,) * len(shape))
    cut = lambda rows: pl.BlockSpec((rows, width), lambda i: (0, i))
    return pl.pallas_call(
        update_kernel,
        grid=(steps,),
        in_specs=[whole(*gain.shape), cut(panel.shape[0]), whole(1, n), whole(1, n), cut(n)],
        out_specs=[cut(n), whole(1, n)],
        out_shape=[jax.ShapeDtypeStruct((n, m), jnp.float32), jax.ShapeDtypeStruct((1, n), jnp.float32)],
        compiler_params=pltpu.CompilerParams(vmem_limit_bytes=16 << 20),
    )(gain, panel, shift, mean, cov)


def far_first(t, n):
    return n // 2 + (1 - 2 * lax.rem(t, 2)) * lax.div(t + 1, 2)


def near_first(t, n):
    return far_first(n - 2 - t, n)


def exchange_kernel(
    ctx_hbm, w_hbm, bias_hbm, cov_hbm, mean_hbm, rew_hbm,
    gain_out, pc_out, shift_out,
    ctx_all, ctx_m, w_v, bias_v, cov_v, mean_v, rew_v, c_hi, c_mid,
    x_send, x_recv, z_send, z_code, z_recv, phi_s, phi_c, phi_r,
    pp_send, pp_recv, p_code, gz_s, gz_r, pz_s, pz_r, g_s, g_all, pred_s, pred_r,
    pr_all, p_z, pc_all,
    local, near, pair_s, pair_r, send, recv, mate, send_pc, recv_pc, send_g, recv_g,
):
    nz, nc, nb = z_recv.shape[0], ctx_all.shape[0], 4
    r, c = lax.axis_index("row"), lax.axis_index("col")
    z, h = lax.div(r, 2), lax.rem(r, 2)
    other = 1 - h

    def at(zz, hh, cc):
        return (zz * 2 + hh, cc)

    def remote(src, dst, s_sem, r_sem, where):
        return pltpu.make_async_remote_copy(
            src_ref=src, dst_ref=dst, send_sem=s_sem, recv_sem=r_sem, device_id=where, device_id_type=MESH
        )

    loads = [
        pltpu.make_async_copy(ctx_hbm, ctx_all.at[c], local.at[0]),
        pltpu.make_async_copy(cov_hbm, cov_v, local.at[1]),
        pltpu.make_async_copy(w_hbm, w_v, local.at[2]),
        pltpu.make_async_copy(bias_hbm, bias_v, local.at[3]),
        pltpu.make_async_copy(mean_hbm, mean_v, local.at[4]),
        pltpu.make_async_copy(rew_hbm, rew_v, local.at[5]),
    ]
    for load in loads:
        load.start()

    barrier = pltpu.get_barrier_semaphore()

    def greet(where):
        pl.semaphore_signal(barrier, inc=1, device_id=where, device_id_type=MESH)

    def greet_plane(t, _):
        greet(at(z, h, lax.rem(c + t, nc)))
        return 0

    def greet_line(t, _):
        greet(at(lax.rem(z + t, nz), h, c))
        greet(at(lax.rem(z - t + nz, nz), h, c))
        return 0

    lax.fori_loop(1, nc, greet_plane, 0)
    lax.fori_loop(1, nb + 1, greet_line, 0)
    greet(at(z, other, c))
    pl.semaphore_wait(barrier, nc - 1 + 2 * nb + 1)
    pl.semaphore_signal(near, inc=1, device_id=at(lax.rem(z + nb, nz), h, c), device_id_type=MESH)
    pl.semaphore_signal(near, inc=1, device_id=at(lax.rem(z - nb + nz, nz), h, c), device_id_type=MESH)

    def ctx_copy(t):
        return remote(ctx_hbm, ctx_all.at[c], send.at[0, t], recv.at[0, c], at(z, h, lax.rem(c + t, nc)))

    def plane_arrival(buf, phase, src):
        return remote(buf.at[src], buf.at[src], send.at[phase, 0], recv.at[phase, src], at(z, other, c))

    def start_ctx(t, _):
        ctx_copy(t).start()
        return 0

    lax.fori_loop(1, nc, start_ctx, 0)

    def covariance_terms(first, last):
        for i in range(first, last):
            cut = slice(i * 128, i * 128 + 128)
            hi, mid, _ = split3(cov_v[cut, :].T)
            c_hi[:, cut] = hi
            c_mid[:, cut] = mid

    for load in loads[:1] + loads[2:]:
        load.wait()

    def wait_ctx(t, _):
        plane_arrival(ctx_all, 0, lax.rem(c + t, nc)).wait_recv()
        return 0

    lax.fori_loop(1, nc, wait_ctx, 0)
    tokens, depth = ctx_m.shape
    half = tokens // 2
    ctx_m[...] = ctx_all[...].astype(jnp.float32).reshape(tokens, depth).astype(jnp.bfloat16)

    def line_copy(src, dst, phase, t):
        return remote(src, dst, send.at[phase, t], recv.at[phase, z], at(lax.rem(z + t, nz), h, c))

    def line_arrival(buf, phase, src):
        return remote(buf.at[src], buf.at[src], send.at[phase, 0], recv.at[phase, src], at(z, other, c))

    def swap_x(block):
        theirs = pl.ds(pl.multiple_of(other * half, half), half)
        return remote(x_send.at[block, theirs], x_recv.at[block], pair_s.at[block], pair_r.at[block], at(z, other, c))

    for block in range(4):
        x_send[block] = jnp.dot(ctx_m[...], w_v[:, block * 256 : block * 256 + 256], preferred_element_type=jnp.float32)
        swap_x(block).start()
    own_rows = pl.ds(pl.multiple_of(h * half, half), half)
    for block in range(4):
        swap_x(block).wait_recv()
        both = x_send[block, own_rows, :] + x_recv[block]
        z_send[block] = both
        z_code[block] = coded_sum(both).reshape(4, 16, 256)
    pl.semaphore_wait(near, 2)

    def start_z(t, _):
        t = far_first(t, nz)
        k = lax.rem(z + t, nz)
        line_copy(z_code.at[lax.rem(k, 4), lax.div(k, 4)], z_recv.at[z], 1, t).start()
        return 0

    lax.fori_loop(0, nz - 1, start_z, 0)

    loads[1].wait()
    covariance_terms(0, 4)

    def add_z(t, acc):
        zz = lax.rem(z + near_first(t, nz), nz)
        line_arrival(z_recv, 1, zz).wait_recv()
        return acc + sum_from(z_recv[zz])

    kb = lax.rem(z, 4)
    own = z_send[kb, pl.ds(pl.multiple_of(lax.div(z, 4) * 16, 16), 16), :]
    total = lax.fori_loop(0, nz - 1, add_z, own)
    total = total + bias_v[:, pl.ds(pl.multiple_of(kb * 256, 256), 256)]
    phi = jnp.tanh(total).astype(jnp.bfloat16)
    phi_s[...] = phi

    def start_phi(t, _):
        t = far_first(t, nz)
        line_copy(phi_s, phi_c.at[h * nz + z], 2, t).start()
        return 0

    lax.fori_loop(0, nz - 1, start_phi, 0)

    def mate_copy(k):
        return remote(phi_c.at[h * nz + k], phi_c.at[h * nz + k], mate.at[0, k], mate.at[1, k], at(z, other, c))

    def plane_copy(src, dst, phase, t):
        return remote(src, dst, send.at[phase, t], recv.at[phase, c], at(z, h, lax.rem(c + t, nc)))

    holder = c == z

    def push(core, k):
        column = lax.rem(k, 4)
        slot = core * 8 + lax.div(k, 4) * 2 + lax.rem(column, 2)

        @pl.when(jnp.logical_and(holder, lax.div(column, 2) == h))
        def _():
            phi_r[slot] = phi_c[core * nz + k]

            @pl.when(slot != z)
            def _():
                remote(phi_c.at[core * nz + k], phi_r.at[slot], send.at[3, slot], recv.at[4, slot], at(z, h, slot)).start()

    phi_c[h * nz + z] = phi
    mate_copy(z).start()
    push(h, z)

    def pass_mate(t, _):
        zz = lax.rem(z + near_first(t, nz), nz)
        remote(phi_s, phi_c.at[h * nz + zz], send.at[2, 0], recv.at[2, zz], at(z, other, c)).wait_recv()
        mate_copy(zz).start()
        push(h, zz)
        return 0

    lax.fori_loop(0, nz - 1, pass_mate, 0)

    def wait_mate(t, _):
        k = lax.rem(z + near_first(t - 1, nz), nz)
        i = other * nz + k
        remote(phi_c.at[i], phi_c.at[i], mate.at[0, k], mate.at[1, k], at(z, other, c)).wait_recv()
        push(other, k)
        return 0

    lax.fori_loop(0, nz, wait_mate, 0)

    part = None
    for k in range(4):
        lhs = jnp.concatenate([phi_c[i * 4 + k] for i in range(8)], 0)
        for term in (c_hi, c_mid):
            prod = jnp.dot(lhs, term[k * 256 : k * 256 + 256, :], preferred_element_type=jnp.float32)
            part = prod if part is None else part + prod
    pp_send[...] = coded_panel(part).reshape(pp_send.shape)

    def start_pp(t, _):
        plane_copy(pp_send.at[lax.rem(c + t, nc)], pp_recv.at[c], 5, t).start()
        return 0

    lax.fori_loop(1, nc, start_pp, 0)
    pp_recv[c] = pp_send[c]

    def pass_row(t):
        return plane_copy(phi_r.at[c], phi_r.at[c], 4, t)

    @pl.when(jnp.logical_not(holder))
    def _():
        plane_arrival(phi_r, 4, c).wait_recv()

    def start_row(t, _):
        @pl.when(lax.rem(c + t, nc) != z)
        def _():
            pass_row(t).start()

        return 0

    lax.fori_loop(1, nc, start_row, 0)

    def wait_row(t, _):
        @pl.when(jnp.logical_not(holder))
        def _():
            plane_arrival(phi_r, 4, lax.rem(c + t, nc)).wait_recv()

        return 0

    def wait_pp(t, _):
        plane_arrival(pp_recv, 5, lax.rem(c + t, nc)).wait_recv()
        return 0

    lax.fori_loop(1, nc, wait_pp, 0)
    p_mine = jnp.sum(panel_from(pp_recv[...]), axis=0)
    p_code[0] = coded_panel(p_mine)
    lax.fori_loop(1, nc, wait_row, 0)

    width = p_mine.shape[1]
    zeros = jnp.zeros((7, width), jnp.float32)
    terms = split3(jnp.concatenate([p_mine, mean_v[...], zeros], 0))
    stacked = jnp.concatenate(terms, 0)
    gram = None
    for k in range(2):
        rhs = jnp.concatenate([phi_r[i * 2 + k] for i in range(8)], 0)
        prod = lax.dot_general(
            stacked[:, k * 256 : k * 256 + 256], rhs, (((1,), (1,)), ((), ())), preferred_element_type=jnp.float32
        )
        gram = prod if gram is None else gram + prod
    both = gram[:16] + gram[16:32] + gram[32:]
    gz_s[...] = both[:8]
    pz_s[...] = both[8:9]
    p_z[z] = p_code[0]

    def start_gz(t, _):
        t = far_first(t, nz)
        line_copy(gz_s, gz_r.at[z], 7, t).start()
        return 0

    lax.fori_loop(0, nz - 1, start_gz, 0)
    gz_r[z] = both[:8]
    pz_r[z] = both[8:9]

    def start_pz(t, _):
        t = far_first(t, nz)
        line_copy(p_code.at[0], p_z.at[z], 9, t).start()
        line_copy(pz_s, pz_r.at[z], 8, t).start()
        return 0

    lax.fori_loop(0, nz - 1, start_pz, 0)

    def start_pr(t, _):
        plane_copy(p_code.at[0], pr_all.at[c], 6, t).start()
        return 0

    lax.fori_loop(1, nc, start_pr, 0)
    pr_all[c] = p_code[0]

    for block in range(4):
        swap_x(block).wait_send()

    def sent_first(t, _):
        ctx_copy(t).wait_send()
        remote(phi_s, z_recv.at[z], send.at[1, t], recv.at[1, z], at(lax.rem(z + t, nz), h, c)).wait_send()
        line_copy(phi_s, phi_c.at[h * nz + z], 2, t).wait_send()
        plane_copy(pp_send.at[lax.rem(c + t, nc)], pp_recv.at[c], 5, t).wait_send()

        @pl.when(lax.rem(c + t, nc) != z)
        def _():
            pass_row(t).wait_send()

        return 0

    lax.fori_loop(1, nz, sent_first, 0)

    def sent_pieces(t, _):
        mate_copy(t).wait_send()

        @pl.when(jnp.logical_and(holder, t != z))
        def _():
            remote(phi_r.at[t], phi_r.at[t], send.at[3, t], recv.at[4, t], at(z, h, t)).wait_send()

        return 0

    lax.fori_loop(0, nz, sent_pieces, 0)

    def wait_gz(t, _):
        zz = lax.rem(z + t, nz)
        line_arrival(gz_r, 7, zz).wait_recv()
        return 0

    lax.fori_loop(1, nz, wait_gz, 0)
    g_s[...] = jnp.sum(gz_r[...], axis=0)

    def g_copy(t, core):
        return remote(g_s, g_all.at[h, c], send_g.at[core, t], recv_g.at[h, c], at(z, core, lax.rem(c + t, nc)))

    def g_arrival(core, p):
        return remote(g_s, g_all.at[core, p], send_g.at[0, 0], recv_g.at[core, p], at(z, other, c))

    def start_g(t, _):
        @pl.when(t > 0)
        def _():
            g_copy(t, h).start()

        g_copy(t, other).start()
        return 0

    lax.fori_loop(0, nc, start_g, 0)
    g_all[h, c] = g_s[...]

    def col_copy(zz, core):
        return remote(p_z.at[zz], pc_all.at[h, c], send_pc.at[core, zz], recv_pc.at[h, c], at(z, core, zz))

    def pass_pz(t, _):
        zz = lax.rem(z + near_first(t - 1, nz), nz)

        @pl.when(t > 0)
        def _():
            line_arrival(p_z, 9, zz).wait_recv()

        @pl.when(zz == c)
        def _():
            pc_all[h, c] = p_z[zz]

        @pl.when(zz != c)
        def _():
            col_copy(zz, h).start()

        col_copy(zz, other).start()
        return 0

    lax.fori_loop(0, nz, pass_pz, 0)

    def wait_pred(t, _):
        line_arrival(pz_r, 8, lax.rem(z + t, nz)).wait_recv()
        return 0

    lax.fori_loop(1, nz, wait_pred, 0)
    pred_s[...] = jnp.sum(pz_r[...], axis=0)
    swap_pred = remote(pred_s, pred_r, pair_s.at[4], pair_r.at[4], at(z, other, c))
    swap_pred.start()

    def wait_g(t, _):
        p = lax.rem(c + t, nc)

        @pl.when(t > 0)
        def _():
            g_arrival(h, p).wait_recv()

        g_arrival(other, p).wait_recv()
        return 0

    lax.fori_loop(0, nc, wait_g, 0)
    eye = (lax.broadcasted_iota(jnp.int32, (tokens, tokens), 0) == lax.broadcasted_iota(jnp.int32, (tokens, tokens), 1)).astype(jnp.float32)
    g = (g_all[0] + g_all[1]).reshape(tokens, tokens) + eye
    blocks = [g[8 * i : 8 * i + 8] for i in range(tokens // 8)]
    for lo in range(0, 32, 16):
        blocks = eliminated(blocks, lo, 16)

    for lo in range(32, 96, 16):
        blocks = eliminated(blocks, lo, 16)

    def wait_last(t, _):
        p = lax.rem(c + t, nc)
        plane_arrival(pr_all, 6, p).wait_recv()
        return 0

    lax.fori_loop(1, nc, wait_last, 0)

    def wait_pc(t, _):
        p = lax.rem(c + t, nc)

        @pl.when(t > 0)
        def _():
            remote(p_code.at[0], pc_all.at[h, p], send_pc.at[0, 0], recv_pc.at[h, p], at(z, other, c)).wait_recv()

        remote(p_code.at[0], pc_all.at[other, p], send_pc.at[0, 0], recv_pc.at[other, p], at(z, other, c)).wait_recv()
        return 0

    lax.fori_loop(0, nc, wait_pc, 0)
    swap_pred.wait()

    for k in range(2):
        panel = panel_from(pc_all[k]).reshape(tokens, width)
        hi, mid, _ = split3(panel)
        cut = slice(k * width, k * width + width)
        pc_out[:tokens, cut] = hi
        pc_out[tokens : 2 * tokens, cut] = mid
        pc_out[2 * tokens :, cut] = hi
    pr = panel_from(pr_all[...]).reshape(tokens, width)
    rh, rm, _ = split3(pr.T)
    pr_t = jnp.concatenate([rh, rh, rm], 1)
    for lo in range(96, 128, 16):
        blocks = eliminated(blocks, lo, 16)
    inv = jnp.concatenate(blocks, 0)
    ih, im, _ = split3(inv)
    gain = jnp.dot(pr_t, jnp.concatenate([ih, im, ih], 0), preferred_element_type=jnp.float32)
    hi, mid, _ = split3(gain)
    gain_out[:, :tokens] = hi
    gain_out[:, tokens : 2 * tokens] = hi
    gain_out[:, 2 * tokens :] = mid
    diff = rew_v[...] - (pred_s[...] + pred_r[...])
    coeffs = jnp.dot(jnp.broadcast_to(diff, (8, tokens)), inv, precision=HI, preferred_element_type=jnp.float32)
    shift_out[...] = jnp.dot(coeffs, pr, precision=HI, preferred_element_type=jnp.float32)[:1]

    def sent(t, _):
        plane_copy(p_code.at[0], pr_all.at[c], 6, t).wait_send()
        line_copy(gz_s, gz_r.at[z], 7, t).wait_send()
        line_copy(pz_s, pz_r.at[z], 8, t).wait_send()
        line_copy(p_code.at[0], p_z.at[z], 9, t).wait_send()
        g_copy(t, h).wait_send()
        return 0

    lax.fori_loop(1, nz, sent, 0)

    def sent_some(t, _):
        col_copy(t, other).wait_send()
        g_copy(t, other).wait_send()

        @pl.when(t != c)
        def _():
            col_copy(t, h).wait_send()

        return 0

    lax.fori_loop(0, nz, sent_some, 0)


def exchange(context, weight, bias, covariance, mean, rewards):
    rows_here, depth = context.shape
    n, m = covariance.shape
    nz, nc = lax.axis_size("row") // 2, lax.axis_size("col")
    b = rows_here * nc
    f32, bf16 = jnp.float32, jnp.bfloat16
    vmem, sem = pltpu.VMEM, pltpu.SemaphoreType
    scratch = [
        vmem((nc, rows_here, depth), bf16), vmem((b, depth), bf16), vmem((depth, m), bf16), vmem((1, m), f32),
        vmem((n, m), f32), vmem((1, n), f32), vmem((1, b), f32), vmem((m, n), bf16), vmem((m, n), bf16),
        vmem((4, b, 256), f32), vmem((4, b // 2, 256), f32), vmem((4, b // 2, 256), f32),
        vmem((4, 4, 16, 256), bf16), vmem((nz, 16, 256), bf16),
        vmem((16, 256), bf16), vmem((2 * nz, 16, 256), bf16), vmem((16, 16, 256), bf16),
        vmem((nc, 8, n), bf16), vmem((nc, 8, n), bf16), vmem((1, 8, n), bf16),
        vmem((8, b), f32), vmem((nz, 8, b), f32), vmem((1, b), f32), vmem((nz, 1, b), f32), vmem((8, b), f32), vmem((2, nc, 8, b), f32),
        vmem((1, b), f32), vmem((1, b), f32),
        vmem((nc, 8, n), bf16), vmem((nz, 8, n), bf16), vmem((2, nc, 8, n), bf16),
        sem.DMA((6,)), sem.REGULAR, sem.DMA((5,)), sem.DMA((5,)), sem.DMA((10, 16)), sem.DMA((10, 16)), sem.DMA((2, 16)),
        sem.DMA((2, 16)), sem.DMA((2, 16)), sem.DMA((2, 16)), sem.DMA((2, 16)),
    ]
    return pl.pallas_call(
        exchange_kernel,
        in_specs=[pl.BlockSpec(memory_space=pltpu.HBM)] * 6,
        out_specs=[pl.BlockSpec(memory_space=pltpu.VMEM)] * 3,
        out_shape=[
            jax.ShapeDtypeStruct((n, 3 * b), bf16), jax.ShapeDtypeStruct((3 * b, m), bf16), jax.ShapeDtypeStruct((1, n), f32),
        ],
        scratch_shapes=scratch,
        compiler_params=pltpu.CompilerParams(collective_id=0, has_side_effects=True, vmem_limit_bytes=28 << 20),
    )(*(pltpu.with_memory_space_constraint(x, pltpu.HBM) for x in (context, weight, bias, covariance, mean, rewards)))


def per_device(context, weight, feature_bias, covariance, prior_mean, rewards):
    mean = prior_mean.reshape(1, -1)
    gain, panel, shift = exchange(context, weight, feature_bias.reshape(1, -1), covariance, mean, rewards.reshape(1, -1))
    cov, mean = update(gain, panel, shift, mean, pltpu.with_memory_space_constraint(covariance, pltpu.HBM))
    return cov, mean.reshape(-1)


def solution(mesh):
    return jax.shard_map(
        per_device,
        mesh=mesh,
        in_specs=(P("col", "row"), P("row", "col"), P("col"), P("row", "col"), P("row"), P()),
        out_specs=(P("row", "col"), P("row")),
        check_vma=False,
    )
```

```python
import jax
import jax.numpy as jnp
from jax import lax
from jax.experimental import pallas as pl
from jax.experimental.pallas import tpu as pltpu
from jax.sharding import PartitionSpec as P

HI = lax.Precision.HIGHEST
MESH = pl.DeviceIdType.MESH


def split3(x):
    hi = x.astype(jnp.bfloat16)
    rest = x - hi.astype(jnp.float32)
    mid = rest.astype(jnp.bfloat16)
    lo = (rest - mid.astype(jnp.float32)).astype(jnp.bfloat16)
    return hi, mid, lo


def coded_sum(x):
    t = x * 16.0
    t2 = t * t
    t4 = t2 * t2
    return ((t4 * t4) * t2 * t).astype(jnp.bfloat16)


def coded_panel(x):
    t = x * 4.0
    t2 = t * t
    return ((t2 * t2) * t2 * t).astype(jnp.bfloat16)


def rooted(y, power, scale):
    y = y.astype(jnp.float32)
    v = jnp.exp(jnp.log(jnp.abs(y)) * (1.0 / power)) * (1.0 / scale)
    return jnp.where(y < 0, -v, v)


def sum_from(y):
    return rooted(y, 11, 16)


def panel_from(y):
    return rooted(y, 7, 4)


def inverse_of_2(a, b, c):
    scale = 1.0 / (a * c - b * b)
    return c * scale, -b * scale, a * scale


def inverse_of_4(m):
    a0, a1, a2 = inverse_of_2(m[0][0], m[0][1], m[1][1])
    t = [[a0 * m[0][2 + k] + a1 * m[1][2 + k] for k in range(2)], [a1 * m[0][2 + k] + a2 * m[1][2 + k] for k in range(2)]]
    s0 = m[2][2] - (m[0][2] * t[0][0] + m[1][2] * t[1][0])
    s1 = m[2][3] - (m[0][2] * t[0][1] + m[1][2] * t[1][1])
    s2 = m[3][3] - (m[0][3] * t[0][1] + m[1][3] * t[1][1])
    c0, c1, c2 = inverse_of_2(s0, s1, s2)
    u = [[t[i][0] * c0 + t[i][1] * c1, t[i][0] * c1 + t[i][1] * c2] for i in range(2)]
    b0 = a0 + u[0][0] * t[0][0] + u[0][1] * t[0][1]
    b1 = a1 + u[0][0] * t[1][0] + u[0][1] * t[1][1]
    b2 = a2 + u[1][0] * t[1][0] + u[1][1] * t[1][1]
    return [
        [b0, b1, -u[0][0], -u[0][1]],
        [b1, b2, -u[1][0], -u[1][1]],
        [-u[0][0], -u[1][0], c0, c1],
        [-u[0][1], -u[1][1], c1, c2],
    ]


def panel4(blocks, lo, lane, sub):
    n = blocks[0].shape[1]
    for j in range(lo, lo + 8 * len(blocks), 4):
        at, s = (j - lo) // 8, j % 8
        mine = blocks[at]
        cell = [[None] * 4 for _ in range(4)]
        for i in range(4):
            for k in range(i, 4):
                cell[i][k] = cell[k][i] = jnp.broadcast_to(mine[s + i : s + i + 1, j + k : j + k + 1], (8, n))
        inv = inverse_of_4(cell)
        inside = (lane >= j) & (lane < j + 4)
        rows = [
            jnp.where(inside, jnp.where(lane == j + m, 1.0, 0.0), jnp.broadcast_to(mine[s + m : s + m + 1], (8, n)))
            for m in range(4)
        ]
        out = [(inv[i][0] * rows[0] + inv[i][1] * rows[1]) + (inv[i][2] * rows[2] + inv[i][3] * rows[3]) for i in range(4)]
        new = []
        for i, block in enumerate(blocks):
            kept = jnp.where(inside, 0.0, block)
            cols = [jnp.broadcast_to(block[:, j + k : j + k + 1], (8, n)) for k in range(4)]
            if i == at:
                here = (sub >= s) & (sub < s + 4)
                kept = jnp.where(here, 0.0, kept)
                cols = [jnp.where(here, jnp.where(sub == s + k, -1.0, 0.0), cols[k]) for k in range(4)]
            new.append(kept - ((cols[0] * out[0] + cols[1] * out[1]) + (cols[2] * out[2] + cols[3] * out[3])))
        blocks = new
    return blocks


def dot3(a, b):
    ah, am, al = split3(a)
    bh, bm, bl = split3(b)
    return jnp.dot(jnp.concatenate([ah, ah, am, am, ah, al], 1), jnp.concatenate([bh, bm, bh, bm, bl, bh], 0), preferred_element_type=jnp.float32)


def eliminated(blocks, lo, w):
    n = blocks[0].shape[1]
    lane = lax.broadcasted_iota(jnp.int32, (8, n), 1)
    sub = lax.broadcasted_iota(jnp.int32, (8, n), 0)
    first, last = lo // 8, (lo + w) // 8
    panel = panel4(blocks[first:last], lo, lane, sub)
    rest = blocks[:first] + blocks[last:]
    cols = jnp.concatenate([b[:, lo : lo + w] for b in rest], 0)
    prod = dot3(cols, jnp.concatenate(panel, 0))
    inside = (lane >= lo) & (lane < lo + w)
    rest = [jnp.where(inside, 0.0, b) - prod[8 * i : 8 * i + 8] for i, b in enumerate(rest)]
    return rest[:first] + panel + rest[first:]


def update_kernel(gain_ref, pc_ref, shift_ref, mean_ref, cov_ref, out_ref, outm_ref):
    out_ref[...] = cov_ref[...] - jnp.dot(gain_ref[...], pc_ref[...], preferred_element_type=jnp.float32)

    @pl.when(pl.program_id(0) == 0)
    def _():
        outm_ref[...] = mean_ref[...] + shift_ref[...]


def update(gain, panel, shift, mean, cov, steps=2):
    n, m = cov.shape
    width = m // steps
    whole = lambda *shape: pl.BlockSpec(shape, lambda i: (0,) * len(shape))
    cut = lambda rows: pl.BlockSpec((rows, width), lambda i: (0, i))
    return pl.pallas_call(
        update_kernel,
        grid=(steps,),
        in_specs=[whole(*gain.shape), cut(panel.shape[0]), whole(1, n), whole(1, n), cut(n)],
        out_specs=[cut(n), whole(1, n)],
        out_shape=[jax.ShapeDtypeStruct((n, m), jnp.float32), jax.ShapeDtypeStruct((1, n), jnp.float32)],
        compiler_params=pltpu.CompilerParams(vmem_limit_bytes=16 << 20),
    )(gain, panel, shift, mean, cov)


def far_first(t, n):
    return n // 2 + (1 - 2 * lax.rem(t, 2)) * lax.div(t + 1, 2)


def near_first(t, n):
    return far_first(n - 2 - t, n)


def exchange_kernel(
    ctx_hbm, w_hbm, bias_hbm, cov_hbm, mean_hbm, rew_hbm,
    gain_out, pc_out, shift_out,
    ctx_all, ctx_m, w_v, bias_v, cov_v, mean_v, rew_v, c_hi, c_mid,
    x_send, x_recv, z_send, z_code, z_recv, phi_s, phi_c, phi_r,
    pp_send, pp_recv, p_code, gz_s, gz_r, pz_s, pz_r, g_s, g_all, pred_s, pred_r,
    pr_all, p_z, pc_all,
    local, near, pair_s, pair_r, send, recv, mate, send_pc, recv_pc, send_g, recv_g,
):
    nz, nc, nb = z_recv.shape[0], ctx_all.shape[0], 4
    r, c = lax.axis_index("row"), lax.axis_index("col")
    z, h = lax.div(r, 2), lax.rem(r, 2)
    other = 1 - h

    def at(zz, hh, cc):
        return (zz * 2 + hh, cc)

    def remote(src, dst, s_sem, r_sem, where):
        return pltpu.make_async_remote_copy(
            src_ref=src, dst_ref=dst, send_sem=s_sem, recv_sem=r_sem, device_id=where, device_id_type=MESH
        )

    loads = [
        pltpu.make_async_copy(ctx_hbm, ctx_all.at[c], local.at[0]),
        pltpu.make_async_copy(cov_hbm, cov_v, local.at[1]),
        pltpu.make_async_copy(w_hbm, w_v, local.at[2]),
        pltpu.make_async_copy(bias_hbm, bias_v, local.at[3]),
        pltpu.make_async_copy(mean_hbm, mean_v, local.at[4]),
        pltpu.make_async_copy(rew_hbm, rew_v, local.at[5]),
    ]
    for load in loads:
        load.start()

    barrier = pltpu.get_barrier_semaphore()

    def greet(where):
        pl.semaphore_signal(barrier, inc=1, device_id=where, device_id_type=MESH)

    def greet_plane(t, _):
        greet(at(z, h, lax.rem(c + t, nc)))
        return 0

    def greet_line(t, _):
        greet(at(lax.rem(z + t, nz), h, c))
        greet(at(lax.rem(z - t + nz, nz), h, c))
        return 0

    lax.fori_loop(1, nc, greet_plane, 0)
    lax.fori_loop(1, nb + 1, greet_line, 0)
    greet(at(z, other, c))
    pl.semaphore_wait(barrier, nc - 1 + 2 * nb + 1)
    pl.semaphore_signal(near, inc=1, device_id=at(lax.rem(z + nb, nz), h, c), device_id_type=MESH)
    pl.semaphore_signal(near, inc=1, device_id=at(lax.rem(z - nb + nz, nz), h, c), device_id_type=MESH)

    def ctx_copy(t):
        return remote(ctx_hbm, ctx_all.at[c], send.at[0, t], recv.at[0, c], at(z, h, lax.rem(c + t, nc)))

    def plane_arrival(buf, phase, src):
        return remote(buf.at[src], buf.at[src], send.at[phase, 0], recv.at[phase, src], at(z, other, c))

    def start_ctx(t, _):
        ctx_copy(t).start()
        return 0

    lax.fori_loop(1, nc, start_ctx, 0)

    def covariance_terms(first, last):
        for i in range(first, last):
            cut = slice(i * 128, i * 128 + 128)
            hi, mid, _ = split3(cov_v[cut, :].T)
            c_hi[:, cut] = hi
            c_mid[:, cut] = mid

    for load in loads[:1] + loads[2:]:
        load.wait()

    def wait_ctx(t, _):
        plane_arrival(ctx_all, 0, lax.rem(c + t, nc)).wait_recv()
        return 0

    lax.fori_loop(1, nc, wait_ctx, 0)
    tokens, depth = ctx_m.shape
    half = tokens // 2
    ctx_m[...] = ctx_all[...].astype(jnp.float32).reshape(tokens, depth).astype(jnp.bfloat16)

    def line_copy(src, dst, phase, t):
        return remote(src, dst, send.at[phase, t], recv.at[phase, z], at(lax.rem(z + t, nz), h, c))

    def line_arrival(buf, phase, src):
        return remote(buf.at[src], buf.at[src], send.at[phase, 0], recv.at[phase, src], at(z, other, c))

    def swap_x(block):
        theirs = pl.ds(pl.multiple_of(other * half, half), half)
        return remote(x_send.at[block, theirs], x_recv.at[block], pair_s.at[block], pair_r.at[block], at(z, other, c))

    for block in range(4):
        x_send[block] = jnp.dot(ctx_m[...], w_v[:, block * 256 : block * 256 + 256], preferred_element_type=jnp.float32)
        swap_x(block).start()
    own_rows = pl.ds(pl.multiple_of(h * half, half), half)
    for block in range(4):
        swap_x(block).wait_recv()
        both = x_send[block, own_rows, :] + x_recv[block]
        z_send[block] = both
        z_code[block] = coded_sum(both).reshape(4, 16, 256)
    pl.semaphore_wait(near, 2)

    def start_z(t, _):
        t = far_first(t, nz)
        k = lax.rem(z + t, nz)
        line_copy(z_code.at[lax.rem(k, 4), lax.div(k, 4)], z_recv.at[z], 1, t).start()
        return 0

    lax.fori_loop(0, nz - 1, start_z, 0)

    loads[1].wait()
    covariance_terms(0, 4)

    def add_z(t, acc):
        zz = lax.rem(z + near_first(t, nz), nz)
        line_arrival(z_recv, 1, zz).wait_recv()
        return acc + sum_from(z_recv[zz])

    kb = lax.rem(z, 4)
    own = z_send[kb, pl.ds(pl.multiple_of(lax.div(z, 4) * 16, 16), 16), :]
    total = lax.fori_loop(0, nz - 1, add_z, own)
    total = total + bias_v[:, pl.ds(pl.multiple_of(kb * 256, 256), 256)]
    phi = jnp.tanh(total).astype(jnp.bfloat16)
    phi_s[...] = phi

    def start_phi(t, _):
        t = far_first(t, nz)
        line_copy(phi_s, phi_c.at[h * nz + z], 2, t).start()
        return 0

    lax.fori_loop(0, nz - 1, start_phi, 0)

    def mate_copy(k):
        return remote(phi_c.at[h * nz + k], phi_c.at[h * nz + k], mate.at[0, k], mate.at[1, k], at(z, other, c))

    def plane_copy(src, dst, phase, t):
        return remote(src, dst, send.at[phase, t], recv.at[phase, c], at(z, h, lax.rem(c + t, nc)))

    holder = c == z

    def push(core, k):
        column = lax.rem(k, 4)
        slot = core * 8 + lax.div(k, 4) * 2 + lax.rem(column, 2)

        @pl.when(jnp.logical_and(holder, lax.div(column, 2) == h))
        def _():
            phi_r[slot] = phi_c[core * nz + k]

            @pl.when(slot != z)
            def _():
                remote(phi_c.at[core * nz + k], phi_r.at[slot], send.at[3, slot], recv.at[4, slot], at(z, h, slot)).start()

    phi_c[h * nz + z] = phi
    mate_copy(z).start()
    push(h, z)

    def pass_mate(t, _):
        zz = lax.rem(z + near_first(t, nz), nz)
        remote(phi_s, phi_c.at[h * nz + zz], send.at[2, 0], recv.at[2, zz], at(z, other, c)).wait_recv()
        mate_copy(zz).start()
        push(h, zz)
        return 0

    lax.fori_loop(0, nz - 1, pass_mate, 0)

    def wait_mate(t, _):
        k = lax.rem(z + near_first(t - 1, nz), nz)
        i = other * nz + k
        remote(phi_c.at[i], phi_c.at[i], mate.at[0, k], mate.at[1, k], at(z, other, c)).wait_recv()
        push(other, k)
        return 0

    lax.fori_loop(0, nz, wait_mate, 0)

    part = None
    for k in range(4):
        lhs = jnp.concatenate([phi_c[i * 4 + k] for i in range(8)], 0)
        for term in (c_hi, c_mid):
            prod = jnp.dot(lhs, term[k * 256 : k * 256 + 256, :], preferred_element_type=jnp.float32)
            part = prod if part is None else part + prod
    pp_send[...] = coded_panel(part).reshape(pp_send.shape)

    def start_pp(t, _):
        plane_copy(pp_send.at[lax.rem(c + t, nc)], pp_recv.at[c], 5, t).start()
        return 0

    lax.fori_loop(1, nc, start_pp, 0)
    pp_recv[c] = pp_send[c]

    def pass_row(t):
        return plane_copy(phi_r.at[c], phi_r.at[c], 4, t)

    @pl.when(jnp.logical_not(holder))
    def _():
        plane_arrival(phi_r, 4, c).wait_recv()

    def start_row(t, _):
        @pl.when(lax.rem(c + t, nc) != z)
        def _():
            pass_row(t).start()

        return 0

    lax.fori_loop(1, nc, start_row, 0)

    def wait_row(t, _):
        @pl.when(jnp.logical_not(holder))
        def _():
            plane_arrival(phi_r, 4, lax.rem(c + t, nc)).wait_recv()

        return 0

    def wait_pp(t, _):
        plane_arrival(pp_recv, 5, lax.rem(c + t, nc)).wait_recv()
        return 0

    lax.fori_loop(1, nc, wait_pp, 0)
    p_mine = jnp.sum(panel_from(pp_recv[...]), axis=0)
    p_code[0] = coded_panel(p_mine)
    lax.fori_loop(1, nc, wait_row, 0)

    width = p_mine.shape[1]
    zeros = jnp.zeros((7, width), jnp.float32)
    terms = split3(jnp.concatenate([p_mine, mean_v[...], zeros], 0))
    stacked = jnp.concatenate(terms, 0)
    gram = None
    for k in range(2):
        rhs = jnp.concatenate([phi_r[i * 2 + k] for i in range(8)], 0)
        prod = lax.dot_general(
            stacked[:, k * 256 : k * 256 + 256], rhs, (((1,), (1,)), ((), ())), preferred_element_type=jnp.float32
        )
        gram = prod if gram is None else gram + prod
    both = gram[:16] + gram[16:32] + gram[32:]
    gz_s[...] = both[:8]
    pz_s[...] = both[8:9]
    p_z[z] = p_code[0]

    def start_gz(t, _):
        t = far_first(t, nz)
        line_copy(gz_s, gz_r.at[z], 7, t).start()
        return 0

    lax.fori_loop(0, nz - 1, start_gz, 0)
    gz_r[z] = both[:8]
    pz_r[z] = both[8:9]

    def start_pz(t, _):
        t = far_first(t, nz)
        line_copy(p_code.at[0], p_z.at[z], 9, t).start()
        line_copy(pz_s, pz_r.at[z], 8, t).start()
        return 0

    lax.fori_loop(0, nz - 1, start_pz, 0)

    def start_pr(t, _):
        plane_copy(p_code.at[0], pr_all.at[c], 6, t).start()
        return 0

    lax.fori_loop(1, nc, start_pr, 0)
    pr_all[c] = p_code[0]

    for block in range(4):
        swap_x(block).wait_send()

    def sent_first(t, _):
        ctx_copy(t).wait_send()
        remote(phi_s, z_recv.at[z], send.at[1, t], recv.at[1, z], at(lax.rem(z + t, nz), h, c)).wait_send()
        line_copy(phi_s, phi_c.at[h * nz + z], 2, t).wait_send()
        plane_copy(pp_send.at[lax.rem(c + t, nc)], pp_recv.at[c], 5, t).wait_send()

        @pl.when(lax.rem(c + t, nc) != z)
        def _():
            pass_row(t).wait_send()

        return 0

    lax.fori_loop(1, nz, sent_first, 0)

    def sent_pieces(t, _):
        mate_copy(t).wait_send()

        @pl.when(jnp.logical_and(holder, t != z))
        def _():
            remote(phi_r.at[t], phi_r.at[t], send.at[3, t], recv.at[4, t], at(z, h, t)).wait_send()

        return 0

    lax.fori_loop(0, nz, sent_pieces, 0)

    def wait_gz(t, _):
        zz = lax.rem(z + t, nz)
        line_arrival(gz_r, 7, zz).wait_recv()
        return 0

    lax.fori_loop(1, nz, wait_gz, 0)
    g_s[...] = jnp.sum(gz_r[...], axis=0)

    def g_copy(t, core):
        return remote(g_s, g_all.at[h, c], send_g.at[core, t], recv_g.at[h, c], at(z, core, lax.rem(c + t, nc)))

    def g_arrival(core, p):
        return remote(g_s, g_all.at[core, p], send_g.at[0, 0], recv_g.at[core, p], at(z, other, c))

    def start_g(t, _):
        @pl.when(t > 0)
        def _():
            g_copy(t, h).start()

        g_copy(t, other).start()
        return 0

    lax.fori_loop(0, nc, start_g, 0)
    g_all[h, c] = g_s[...]

    def wait_last(t, _):
        p = lax.rem(c + t, nc)
        plane_arrival(pr_all, 6, p).wait_recv()
        return 0

    lax.fori_loop(1, nc, wait_last, 0)

    pr = panel_from(pr_all[...]).reshape(tokens, width)
    rh, rm, _ = split3(pr.T)
    pr_t = jnp.concatenate([rh, rh, rm], 1)

    def col_copy(zz, core):
        return remote(p_z.at[zz], pc_all.at[h, c], send_pc.at[core, zz], recv_pc.at[h, c], at(z, core, zz))

    def pass_pz(t, _):
        zz = lax.rem(z + near_first(t - 1, nz), nz)

        @pl.when(t > 0)
        def _():
            line_arrival(p_z, 9, zz).wait_recv()

        @pl.when(zz == c)
        def _():
            pc_all[h, c] = p_z[zz]

        @pl.when(zz != c)
        def _():
            col_copy(zz, h).start()

        col_copy(zz, other).start()
        return 0

    lax.fori_loop(0, nz, pass_pz, 0)

    def wait_pred(t, _):
        line_arrival(pz_r, 8, lax.rem(z + t, nz)).wait_recv()
        return 0

    lax.fori_loop(1, nz, wait_pred, 0)
    pred_s[...] = jnp.sum(pz_r[...], axis=0)
    swap_pred = remote(pred_s, pred_r, pair_s.at[4], pair_r.at[4], at(z, other, c))
    swap_pred.start()

    def wait_g(t, _):
        p = lax.rem(c + t, nc)

        @pl.when(t > 0)
        def _():
            g_arrival(h, p).wait_recv()

        g_arrival(other, p).wait_recv()
        return 0

    lax.fori_loop(0, nc, wait_g, 0)
    eye = (lax.broadcasted_iota(jnp.int32, (tokens, tokens), 0) == lax.broadcasted_iota(jnp.int32, (tokens, tokens), 1)).astype(jnp.float32)
    g = (g_all[0] + g_all[1]).reshape(tokens, tokens) + eye
    blocks = [g[8 * i : 8 * i + 8] for i in range(tokens // 8)]
    for lo in range(0, 32, 16):
        blocks = eliminated(blocks, lo, 16)

    for lo in range(32, 96, 16):
        blocks = eliminated(blocks, lo, 16)

    def wait_pc(t, _):
        p = lax.rem(c + t, nc)

        @pl.when(t > 0)
        def _():
            remote(p_code.at[0], pc_all.at[h, p], send_pc.at[0, 0], recv_pc.at[h, p], at(z, other, c)).wait_recv()

        remote(p_code.at[0], pc_all.at[other, p], send_pc.at[0, 0], recv_pc.at[other, p], at(z, other, c)).wait_recv()
        return 0

    lax.fori_loop(0, nc, wait_pc, 0)
    swap_pred.wait()

    for k in range(2):
        panel = panel_from(pc_all[k]).reshape(tokens, width)
        hi, mid, _ = split3(panel)
        cut = slice(k * width, k * width + width)
        pc_out[:tokens, cut] = hi
        pc_out[tokens : 2 * tokens, cut] = mid
        pc_out[2 * tokens :, cut] = hi
    for lo in range(96, 128, 16):
        blocks = eliminated(blocks, lo, 16)
    inv = jnp.concatenate(blocks, 0)
    ih, im, _ = split3(inv)
    gain = jnp.dot(pr_t, jnp.concatenate([ih, im, ih], 0), preferred_element_type=jnp.float32)
    hi, mid, _ = split3(gain)
    gain_out[:, :tokens] = hi
    gain_out[:, tokens : 2 * tokens] = hi
    gain_out[:, 2 * tokens :] = mid
    diff = rew_v[...] - (pred_s[...] + pred_r[...])
    coeffs = jnp.dot(jnp.broadcast_to(diff, (8, tokens)), inv, precision=HI, preferred_element_type=jnp.float32)
    shift_out[...] = jnp.dot(coeffs, pr, precision=HI, preferred_element_type=jnp.float32)[:1]

    def sent(t, _):
        plane_copy(p_code.at[0], pr_all.at[c], 6, t).wait_send()
        line_copy(gz_s, gz_r.at[z], 7, t).wait_send()
        line_copy(pz_s, pz_r.at[z], 8, t).wait_send()
        line_copy(p_code.at[0], p_z.at[z], 9, t).wait_send()
        g_copy(t, h).wait_send()
        return 0

    lax.fori_loop(1, nz, sent, 0)

    def sent_some(t, _):
        col_copy(t, other).wait_send()
        g_copy(t, other).wait_send()

        @pl.when(t != c)
        def _():
            col_copy(t, h).wait_send()

        return 0

    lax.fori_loop(0, nz, sent_some, 0)


def exchange(context, weight, bias, covariance, mean, rewards):
    rows_here, depth = context.shape
    n, m = covariance.shape
    nz, nc = lax.axis_size("row") // 2, lax.axis_size("col")
    b = rows_here * nc
    f32, bf16 = jnp.float32, jnp.bfloat16
    vmem, sem = pltpu.VMEM, pltpu.SemaphoreType
    scratch = [
        vmem((nc, rows_here, depth), bf16), vmem((b, depth), bf16), vmem((depth, m), bf16), vmem((1, m), f32),
        vmem((n, m), f32), vmem((1, n), f32), vmem((1, b), f32), vmem((m, n), bf16), vmem((m, n), bf16),
        vmem((4, b, 256), f32), vmem((4, b // 2, 256), f32), vmem((4, b // 2, 256), f32),
        vmem((4, 4, 16, 256), bf16), vmem((nz, 16, 256), bf16),
        vmem((16, 256), bf16), vmem((2 * nz, 16, 256), bf16), vmem((16, 16, 256), bf16),
        vmem((nc, 8, n), bf16), vmem((nc, 8, n), bf16), vmem((1, 8, n), bf16),
        vmem((8, b), f32), vmem((nz, 8, b), f32), vmem((1, b), f32), vmem((nz, 1, b), f32), vmem((8, b), f32), vmem((2, nc, 8, b), f32),
        vmem((1, b), f32), vmem((1, b), f32),
        vmem((nc, 8, n), bf16), vmem((nz, 8, n), bf16), vmem((2, nc, 8, n), bf16),
        sem.DMA((6,)), sem.REGULAR, sem.DMA((5,)), sem.DMA((5,)), sem.DMA((10, 16)), sem.DMA((10, 16)), sem.DMA((2, 16)),
        sem.DMA((2, 16)), sem.DMA((2, 16)), sem.DMA((2, 16)), sem.DMA((2, 16)),
    ]
    return pl.pallas_call(
        exchange_kernel,
        in_specs=[pl.BlockSpec(memory_space=pltpu.HBM)] * 6,
        out_specs=[pl.BlockSpec(memory_space=pltpu.VMEM)] * 3,
        out_shape=[
            jax.ShapeDtypeStruct((n, 3 * b), bf16), jax.ShapeDtypeStruct((3 * b, m), bf16), jax.ShapeDtypeStruct((1, n), f32),
        ],
        scratch_shapes=scratch,
        compiler_params=pltpu.CompilerParams(collective_id=0, has_side_effects=True, vmem_limit_bytes=28 << 20),
    )(*(pltpu.with_memory_space_constraint(x, pltpu.HBM) for x in (context, weight, bias, covariance, mean, rewards)))


def per_device(context, weight, feature_bias, covariance, prior_mean, rewards):
    mean = prior_mean.reshape(1, -1)
    gain, panel, shift = exchange(context, weight, feature_bias.reshape(1, -1), covariance, mean, rewards.reshape(1, -1))
    cov, mean = update(gain, panel, shift, mean, pltpu.with_memory_space_constraint(covariance, pltpu.HBM))
    return cov, mean.reshape(-1)


def solution(mesh):
    return jax.shard_map(
        per_device,
        mesh=mesh,
        in_specs=(P("col", "row"), P("row", "col"), P("col"), P("row", "col"), P("row"), P()),
        out_specs=(P("row", "col"), P("row")),
        check_vma=False,
    )
```
